32 devices in a mesh: grp: 4 (over y, x), ty: 4 (over z), tx: 2 (over core).
Axes of the slice: x: 2, y: 2, z: 4, core: 2. Of those that a mesh axis runs over, the one named last changes fastest.
Arguments:
- tracers: float32 [16, 8, 512, 256], P(None, 'grp', 'ty', 'tx'), may hold values from -1.5 to 3, as said below
- east_velocity: float32 [8, 512, 256], P('grp', 'ty', 'tx'), may hold values from -0.6 to 0.6
- north_velocity: float32 [8, 512, 256], P('grp', 'ty', 'tx'), may hold values from -0.6 to 0.6
- surface: float32 [512, 256], P('ty', 'tx'), may hold values from -1.5 to 1.5
- depth: float32 [512, 256], P('ty', 'tx'), may hold values from 1 to 3
- wet_mask: int32 [512, 256], P('ty', 'tx'), may hold values 0 or 1
- river_cells: int32 [32], P(('ty', 'tx')), may hold values from 0 to 16383
- river_loads: float32 [32, 16], P(('ty', 'tx')), may hold values from 0.2 to 2
- kinetics: float32 [16, 16], replicated, may hold values from -0.3 to 0.24, as said below
Outputs:
- new_tracers: float32 [16, 8, 512, 256], P(None, 'grp', 'ty', 'tx')
- new_east: float32 [8, 512, 256], P('grp', 'ty', 'tx')
- new_north: float32 [8, 512, 256], P('grp', 'ty', 'tx')
- new_surface: float32 [512, 256], P('ty', 'tx')
The draws below stay inside these ranges and needn't reach their ends.
Inputs may be any that keep to these rules, and one draw needn't show every extreme that they name: `tracers`: tracer 0 lies in -1.5 to 1.5, tracer 1 in -1 to 1, the others in 0.1 to 3. `kinetics`: diagonal entries lie in -0.3 to -0.05. `river_cells`: entry r is row * 128 + column of a cell in the tile of the device that holds entry r.
All inputs are finite; a program needn't handle non-finite values. No bound on the sum of `wet_mask` on one device may be relied on, other than what follows from the above.
Results may differ from the reference program's by a relative error of at most 0.000096.
Values sent between devices are 32-bit elements; how exact they have to be, the bound alone decides.
No kernel may reach another device: no remote copies, remote signals or barrier semaphores. Data moves between devices by JAX's collectives and lax.ppermute only.
A program may use at most 64 MiB of HBM per device.

```python
import math
import jax
import jax.numpy as jnp
from jax import lax

NTR = 16
CY = 128
CX = 128
RIV_DEV = 4
NY = 512
NX = 256
LEV = 8
RIVERS = 32
N_TX = 2


def draw_tracers(key, part):
    keys = jax.random.split(jax.random.fold_in(key, 11), 3)
    salinity = jax.random.uniform(keys[0], (1, LEV, NY, NX), jnp.float32, -1.5, 1.5)
    heat = jax.random.uniform(keys[1], (1, LEV, NY, NX), jnp.float32, -1.0, 1.0)
    others = jnp.exp(jax.random.uniform(keys[2], (NTR - 2, LEV, NY, NX), jnp.float32, math.log(0.1), math.log(3.0)))
    return jnp.concatenate([salinity, heat, others], 0)


def draw_kinetics(key, part):
    keys = jax.random.split(jax.random.fold_in(key, 23), 2)
    coupling = jax.random.truncated_normal(keys[0], -4.0, 4.0, (NTR, NTR), jnp.float32) * 0.06
    rates = jnp.exp(jax.random.uniform(keys[1], (NTR,), jnp.float32, math.log(0.05), math.log(0.3)))
    identity = jnp.eye(NTR, dtype=jnp.float32)
    return coupling * (1.0 - identity) - identity * rates[None, :]


def plant(drawn, stream_key, smallest, largest):
    longest = drawn.shape.index(max(drawn.shape))
    spots = []
    for shift in (0, 1):
        where = [jax.random.randint(jax.random.fold_in(stream_key, axis), (), 0, length) for axis, length in enumerate(drawn.shape)]
        where[longest] = (where[longest] + shift) % drawn.shape[longest]
        spots.append(tuple(where))
    return drawn.at[spots[0]].set(smallest).at[spots[1]].set(largest)


def level_of(own_key, dims, cuts, smallest, largest):
    def one(axis_at, parts):
        heights = jax.random.uniform(jax.random.fold_in(jax.random.fold_in(own_key, 6), axis_at), (parts,), jnp.float32, smallest / len(cuts), largest / len(cuts))
        return jnp.repeat(jnp.exp(heights), dims[axis_at] // parts).reshape((-1,) + (1,) * (len(dims) - axis_at - 1))

    gain = one(*cuts[0])
    for cut in cuts[1:]:
        gain = gain * one(*cut)
    return gain


def noise(stream_key, shape, deviation, bound, pieces=(), kind=jnp.bfloat16):
    values = deviation * jax.random.normal(stream_key, shape, jnp.float32)
    if pieces:
        values = values * level_of(stream_key, shape, pieces, -0.22, 0.18)
    return jnp.clip(values, -bound, bound).astype(kind)


def setup_inputs(seed: int = 0) -> dict:
    key_list = jax.random.split(jax.random.key(seed), 10)
    tracers = draw_tracers(jax.random.fold_in(key_list[9], 71), 0)
    east_velocity = noise(key_list[1], (LEV, NY, NX), 0.2, 0.6, ((0, 4), (1, 4), (2, 2)), jnp.float32)
    north_velocity = noise(key_list[2], (LEV, NY, NX), 0.2, 0.6, ((0, 4), (1, 4), (2, 2)), jnp.float32)
    surface = noise(key_list[3], (NY, NX), 0.3, 1.5, ((0, 4), (1, 2)), jnp.float32)
    depth = jnp.clip(1.0 + 2.0 * jax.random.uniform(key_list[4], (NY, NX), jnp.float32) ** level_of(key_list[4], (NY, NX), ((0, 4), (1, 2)), -0.2, 0.2), 1.0, 3.0)
    wet_mask = plant((jax.random.randint(key_list[5], (NY, NX), 0, 8) < 7).astype(jnp.int32), jax.random.fold_in(key_list[5], 1), 0, 1)
    river_cells = plant(jax.random.randint(key_list[6], (RIVERS,), 0, CY * CX), jax.random.fold_in(key_list[6], 1), 0, (CY * CX) - 1).astype(jnp.int32)
    river_loads = jnp.clip(0.2 + 1.8 * jax.random.uniform(key_list[7], (RIVERS, NTR), jnp.float32) ** level_of(key_list[7], (RIVERS, NTR), ((0, 8),), -0.2, 0.2), 0.2, 2.0)
    kinetics = draw_kinetics(jax.random.fold_in(key_list[9], 71), 0)
    return {"tracers": tracers, "east_velocity": east_velocity, "north_velocity": north_velocity, "surface": surface, "depth": depth, "wet_mask": wet_mask, "river_cells": river_cells, "river_loads": river_loads, "kinetics": kinetics}


eta_rate = 0.25
gravity_rate = 0.25
baroclinic_rate = 0.4
viscous_rate = 0.1
friction_rate = 0.3
advect_rate = 0.3
mixing_rate = 0.2
haline_coef = 0.8
thermal_coef = 0.2
warming_rate = 0.46


def face_terms(depth_pad, wet_pad):
    east_open = wet_pad[:, :-1] * wet_pad[:, 1:]
    north_open = wet_pad[:-1, :] * wet_pad[1:, :]
    east_depth = 0.5 * (depth_pad[:, :-1] + depth_pad[:, 1:]) * east_open
    north_depth = 0.5 * (depth_pad[:-1, :] + depth_pad[1:, :]) * north_open
    return east_open, north_open, east_depth, north_depth


def laplace(field_pad):
    inner = field_pad[:, 1:-1, 1:-1]
    return (field_pad[:, 2:, 1:-1] + field_pad[:, :-2, 1:-1] + field_pad[:, 1:-1, 2:]
            + field_pad[:, 1:-1, :-2] - 4.0 * inner)


def advect(tracer_pad, east_flux, north_flux, depth, levels):
    east_speed = east_flux[:, 1:-1, :]
    east_term = (jnp.maximum(east_speed, 0.0) * tracer_pad[..., 1:-1, :-1]
                 + jnp.minimum(east_speed, 0.0) * tracer_pad[..., 1:-1, 1:])
    north_speed = north_flux[:, :, 1:-1]
    north_term = (jnp.maximum(north_speed, 0.0) * tracer_pad[..., :-1, 1:-1]
                  + jnp.minimum(north_speed, 0.0) * tracer_pad[..., 1:, 1:-1])
    divergence = (east_term[..., 1:] - east_term[..., :-1]
                  + north_term[..., 1:, :] - north_term[..., :-1, :])
    return tracer_pad[..., 1:-1, 1:-1] - advect_rate * levels * divergence / depth


def vertical_mix(advected, level_above, level_below, has_above, has_below):
    return advected + mixing_rate * (has_above * (level_above - advected)
                                     + has_below * (level_below - advected))


def pad_plane(field):
    return jnp.pad(field, ((1, 1), (1, 1)))


def pad_levels(field):
    return jnp.pad(field, ((0, 0), (1, 1), (1, 1)))


def reference(tracers, east_velocity, north_velocity, surface, depth, wet_mask, river_cells, river_loads, kinetics):
    levels = tracers.shape[1]
    wet_cells = wet_mask.astype(jnp.float32)
    east_open, north_open, east_depth, north_depth = face_terms(pad_plane(depth), pad_plane(wet_cells))
    east_pad = pad_levels(east_velocity)
    north_pad = pad_levels(north_velocity)
    east_flux = east_pad[:, :, :-1] * east_depth / levels
    north_flux = north_pad[:, :-1, :] * north_depth / levels
    column_east = jnp.sum(east_flux, 0)
    column_north = jnp.sum(north_flux, 0)
    divergence = (column_east[1:-1, 1:] - column_east[1:-1, :-1]
                  + column_north[1:, 1:-1] - column_north[:-1, 1:-1])
    new_surface = surface - eta_rate * wet_cells * divergence
    density = haline_coef * tracers[0] - thermal_coef * tracers[1]
    pressure = baroclinic_rate * depth * (jnp.cumsum(density, 0) - 0.5 * density) / levels
    pressure_pad = pad_levels(pressure)
    surface_pad = pad_plane(new_surface)
    level_index = jnp.arange(levels, dtype=jnp.int32)
    bottom = (level_index == levels - 1).astype(jnp.float32)[:, None, None]
    new_east = east_open[1:-1, 1:] * (
        east_velocity - gravity_rate * (surface_pad[1:-1, 2:] - surface_pad[1:-1, 1:-1])
        - (pressure_pad[:, 1:-1, 2:] - pressure_pad[:, 1:-1, 1:-1])
        + viscous_rate * laplace(east_pad) - friction_rate * bottom * east_velocity)
    new_north = north_open[1:, 1:-1] * (
        north_velocity - gravity_rate * (surface_pad[2:, 1:-1] - surface_pad[1:-1, 1:-1])
        - (pressure_pad[:, 2:, 1:-1] - pressure_pad[:, 1:-1, 1:-1])
        + viscous_rate * laplace(north_pad) - friction_rate * bottom * north_velocity)
    has_above = (level_index > 0).astype(jnp.float32)[:, None, None]
    has_below = (level_index < levels - 1).astype(jnp.float32)[:, None, None]

    def one_tracer(field):
        advected = advect(pad_levels(field), east_flux, north_flux, depth, levels)
        zero_level = jnp.zeros_like(advected[:1])
        level_above = jnp.concatenate([zero_level, advected[:-1]], 0)
        level_below = jnp.concatenate([advected[1:], zero_level], 0)
        blended = vertical_mix(advected, level_above, level_below, has_above, has_below)
        return field + wet_cells * (blended - field)

    updated = lax.map(one_tracer, tracers)
    warming = jnp.exp(warming_rate * updated[1])
    reaction = jnp.einsum('ab,blyx->alyx', kinetics, updated, precision=lax.Precision.HIGHEST)
    river_index = jnp.arange(river_cells.shape[0], dtype=jnp.int32)
    tile = river_index // RIV_DEV
    river_rows = (tile // N_TX) * CY + river_cells // CX
    river_cols = (tile % N_TX) * CX + river_cells % CX
    source = jnp.zeros((tracers.shape[0],) + depth.shape, jnp.float32)
    source = source.at[:, river_rows, river_cols].add(river_loads.T)
    level_top = (level_index == 0).astype(jnp.float32)[:, None, None]
    new_tracers = updated + wet_cells * (warming * reaction + level_top * source[:, None])
    return new_tracers, new_east, new_north, new_surface
```

```python
from functools import partial

import jax
import jax.numpy as jnp
from jax import lax
from jax.experimental import pallas as pl
from jax.experimental.pallas import tpu as pltpu
from jax.sharding import PartitionSpec as P

eta_rate = 0.25
gravity_rate = 0.25
baroclinic_rate = 0.4
viscous_rate = 0.1
friction_rate = 0.3
advect_rate = 0.3
mixing_rate = 0.2
haline_coef = 0.8
thermal_coef = 0.2
warming_rate = 0.46

f32 = jnp.float32
SUB = 8


def lanes_of(shape):
    return lax.broadcasted_iota(jnp.int32, shape, len(shape) - 1)


def rows_of(shape):
    return lax.broadcasted_iota(jnp.int32, shape, len(shape) - 2)


def east_of(x):
    return pltpu.roll(x, x.shape[-1] - 1, x.ndim - 1)


def west_of(x):
    return pltpu.roll(x, 1, x.ndim - 1)


def north_of(x):
    return pltpu.roll(x, x.shape[-2] - 1, x.ndim - 2)


def south_of(x):
    return pltpu.roll(x, 1, x.ndim - 2)


def keep(ref, rows, value):
    ref[rows, :] = value


def closed_kernel(
    where_ref, c_ref, u_ref, v_ref, depth_ref, wet_ref,
    x_lo, x_hi, m_lo, m_hi, fields_ref, north_ref, south_ref, sides_ref,
    coef_ref, turned_ref, *, levels, tracer_count, chunk,
):
    slot, part = pl.program_id(0), pl.program_id(1)
    height, width = depth_ref.shape
    half = height // 2
    lane = lanes_of((height, width))

    def edges(field, q):
        keep(north_ref, pl.ds(q, 1), field[height - 1:, :])
        keep(south_ref, pl.ds(q, 1), field[:1, :])
        moved = pltpu.roll(field, 2 * q + 1, 1)
        turned_ref[...] = jnp.where(lane // 2 == q, moved, turned_ref[...])

    @pl.when((slot == 0) & (part == 0))
    def _():
        north_ref[...] = jnp.zeros_like(north_ref)
        south_ref[...] = jnp.zeros_like(south_ref)
        turned_ref[...] = jnp.zeros_like(turned_ref)
        edges(depth_ref[...], 2 * tracer_count + 4)
        edges(wet_ref[...].astype(f32), 2 * tracer_count + 5)

    @pl.when(part == 0)
    def _():
        depth = depth_ref[...]
        wet = wet_ref[...].astype(f32)
        u, v = u_ref[...], v_ref[...]
        edges(u, 2 * tracer_count + slot)
        edges(v, 2 * tracer_count + 2 + slot)
        flow_e = u * (0.5 * (depth + east_of(depth)) * (wet * east_of(wet))) / levels
        flow_e = jnp.where(lane < width - 1, flow_e, 0.0)
        flow_n = v * (0.5 * (depth + north_of(depth)) * (wet * north_of(wet))) / levels
        flow_n = jnp.where(rows_of((height, width)) < height - 1, flow_n, 0.0)
        flow_w, flow_s = west_of(flow_e), south_of(flow_n)
        scale = advect_rate * levels / depth
        coef_ref[0] = 1.0 - scale * (
            jnp.maximum(flow_e, 0.0) - jnp.minimum(flow_w, 0.0)
            + jnp.maximum(flow_n, 0.0) - jnp.minimum(flow_s, 0.0)
        )
        coef_ref[1] = -scale * jnp.minimum(flow_e, 0.0)
        coef_ref[2] = scale * jnp.maximum(flow_w, 0.0)
        coef_ref[3] = -scale * jnp.minimum(flow_n, 0.0)
        coef_ref[4] = scale * jnp.maximum(flow_s, 0.0)
        fields_ref[slot] = flow_e - flow_w + flow_n - flow_s
        fields_ref[2 + slot] = haline_coef * c_ref[0] - thermal_coef * c_ref[1]

    for t in range(chunk):
        c = c_ref[t]
        edges(c, slot * tracer_count + part * chunk + t)
        moved = (
            coef_ref[0] * c + coef_ref[1] * east_of(c) + coef_ref[2] * west_of(c)
            + coef_ref[3] * north_of(c) + coef_ref[4] * south_of(c)
        )

        @pl.when(slot == 0)
        def _():
            x_lo[t] = moved[:half]
            x_hi[t] = moved[half:]

        @pl.when(slot == 1)
        def _():
            m_lo[t] = moved[:half]
            m_hi[t] = moved[half:]

    @pl.when((slot == 1) & (part == pl.num_programs(1) - 1))
    def _():
        sides_ref[...] = turned_ref[...].T[: sides_ref.shape[0]]


def closed_advection(where, tracers, u, v, depth, wet_mask, levels, chunk=8):
    count, _, height, width = tracers.shape
    parts = count // chunk
    half = height // 2
    edge_rows = -(-(2 * count + 6) // SUB) * SUB
    plane = lambda s, c, w: (0, 0)
    level = pl.BlockSpec((None, height, width), lambda s, c, w: (w[s], 0, 0))
    x_out = pl.BlockSpec((chunk, half, width), lambda s, c, w: (jnp.where(s == 0, c, parts - 1), 0, 0))
    m_out = pl.BlockSpec((chunk, half, width), lambda s, c, w: (jnp.where(s == 0, 0, c), 0, 0))
    piece = jax.ShapeDtypeStruct((count, half, width), f32)
    return pl.pallas_call(
        partial(closed_kernel, levels=levels, tracer_count=count, chunk=chunk),
        grid_spec=pltpu.PrefetchScalarGridSpec(
            num_scalar_prefetch=1,
            grid=(2, parts),
            in_specs=[
                pl.BlockSpec((chunk, None, height, width), lambda s, c, w: (c, w[s], 0, 0)),
                level, level,
                pl.BlockSpec((height, width), plane),
                pl.BlockSpec((height, width), plane),
            ],
            out_specs=[
                x_out, x_out, m_out, m_out,
                pl.BlockSpec((4, height, width), lambda s, c, w: (0, 0, 0)),
                pl.BlockSpec((edge_rows, width), plane),
                pl.BlockSpec((edge_rows, width), plane),
                pl.BlockSpec((2 * edge_rows, height), plane),
            ],
            scratch_shapes=[pltpu.VMEM((5, height, width), f32), pltpu.VMEM((height, width), f32)],
        ),
        out_shape=[
            piece, piece, piece, piece,
            jax.ShapeDtypeStruct((4, height, width), f32),
            jax.ShapeDtypeStruct((edge_rows, width), f32),
            jax.ShapeDtypeStruct((edge_rows, width), f32),
            jax.ShapeDtypeStruct((2 * edge_rows, height), f32),
        ],
        compiler_params=pltpu.CompilerParams(dimension_semantics=("arbitrary", "arbitrary")),
        name="closed",
    )(where, tracers, u, v, depth, wet_mask)


def faces_kernel(
    where_ref, fields_ref, north_ref, south_ref, sides_ref, from_north_ref, from_south_ref,
    from_west_ref, from_east_ref, packet_ref, other_ref, *, levels, tracer_count,
):
    count = tracer_count
    height, width = fields_ref.shape[1:]
    half_rows = sides_ref.shape[0] // 2
    us, vs, ds, ws = 2 * count, 2 * count + 2, 2 * count + 4, 2 * count + 5
    east, west = (pl.ds(0, half_rows, stride=2), pl.ds(1, half_rows, stride=2))
    own = (north_ref[...], south_ref[...], sides_ref[west, :], sides_ref[east, :])
    halo = (from_north_ref[...], from_south_ref[...], from_west_ref[east, :], from_east_ref[west, :])
    known = (1.0, 1.0, where_ref[2].astype(f32), where_ref[3].astype(f32))

    def side(k, slot):
        mine, theirs = own[k], halo[k]
        outgoing = k in (0, 3)
        speed = (mine if outgoing else theirs)[(vs if k < 2 else us) + slot:][:1]
        d_mine, d_theirs = mine[ds:ds + 1], theirs[ds:ds + 1]
        opened = mine[ws:ws + 1] * (theirs[ws:ws + 1] * known[k])
        flow = speed * (0.5 * (d_mine + d_theirs) * opened) / levels
        c_mine = mine[slot * count:(slot + 1) * count]
        c_theirs = theirs[slot * count:(slot + 1) * count]
        scale = advect_rate * levels / d_mine
        if outgoing:
            return -scale * (jnp.maximum(flow, 0.0) * c_mine + jnp.minimum(flow, 0.0) * c_theirs), flow
        return scale * (jnp.maximum(flow, 0.0) * c_theirs + jnp.minimum(flow, 0.0) * c_mine), -flow

    flows = [0.0, 0.0, 0.0, 0.0]
    for slot in range(2):
        ref, at = (packet_ref, 2 * height) if slot == 0 else (other_ref, 0)
        for k in range(4):
            fix, flow = side(k, slot)
            flows[k] = flows[k] + flow
            if k < 2:
                ref[pl.ds(at + k * count, count), :] = fix
            else:
                for t in range(count):
                    ref[pl.ds(at + 2 * count + 2 * t + 3 - k, 1), :] = fix[t:t + 1]
    lane, row = lanes_of((height, width)), rows_of((height, width))
    spill = jnp.concatenate([flows[3], flows[2], jnp.zeros((width - 2, height), f32)], 0).T
    spill = east_of(spill)
    spill = jnp.where((lane == 0) | (lane == width - 1), spill, 0.0)
    spill = spill + jnp.where(row == 0, flows[1], 0.0) + jnp.where(row == height - 1, flows[0], 0.0)
    packet_ref[pl.ds(0, height), :] = fields_ref[0] + fields_ref[1] + spill
    packet_ref[pl.ds(height, height), :] = fields_ref[2] + fields_ref[3]


def face_corrections(where, fields, north, south, sides, halos, levels, count):
    height, width = fields.shape[1:]
    return pl.pallas_call(
        partial(faces_kernel, levels=levels, tracer_count=count),
        grid_spec=pltpu.PrefetchScalarGridSpec(num_scalar_prefetch=1, grid=(1,), in_specs=[
            pl.BlockSpec(a.shape, lambda i, w, r=a.ndim: (0,) * r)
            for a in (fields, north, south, sides, *halos)
        ], out_specs=[
            pl.BlockSpec((2 * height + 4 * count, width), lambda i, w: (0, 0)),
            pl.BlockSpec((4 * count, width), lambda i, w: (0, 0)),
        ]),
        out_shape=[
            jax.ShapeDtypeStruct((2 * height + 4 * count, width), f32),
            jax.ShapeDtypeStruct((4 * count, width), f32),
        ],
        name="faces",
    )(where, fields, north, south, sides, *halos)


def surface_kernel(
    where_ref, packet_ref, near_ref, far_ref, fields_ref, surface_ref, depth_ref, wet_ref,
    surface_out, pressure_out, south_out, west_out, *, levels,
):
    height, width = surface_ref.shape
    top, below = pl.ds(0, height), pl.ds(height, height)
    near_above, far_above = where_ref[4].astype(f32), where_ref[5].astype(f32)
    total = packet_ref[top, :] + near_ref[top, :] + far_ref[top, :]
    surface = surface_ref[...] - eta_rate * wet_ref[...].astype(f32) * total
    above = near_above * near_ref[below, :] + far_above * far_ref[below, :]
    surface_out[...] = surface
    lane = lanes_of((height, width))
    turned = jnp.where(lane == 0, surface, 0.0)
    south_out[...] = jnp.zeros_like(south_out)
    keep(south_out, pl.ds(0, 1), surface[:1])
    for slot in range(2):
        lower = where_ref[slot].astype(f32)
        density = fields_ref[2 + slot]
        column = above + lower * fields_ref[3 - slot] + density - 0.5 * density
        pressure = baroclinic_rate * depth_ref[...] * column / levels
        pressure_out[slot] = pressure
        keep(south_out, pl.ds(1 + slot, 1), pressure[:1])
        turned = jnp.where(lane == 1 + slot, pltpu.roll(pressure, 1 + slot, 1), turned)
    west_out[...] = turned.T[:SUB]


def new_surface_and_pressure(where, packet, near, far, fields, surface, depth, wet_mask, levels):
    height, width = surface.shape
    args = (packet, near, far, fields, surface, depth, wet_mask)
    outs = [(height, width), (2, height, width), (SUB, width), (SUB, height)]
    return pl.pallas_call(
        partial(surface_kernel, levels=levels),
        grid_spec=pltpu.PrefetchScalarGridSpec(num_scalar_prefetch=1, grid=(1,), in_specs=[
            pl.BlockSpec(a.shape, lambda i, w, r=a.ndim: (0,) * r) for a in args
        ], out_specs=[pl.BlockSpec(s, lambda i, w, r=len(s): (0,) * r) for s in outs]),
        out_shape=[jax.ShapeDtypeStruct(s, f32) for s in outs],
        name="level",
    )(where, *args)


def momentum_kernel(
    where_ref, u_ref, v_ref, depth_ref, wet_ref, surface_ref, pressure_ref, from_north_ref,
    from_south_ref, from_west_ref, from_east_ref, north_state_ref, east_state_ref,
    east_out, north_out, *, count,
):
    height, width = depth_ref.shape
    lane, row = lanes_of((height, width)), rows_of((height, width))
    us, vs, ds, ws = 2 * count, 2 * count + 2, 2 * count + 4, 2 * count + 5
    half_rows = from_west_ref.shape[0] // 2
    known_w, known_e = where_ref[2].astype(f32), where_ref[3].astype(f32)
    west_halo = from_west_ref[pl.ds(0, half_rows, stride=2), :][us:us + SUB] * known_w
    east_halo = from_east_ref[pl.ds(1, half_rows, stride=2), :][us:us + SUB] * known_e
    used = 3 * SUB
    columns = jnp.concatenate(
        [west_halo, east_halo, east_state_ref[...], jnp.zeros((width - used, height), f32)], 0
    ).T
    north_halo, south_halo = from_north_ref[...], from_south_ref[...]

    def shifted(field, q, state=None):
        e_from = SUB + q if state is None else 2 * SUB + state
        e = jnp.where(lane == width - 1, pltpu.roll(columns, width - 1 - e_from, 1), east_of(field))
        line = north_halo[us + q:us + q + 1] if state is None else north_state_ref[pl.ds(state, 1), :]
        n = jnp.where(row == height - 1, line, north_of(field))
        return e, n

    def whole(field, q):
        e, n = shifted(field, q)
        w = jnp.where(lane == 0, pltpu.roll(columns, (width - q) % width, 1), west_of(field))
        s = jnp.where(row == 0, south_halo[us + q:us + q + 1], south_of(field))
        return n + s + e + w - 4.0 * field

    wet = wet_ref[...].astype(f32)
    wet_e, wet_n = shifted(wet, 5)
    open_e, open_n = wet * wet_e, wet * wet_n
    surface = surface_ref[...]
    surface_e, surface_n = shifted(surface, 0, 0)
    for slot in range(2):
        at = where_ref[slot]
        bottom = where_ref[6].astype(f32) * at.astype(f32)
        pressure = pressure_ref[slot]
        pressure_e, pressure_n = shifted(pressure, 0, 1 + slot)
        u, v = u_ref[at], v_ref[at]
        east_out[at] = open_e * (
            u - gravity_rate * (surface_e - surface) - (pressure_e - pressure)
            + viscous_rate * whole(u, slot) - friction_rate * bottom * u
        )
        north_out[at] = open_n * (
            v - gravity_rate * (surface_n - surface) - (pressure_n - pressure)
            + viscous_rate * whole(v, 2 + slot) - friction_rate * bottom * v
        )


def momentum(where, u, v, depth, wet_mask, surface, pressure, halos, states, count):
    args = (u, v, depth, wet_mask, surface, pressure, *halos, *states)
    return pl.pallas_call(
        partial(momentum_kernel, count=count),
        grid_spec=pltpu.PrefetchScalarGridSpec(num_scalar_prefetch=1, grid=(1,), in_specs=[
            pl.BlockSpec(a.shape, lambda i, w, r=a.ndim: (0,) * r) for a in args
        ], out_specs=[pl.BlockSpec(u.shape, lambda i, w: (0, 0, 0))] * 2),
        out_shape=[jax.ShapeDtypeStruct(u.shape, f32)] * 2,
        name="momentum",
    )(where, *args)


def react_kernel(
    where_ref, cells_ref, loads_ref, c_ref, own_ref, other_ref, next_ref, own_fix, other_fix,
    next_fix, wet_ref, rates_ref, *rest, slot, base, fix_at, count,
):
    out_ref, fix_ref, turned_ref = rest[-3:]
    step = pl.program_id(0)
    height_here, width = out_ref.shape[1:]
    height = turned_ref.shape[0]
    first = base + step * height_here
    has_next = 1.0 if slot == 0 else where_ref[7].astype(f32)
    keep_rate = 1.0 - mixing_rate - mixing_rate * has_next
    next_rate = mixing_rate * has_next

    @pl.when(step == 0)
    def _():
        size = 4 * count
        mixed = (
            keep_rate * own_fix[pl.ds(fix_at[0], size), :]
            + mixing_rate * other_fix[pl.ds(fix_at[1], size), :]
            + next_rate * next_fix[pl.ds(fix_at[2], size), :]
        )
        fix_ref[...] = mixed
        columns = jnp.concatenate([mixed[2 * count:], jnp.zeros((width - 2 * count, height), f32)], 0)
        turned_ref[...] = columns.T

    shape = (height_here, width)
    lane, row = lanes_of(shape), rows_of(shape) + first
    rim = (lane == 0) | (lane == width - 1)
    columns = turned_ref[pl.ds(pl.multiple_of(first, SUB), height_here), :]
    wet = wet_ref[...] != 0
    values = []
    for t in range(count):
        mixed = keep_rate * own_ref[t] + mixing_rate * other_ref[t] + next_rate * next_ref[t]
        mixed = mixed + jnp.where(rim, pltpu.roll(columns, width - 1 - 2 * t, 1), 0.0)
        if base == 0:
            mixed = mixed + jnp.where(row == 0, fix_ref[pl.ds(count + t, 1), :], 0.0)
        else:
            mixed = mixed + jnp.where(row == height - 1, fix_ref[pl.ds(t, 1), :], 0.0)
        values.append(jnp.where(wet, mixed, c_ref[t]))
    groups = height_here // SUB
    stacked = jnp.concatenate(
        [
            jnp.concatenate([value[k * SUB:(k + 1) * SUB] for value in values], 0)
            for k in range(groups)
        ],
        1,
    )
    reaction = jnp.dot(
        rates_ref[...], stacked, precision=lax.Precision.HIGHEST, preferred_element_type=f32
    )
    warming = jnp.where(wet, jnp.exp(warming_rate * values[1]), 0.0)
    for t in range(count):
        gained = jnp.concatenate(
            [reaction[t * SUB:(t + 1) * SUB, k * width:(k + 1) * width] for k in range(groups)], 0
        )
        out_ref[t] = values[t] + warming * gained

    if slot == 1:
        for r in range(cells_ref.shape[0]):
            cell = cells_ref[r]
            line, spot = cell // width, cell % width

            @pl.when((where_ref[8] == 1) & (line >= first) & (line < first + height_here))
            def _():
                at = pl.ds(line - first, 1)
                here = (lanes_of((1, width)) == spot) & (wet_ref[at, :] != 0)
                for t in range(count):
                    load = loads_ref[r, t]
                    out_ref[t, at, :] = out_ref[t, at, :] + jnp.where(here, load, 0.0)


def react(where, cells, loads, tracers, own, other, received, fixes, fix_at, wet_mask, rates,
          slot, base, into=None, rows=32):
    count, _, height, width = tracers.shape
    span = own.shape[1]
    steps, before = span // rows, base // rows
    piece = pl.BlockSpec((count, rows, width), lambda i, w, *_: (0, i, 0))
    level = pl.BlockSpec((count, None, rows, width), lambda i, w, *_: (0, w[slot], before + i, 0))
    whole = lambda a: pl.BlockSpec(a.shape, lambda i, w, *_: (0, 0))
    args = [tracers, own, other, received, *fixes, wet_mask, rates]
    specs = [level, piece, piece, piece, *(whole(a) for a in fixes),
             pl.BlockSpec((rows, width), lambda i, w, *_: (before + i, 0)), whole(rates)]
    aliases = {}
    if into is not None:
        aliases = {3 + len(args): 0}
        args.append(into)
        specs.append(pl.BlockSpec(memory_space=pl.ANY))
    return pl.pallas_call(
        partial(react_kernel, slot=slot, base=base, fix_at=fix_at, count=count),
        grid_spec=pltpu.PrefetchScalarGridSpec(
            num_scalar_prefetch=3, grid=(steps,), in_specs=specs, out_specs=level,
            scratch_shapes=[pltpu.VMEM((4 * count, width), f32), pltpu.VMEM((height, width), f32)],
        ),
        out_shape=jax.ShapeDtypeStruct(tracers.shape, f32),
        input_output_aliases=aliases,
        compiler_params=pltpu.CompilerParams(dimension_semantics=("arbitrary",)),
        name="react",
    )(where, cells, loads, *args)


def shards(tracers, u, v, surface, depth, wet_mask, river_cells, river_loads, kinetics):
    count, own_levels, height, width = tracers.shape
    groups, tys, txs = (lax.axis_size(a) for a in ("grp", "ty", "tx"))
    levels = own_levels * groups
    assert own_levels == 2 and groups in (2, 4)
    g, x = lax.axis_index("grp"), lax.axis_index("tx")
    odd = g % 2
    where = jnp.stack([
        1 - odd, odd, x > 0, x < txs - 1, odd, g // 2, g == groups - 1,
        (g > 0) & (g < groups - 1), g == 0,
    ]).astype(jnp.int32)
    x_lo, x_hi, m_lo, m_hi, fields, north, south, sides = closed_advection(
        where, tracers, u, v, depth, wet_mask, levels
    )
    swap = [(i, i ^ 1) for i in range(groups)]
    middle = [(i, i + 1) for i in range(1, groups - 1, 2)]
    middle = middle + [(b, a) for a, b in middle]
    near_x_lo = lax.ppermute(x_lo, "grp", swap)
    near_x_hi = lax.ppermute(x_hi, "grp", swap)
    if groups == 4:
        handed = lax.ppermute(m_hi, "grp", [(1, 3), (2, 0)])
        near_m_hi = lax.ppermute(handed, "grp", [(3, 2), (0, 1)])
    else:
        near_m_hi = lax.ppermute(m_hi, "grp", middle)
    near_m_lo = lax.ppermute(m_lo, "grp", middle)

    up = [(i, i + 1) for i in range(tys - 1)]
    down = [(i + 1, i) for i in range(tys - 1)]
    from_south = lax.ppermute(north, "ty", up)
    from_north = lax.ppermute(south, "ty", down)
    if txs == 2:
        from_west = from_east = lax.ppermute(sides, "tx", [(0, 1), (1, 0)])
    else:
        from_west = lax.ppermute(sides, "tx", [(i, i + 1) for i in range(txs - 1)])
        from_east = lax.ppermute(sides, "tx", [(i + 1, i) for i in range(txs - 1)])
    halos = (from_north, from_south, from_west, from_east)
    packet, fix_m = face_corrections(where, fields, north, south, sides, halos, levels, count)
    near = lax.ppermute(packet, "grp", swap)
    near_fix_m = lax.ppermute(fix_m, "grp", middle)
    columns = packet[:2 * height] + near[:2 * height]
    if groups == 4:
        far = lax.ppermute(columns, "grp", [(i, i ^ 2) for i in range(groups)])
    else:
        far = jnp.zeros_like(columns)
    new_surface, pressure, south_state, west_state = new_surface_and_pressure(
        where, packet, near, far, fields, surface, depth, wet_mask, levels
    )
    north_state = lax.ppermute(south_state, "ty", down)
    east_state = lax.ppermute(west_state, "tx", [(i + 1, i) for i in range(txs - 1)])
    new_east, new_north = momentum(
        where, u, v, depth, wet_mask, new_surface, pressure, halos, (north_state, east_state), count
    )

    rates = jnp.kron(kinetics, jnp.eye(SUB, dtype=f32))
    common = (where, river_cells, river_loads, tracers)
    at = 2 * height
    half = height // 2
    x_fix = ((packet, fix_m, near), (at, 0, at))
    m_fix = ((fix_m, packet, near_fix_m), (0, at, 0))
    out = react(*common, x_lo, m_lo, near_x_lo, *x_fix, wet_mask, rates, 0, 0)
    out = react(*common, x_hi, m_hi, near_x_hi, *x_fix, wet_mask, rates, 0, half, out)
    out = react(*common, m_lo, x_lo, near_m_lo, *m_fix, wet_mask, rates, 1, 0, out)
    out = react(*common, m_hi, x_hi, near_m_hi, *m_fix, wet_mask, rates, 1, half, out)
    return (out, new_east, new_north, new_surface)


def solution(mesh):
    field = P("grp", "ty", "tx")
    plane = P("ty", "tx")
    return jax.shard_map(
        shards,
        mesh=mesh,
        in_specs=(
            P(None, "grp", "ty", "tx"), field, field, plane, plane, plane,
            P(("ty", "tx")), P(("ty", "tx"), None), P(),
        ),
        out_specs=(P(None, "grp", "ty", "tx"), field, field, plane),
        check_vma=False,
    )
```

```python
from functools import partial

import jax
import jax.numpy as jnp
from jax import lax
from jax.experimental import pallas as pl
from jax.experimental.pallas import tpu as pltpu
from jax.sharding import PartitionSpec as P


eta_rate = 0.25
gravity_rate = 0.25
baroclinic_rate = 0.4
viscous_rate = 0.1
friction_rate = 0.3
advect_rate = 0.3
mixing_rate = 0.2
haline_coef = 0.8
thermal_coef = 0.2
warming_rate = 0.46

f32 = jnp.float32
SUB = 8


def lanes_of(shape):
    return lax.broadcasted_iota(jnp.int32, shape, len(shape) - 1)


def rows_of(shape):
    return lax.broadcasted_iota(jnp.int32, shape, len(shape) - 2)


def east_of(x):
    return pltpu.roll(x, x.shape[-1] - 1, x.ndim - 1)


def west_of(x):
    return pltpu.roll(x, 1, x.ndim - 1)


def north_of(x):
    return pltpu.roll(x, x.shape[-2] - 1, x.ndim - 2)


def south_of(x):
    return pltpu.roll(x, 1, x.ndim - 2)


def keep(ref, rows, value):
    ref[rows, :] = value


VM = pl.BlockSpec(memory_space=pltpu.VMEM)


small = pltpu.CompilerParams(vmem_limit_bytes=16 << 20)


def near_core(*arrays):
    return [pltpu.with_memory_space_constraint(a, pltpu.VMEM) for a in arrays]


def far_core(*arrays):
    return [pltpu.with_memory_space_constraint(a, pltpu.HBM) for a in arrays]


def kept(shape):
    return pltpu.VMEM(shape, f32)


SM = pl.BlockSpec(memory_space=pltpu.SMEM)
HB = pl.BlockSpec(memory_space=pl.ANY)


def places():
    g, groups = lax.axis_index("grp"), lax.axis_size("grp")
    return g, groups, (1 - g % 2, g % 2)


def as_f32(flag):
    return jnp.where(flag, 1.0, 0.0).astype(f32)


def pick(refs, row):
    for ref in refs:
        if row < ref.shape[1]:
            return ref, row
        row -= ref.shape[1]


def strips(height, strip, *parts):
    ends = {height}
    for part in parts:
        ends |= {sum(part[:k + 1]) for k in range(len(part))}
    first = 0
    while first < height:
        size = min(strip, min(e for e in ends if e > first) - first)
        yield first, size
        first += size


def rows_in(parts):
    return [p.shape[1] for p in parts]


def weights(coef_ref, u, v, depth, wet, levels):
    height, width = depth.shape
    lane, row = lanes_of((height, width)), rows_of((height, width))
    half_e = 0.5 * (depth + east_of(depth)) * (wet * east_of(wet))
    half_n = 0.5 * (depth + north_of(depth)) * (wet * north_of(wet))
    flow_e = jnp.where(lane < width - 1, u * half_e / levels, 0.0)
    flow_n = jnp.where(row < height - 1, v * half_n / levels, 0.0)
    flow_w, flow_s = west_of(flow_e), south_of(flow_n)
    scale = advect_rate * levels / depth
    coef_ref[0] = 1.0 - scale * (
        jnp.maximum(flow_e, 0.0) - jnp.minimum(flow_w, 0.0)
        + jnp.maximum(flow_n, 0.0) - jnp.minimum(flow_s, 0.0)
    )
    coef_ref[1] = -scale * jnp.minimum(flow_e, 0.0)
    coef_ref[2] = scale * jnp.maximum(flow_w, 0.0)
    coef_ref[3] = -scale * jnp.minimum(flow_n, 0.0)
    coef_ref[4] = scale * jnp.maximum(flow_s, 0.0)
    return flow_e - flow_w + flow_n - flow_s


def weighed(coefs, c, above, under):
    return (
        coefs[0] * c + coefs[1] * east_of(c) + coefs[2] * west_of(c)
        + coefs[3] * above + coefs[4] * under
    )


def early_kernel(
    c_hbm, u_hbm, v_hbm, depth_hbm, wet_hbm, out_ref,
    c_ref, u_ref, v_ref, depth_ref, wet_ref, coef_ref, flat_sem, c_sem, *, levels, strip,
):
    _, _, at_level = places()
    count, taken, _ = c_ref.shape
    at, rows = at_level[0], pl.ds(0, taken)
    flat = [
        pltpu.make_async_copy(h, r, flat_sem.at[k])
        for k, (h, r) in enumerate((
            (depth_hbm.at[rows], depth_ref), (wet_hbm.at[rows], wet_ref),
            (u_hbm.at[at, rows], u_ref), (v_hbm.at[at, rows], v_ref),
        ))
    ]
    bulk = pltpu.make_async_copy(c_hbm.at[:, at, rows], c_ref, c_sem)
    for copy in flat:
        copy.start()
    bulk.start()
    for copy in flat:
        copy.wait()
    weights(coef_ref, u_ref[...], v_ref[...], depth_ref[...], wet_ref[...].astype(f32), levels)
    bulk.wait()
    for first in range(0, out_ref.shape[1], strip):
        here = pl.ds(first, strip)
        coefs = [coef_ref[k, here, :] for k in range(5)]
        for t in range(count):
            c = c_ref[t, here, :]
            above = c_ref[t, pl.ds(first + 1, strip), :]
            under = c_ref[t, pl.ds(first - 1, strip), :] if first else south_of(c)
            out_ref[t, here, :] = weighed(coefs, c, above, under)


def early_advection(tracers, u, v, depth, wet_mask, levels, rows, strip=16):
    count, _, _, width = tracers.shape
    taken = rows + SUB
    plane = pltpu.VMEM((taken, width), f32)
    return pl.pallas_call(
        partial(early_kernel, levels=levels, strip=strip),
        in_specs=[HB] * 5,
        out_specs=VM,
        out_shape=kept((count, rows, width)),
        scratch_shapes=[
            pltpu.VMEM((count, taken, width), f32), plane, plane, plane,
            pltpu.VMEM((taken, width), jnp.int32), pltpu.VMEM((5, taken, width), f32),
            pltpu.SemaphoreType.DMA((4,)), pltpu.SemaphoreType.DMA,
        ],
        compiler_params=small,
        name="early",
    )(*far_core(tracers, u, v, depth, wet_mask))


def closed_kernel(
    c_hbm, u_hbm, v_hbm, depth_hbm, wet_hbm,
    c_ref, x_hi, m_lo, m_hi, m_top, fields_ref, north_ref, south_ref, sides_ref,
    u_ref, v_ref, depth_ref, wet_ref, coef_ref, turned_ref, flat_sem, c_sem,
    *, levels, count, parts, strip,
):
    _, _, at_level = places()
    height, width = depth_ref.shape
    sent = height - x_hi.shape[1]
    chunk = count // parts
    flat = [
        pltpu.make_async_copy(h, r, flat_sem.at[k])
        for k, (h, r) in enumerate(
            ((depth_hbm, depth_ref), (wet_hbm, wet_ref), (u_hbm, u_ref), (v_hbm, v_ref))
        )
    ]
    for copy in flat:
        copy.start()
    bulk = []
    for slot in range(2):
        for part in range(parts):
            some = pl.ds(part * chunk, chunk)
            bulk.append(pltpu.make_async_copy(
                c_hbm.at[some, at_level[slot]], c_ref.at[slot, some], c_sem.at[slot, part]
            ))
            bulk[-1].start()
    north_ref[...] = jnp.zeros_like(north_ref)
    south_ref[...] = jnp.zeros_like(south_ref)
    for copy in flat:
        copy.wait()
    depth, wet = depth_ref[...], wet_ref[...].astype(f32)

    def lines(field, q):
        keep(north_ref, pl.ds(q, 1), field[height - 1:])
        keep(south_ref, pl.ds(q, 1), field[:1])

    def gather(got, field, q):
        mask = lanes_of((1, width)) // 2 == q
        return jnp.where(mask, pltpu.roll(field, (2 * q + 1) % width, 1), got)

    turned = jnp.zeros((height, width), f32)
    for q, field in ((4, depth), (5, wet)):
        lines(field, 2 * count + q)
        turned = gather(turned, field, 2 * count + q)
    for slot in range(2):
        u, v = u_ref[at_level[slot]], v_ref[at_level[slot]]
        lines(u, 2 * count + slot)
        lines(v, 2 * count + 2 + slot)
        turned = gather(turned, u, 2 * count + slot)
        turned = gather(turned, v, 2 * count + 2 + slot)
        fields_ref[slot] = weights(coef_ref.at[slot], u, v, depth, wet, levels)
    turned_ref[...] = turned

    for slot in range(2):
        for part in range(parts):
            bulk[slot * parts + part].wait()
            if part == 0:
                fields_ref[2 + slot] = haline_coef * c_ref[slot, 0] - thermal_coef * c_ref[slot, 1]
            cut = (rows_in((m_lo, m_hi, m_top)), [sent])[1 - slot]
            for first, size in strips(height, strip, cut):
                here = pl.ds(first, size)
                coefs = [coef_ref[slot, k, here, :] for k in range(5)]
                got = turned_ref[here, :]
                for t in range(part * chunk, (part + 1) * chunk):
                    q = slot * count + t
                    c = c_ref[slot, t, here, :]
                    got = gather(got, c, q)
                    if first == 0:
                        keep(south_ref, pl.ds(q, 1), c[:1])
                    if first + size == height:
                        keep(north_ref, pl.ds(q, 1), c[size - 1:])
                    if slot == 0 and first < sent:
                        continue
                    if first + size < height:
                        above = c_ref[slot, t, pl.ds(first + 1, size), :]
                    else:
                        above = north_of(c)
                    under = c_ref[slot, t, pl.ds(first - 1, size), :] if first else south_of(c)
                    moved = weighed(coefs, c, above, under)
                    if slot == 0:
                        x_hi[t, pl.ds(first - sent, size), :] = moved
                    else:
                        to, at = pick((m_lo, m_hi, m_top), first)
                        to[t, pl.ds(at, size), :] = moved
                turned_ref[here, :] = got
    sides_ref[...] = turned_ref[...].T[: sides_ref.shape[0]]


def closed_advection(tracers, u, v, depth, wet_mask, levels, sent, cut, parts=2, strip=16):
    count, _, height, width = tracers.shape
    edge_rows = -(-(2 * count + 6) // SUB) * SUB
    assert width == height and 2 * edge_rows <= width
    outs = [
        kept((2, count, height, width)), kept((count, height - sent, width)),
        *(kept((count, rows, width)) for rows in cut), kept((4, height, width)),
        kept((edge_rows, width)), kept((edge_rows, width)), kept((2 * edge_rows, height)),
    ]
    plane = pltpu.VMEM((height, width), f32)
    return pl.pallas_call(
        partial(closed_kernel, levels=levels, count=count, parts=parts, strip=strip),
        in_specs=[HB] * 5,
        out_specs=[VM] * len(outs),
        out_shape=outs,
        scratch_shapes=[
            pltpu.VMEM(u.shape, f32), pltpu.VMEM(v.shape, f32), plane,
            pltpu.VMEM((height, width), jnp.int32), pltpu.VMEM((2, 5, height, width), f32), plane,
            pltpu.SemaphoreType.DMA((4,)), pltpu.SemaphoreType.DMA((2, parts)),
        ],
        compiler_params=small,
        name="closed",
    )(*far_core(tracers, u, v, depth, wet_mask))


def faces_kernel(
    fields_ref, north_ref, south_ref, sides_ref, from_north_ref, from_south_ref,
    from_west_ref, from_east_ref, packet_ref, x_fix_ref, m_fix_ref, *, levels, count,
):
    height, width = fields_ref.shape[1:]
    x, txs = lax.axis_index("tx"), lax.axis_size("tx")
    half_rows = sides_ref.shape[0] // 2
    us, vs, ds, ws = 2 * count, 2 * count + 2, 2 * count + 4, 2 * count + 5
    east, west = (pl.ds(0, half_rows, stride=2), pl.ds(1, half_rows, stride=2))
    own = (north_ref[...], south_ref[...], sides_ref[west, :], sides_ref[east, :])
    halo = (from_north_ref[...], from_south_ref[...], from_west_ref[east, :], from_east_ref[west, :])
    known = (1.0, 1.0, as_f32(x > 0), as_f32(x < txs - 1))

    def side(k, slot):
        mine, theirs = own[k], halo[k]
        outgoing = k in (0, 3)
        speed = (mine if outgoing else theirs)[(vs if k < 2 else us) + slot:][:1]
        d_mine, d_theirs = mine[ds:ds + 1], theirs[ds:ds + 1]
        opened = mine[ws:ws + 1] * (theirs[ws:ws + 1] * known[k])
        flow = speed * (0.5 * (d_mine + d_theirs) * opened) / levels
        c_mine = mine[slot * count:(slot + 1) * count]
        c_theirs = theirs[slot * count:(slot + 1) * count]
        scale = advect_rate * levels / d_mine
        if outgoing:
            return -scale * (jnp.maximum(flow, 0.0) * c_mine + jnp.minimum(flow, 0.0) * c_theirs), flow
        return scale * (jnp.maximum(flow, 0.0) * c_theirs + jnp.minimum(flow, 0.0) * c_mine), -flow

    flows = [0.0, 0.0, 0.0, 0.0]
    for slot in range(2):
        ref = (x_fix_ref, m_fix_ref)[slot]
        for k in range(4):
            fix, flow = side(k, slot)
            flows[k] = flows[k] + flow
            if k < 2:
                ref[pl.ds(k * count, count), :] = fix
            else:
                ref[pl.ds(2 * count + 3 - k, count, stride=2), :] = fix
    lane, row = lanes_of((height, width)), rows_of((height, width))
    spill = jnp.concatenate([flows[3], flows[2], jnp.zeros((width - 2, height), f32)], 0).T
    spill = east_of(spill)
    spill = jnp.where((lane == 0) | (lane == width - 1), spill, 0.0)
    spill = spill + jnp.where(row == 0, flows[1], 0.0) + jnp.where(row == height - 1, flows[0], 0.0)
    packet_ref[pl.ds(0, height), :] = fields_ref[0] + fields_ref[1] + spill
    packet_ref[pl.ds(height, height), :] = fields_ref[2] + fields_ref[3]
    packet_ref[pl.ds(2 * height, 3 * count), :] = x_fix_ref[pl.ds(count, 3 * count), :]


def face_corrections(fields, north, south, sides, halos, levels, count):
    height, width = fields.shape[1:]
    return pl.pallas_call(
        partial(faces_kernel, levels=levels, count=count),
        in_specs=[VM] * 8,
        out_specs=[VM] * 3,
        out_shape=[kept((2 * height + 3 * count, width))] + [kept((4 * count, width))] * 2,
        compiler_params=small,
        name="faces",
    )(*near_core(fields, north, south, sides, *halos))


def turned_columns(rows):
    return jnp.concatenate([rows, jnp.zeros((rows.shape[1] - rows.shape[0], rows.shape[1]), f32)], 0).T


def mend_kernel(x_fix, m_fix, *rest, strip):
    ins, outs, turned_ref = rest[:5], rest[5:10], rest[10]
    height, width = turned_ref.shape[1:]
    count = ins[0].shape[0]
    for slot, fix in enumerate((x_fix, m_fix)):
        turned_ref[slot] = turned_columns(fix[pl.ds(2 * count, 2 * count), :])
        base = 0
        some = slice(2, 5) if slot else slice(0, 2)
        for source, target in zip(ins[some], outs[some]):
            for first, size in strips(source.shape[1], strip):
                here = pl.ds(first, size)
                lane, row = lanes_of((size, width)), rows_of((size, width))
                rim = (lane == 0) | (lane == width - 1)
                columns = turned_ref[slot, pl.ds(base + first, size), :]
                for t in range(count):
                    value = source[t, here, :]
                    value = value + jnp.where(rim, pltpu.roll(columns, width - 1 - 2 * t, 1), 0.0)
                    if base + first == 0:
                        value = value + jnp.where(row == 0, fix[pl.ds(count + t, 1), :], 0.0)
                    if base + first + size == height:
                        value = value + jnp.where(row == size - 1, fix[pl.ds(t, 1), :], 0.0)
                    target[t, here, :] = value
            base += source.shape[1]


def mend(x_fix, m_fix, *parts, strip=16):
    height = parts[0].shape[1] + parts[1].shape[1]
    return pl.pallas_call(
        partial(mend_kernel, strip=strip),
        in_specs=[VM] * 7,
        out_specs=[VM] * 5,
        out_shape=[kept(p.shape) for p in parts],
        input_output_aliases={2 + k: k for k in range(1, 5)},
        scratch_shapes=[pltpu.VMEM((2, height, x_fix.shape[1]), f32)],
        compiler_params=small,
        name="mend",
    )(*near_core(x_fix, m_fix, *parts))


def sum_kernel(a_ref, b_ref, out_ref):
    out_ref[...] = a_ref[pl.ds(0, out_ref.shape[0]), :] + b_ref[pl.ds(0, out_ref.shape[0]), :]


def pair_sum(packet, near, rows):
    return pl.pallas_call(
        sum_kernel, in_specs=[VM] * 2, out_specs=VM,
        out_shape=kept((rows, packet.shape[1])), compiler_params=small, name="pair",
    )(*near_core(packet, near))


def surface_kernel(
    packet_ref, near_ref, far_ref, fields_ref, surface_ref, depth_ref, wet_ref,
    surface_out, pressure_out, south_out, west_out, *, levels,
):
    g, _, at_level = places()
    height, width = surface_ref.shape
    top, below = pl.ds(0, height), pl.ds(height, height)
    near_above, far_above = as_f32(g % 2 == 1), as_f32(g >= 2)
    total = packet_ref[top, :] + near_ref[top, :] + far_ref[top, :]
    surface = surface_ref[...] - eta_rate * wet_ref[...].astype(f32) * total
    above = near_above * near_ref[below, :] + far_above * far_ref[below, :]
    surface_out[...] = surface
    lane = lanes_of((height, width))
    turned = jnp.where(lane == 0, surface, 0.0)
    south_out[...] = jnp.zeros_like(south_out)
    keep(south_out, pl.ds(0, 1), surface[:1])
    for slot in range(2):
        lower = as_f32(at_level[slot] == 1)
        density = fields_ref[2 + slot]
        column = above + lower * fields_ref[3 - slot] + density - 0.5 * density
        pressure = baroclinic_rate * depth_ref[...] * column / levels
        pressure_out[slot] = pressure
        keep(south_out, pl.ds(1 + slot, 1), pressure[:1])
        turned = jnp.where(lane == 1 + slot, pltpu.roll(pressure, 1 + slot, 1), turned)
    west_out[...] = turned.T[:SUB]


def new_surface_and_pressure(packet, near, far, fields, surface, depth, wet_mask, levels):
    height, width = surface.shape
    args = (packet, near, far, fields, surface, depth, wet_mask)
    outs = [(height, width), (2, height, width), (SUB, width), (SUB, height)]
    return pl.pallas_call(
        partial(surface_kernel, levels=levels),
        in_specs=[VM] * len(args), out_specs=[VM] * len(outs),
        out_shape=[kept(s) for s in outs],
        compiler_params=small,
        name="level",
    )(*near_core(*args))


def momentum_kernel(
    u_ref, v_ref, depth_ref, wet_ref, surface_ref, pressure_ref, from_north_ref,
    from_south_ref, from_west_ref, from_east_ref, north_state_ref, east_state_ref,
    east_out, north_out, *, count,
):
    g, groups, at_level = places()
    x, txs = lax.axis_index("tx"), lax.axis_size("tx")
    height, width = depth_ref.shape
    lane, row = lanes_of((height, width)), rows_of((height, width))
    us = 2 * count
    half_rows = from_west_ref.shape[0] // 2
    known_w, known_e = as_f32(x > 0), as_f32(x < txs - 1)
    west_halo = from_west_ref[pl.ds(0, half_rows, stride=2), :][us:us + SUB] * known_w
    east_halo = from_east_ref[pl.ds(1, half_rows, stride=2), :][us:us + SUB] * known_e
    used = 3 * SUB
    columns = jnp.concatenate(
        [west_halo, east_halo, east_state_ref[...], jnp.zeros((width - used, height), f32)], 0
    ).T
    north_halo, south_halo = from_north_ref[...], from_south_ref[...]

    def shifted(field, q, state=None):
        e_from = SUB + q if state is None else 2 * SUB + state
        e = jnp.where(lane == width - 1, pltpu.roll(columns, width - 1 - e_from, 1), east_of(field))
        line = north_halo[us + q:us + q + 1] if state is None else north_state_ref[pl.ds(state, 1), :]
        n = jnp.where(row == height - 1, line, north_of(field))
        return e, n

    def whole(field, q):
        e, n = shifted(field, q)
        w = jnp.where(lane == 0, pltpu.roll(columns, (width - q) % width, 1), west_of(field))
        s = jnp.where(row == 0, south_halo[us + q:us + q + 1], south_of(field))
        return n + s + e + w - 4.0 * field

    wet = wet_ref[...].astype(f32)
    wet_e, wet_n = shifted(wet, 5)
    open_e, open_n = wet * wet_e, wet * wet_n
    surface = surface_ref[...]
    surface_e, surface_n = shifted(surface, 0, 0)
    for slot in range(2):
        at = at_level[slot]
        bottom = as_f32((g == groups - 1) & (at == 1))
        pressure = pressure_ref[slot]
        pressure_e, pressure_n = shifted(pressure, 0, 1 + slot)
        u, v = u_ref[at], v_ref[at]
        east_out[at] = open_e * (
            u - gravity_rate * (surface_e - surface) - (pressure_e - pressure)
            + viscous_rate * whole(u, slot) - friction_rate * bottom * u
        )
        north_out[at] = open_n * (
            v - gravity_rate * (surface_n - surface) - (pressure_n - pressure)
            + viscous_rate * whole(v, 2 + slot) - friction_rate * bottom * v
        )


def momentum(u, v, depth, wet_mask, surface, pressure, halos, states, count):
    args = (u, v, depth, wet_mask, surface, pressure, *halos, *states)
    return pl.pallas_call(
        partial(momentum_kernel, count=count),
        in_specs=[VM] * len(args), out_specs=[VM] * 2,
        out_shape=[jax.ShapeDtypeStruct(u.shape, f32)] * 2,
        compiler_params=small,
        name="momentum",
    )(*near_core(*args))


def rates_kernel(cells_ref, loads_ref, kinetics_ref, wet_ref, out_ref, source_ref):
    g, _, _ = places()
    count, _, width = source_ref.shape
    size = count * SUB
    spread = (
        lax.broadcasted_iota(jnp.int32, (size, count), 0) // SUB
        == lax.broadcasted_iota(jnp.int32, (size, count), 1)
    ).astype(f32)
    full = jnp.dot(spread, kinetics_ref[...], precision=lax.Precision.HIGHEST)
    full = lax.dot_general(
        full, spread, (((1,), (1,)), ((), ())), precision=lax.Precision.HIGHEST
    )
    same = lax.broadcasted_iota(jnp.int32, (size, size), 0) % SUB
    same = same == lax.broadcasted_iota(jnp.int32, (size, size), 1) % SUB
    high, low = split(jnp.where(same, full, 0.0))
    out_ref[...] = jnp.concatenate([high, high, low], 1)
    source_ref[...] = jnp.zeros_like(source_ref)

    @pl.when(g == 0)
    def _():
        @pl.loop(0, cells_ref.shape[0])
        def _(r):
            at, spot = pl.ds(cells_ref[r] // width, 1), cells_ref[r] % width
            here = (lanes_of((1, width)) == spot) & (wet_ref[at, :] != 0)
            for t in range(count):
                source_ref[t, at, :] = source_ref[t, at, :] + jnp.where(here, loads_ref[r, t], 0.0)


def rates_and_source(cells, loads, kinetics, wet_mask):
    count = kinetics.shape[0]
    size = count * SUB
    return pl.pallas_call(
        rates_kernel, in_specs=[SM, SM, VM, VM], out_specs=[VM, VM],
        out_shape=[pltpu.VMEM((size, 3 * size), jnp.bfloat16), kept((count,) + wet_mask.shape)],
        compiler_params=small, name="rates",
    )(cells, loads, kinetics, *near_core(wet_mask))


def split(x):
    high = x.astype(jnp.bfloat16)
    return high, (x - high.astype(f32)).astype(jnp.bfloat16)


def react_kernel(
    c_ref, wet_ref, rates_ref, extra_ref, *rest, slot, fixed, sizes, strip,
):
    out_hbm, done_ref, turned_ref, out_sem = rest[-4:]
    parts = [rest[sum(sizes[:k]):sum(sizes[:k + 1])] for k in range(3)]
    g, groups, at_level = places()
    count, height, width = done_ref.shape
    has_next = 1.0 if slot == 0 else as_f32((g > 0) & (g < groups - 1))
    keep_rate = 1.0 - mixing_rate - mixing_rate * has_next
    next_rate = mixing_rate * has_next
    early = parts[0][0].shape[1] if slot == 0 else 0
    if early:
        turned_ref[...] = next_rate * turned_columns(extra_ref[pl.ds(fixed + count, 2 * count), :])
    rates = rates_ref[...]
    copies = []
    for first, size in strips(height, strip, *(rows_in(refs) for refs in parts)):
        here = pl.ds(first, size)
        groups_of = size // SUB
        lane, row = lanes_of((size, width)), rows_of((size, width))
        rim = (lane == 0) | (lane == width - 1)
        sources = [pick(refs, first) for refs in parts]
        wet = wet_ref[here, :] != 0
        values = []
        for t in range(count):
            own, other, beyond = (ref[t, pl.ds(at, size), :] for ref, at in sources)
            value = keep_rate * own + mixing_rate * other + next_rate * beyond
            if first < early:
                columns = turned_ref[here, :]
                value = value + jnp.where(rim, pltpu.roll(columns, width - 1 - 2 * t, 1), 0.0)
                if first == 0:
                    line = next_rate * extra_ref[pl.ds(fixed + t, 1), :]
                    value = value + jnp.where(row == 0, line, 0.0)
            values.append(jnp.where(wet, value, c_ref[slot, t, here, :]))
        stacked = jnp.concatenate(
            [
                jnp.concatenate([v[k * SUB:(k + 1) * SUB] for v in values], 0)
                for k in range(groups_of)
            ],
            1,
        )
        high, low = split(stacked)
        reaction = jnp.dot(
            rates, jnp.concatenate([high, low, high], 0), preferred_element_type=f32
        )
        warming = jnp.where(wet, jnp.exp(warming_rate * values[1]), 0.0)
        for t in range(count):
            gained = jnp.concatenate(
                [reaction[t * SUB:(t + 1) * SUB, k * width:(k + 1) * width] for k in range(groups_of)],
                0,
            )
            done = values[t] + warming * gained
            done_ref[t, here, :] = done if slot == 0 else done + extra_ref[t, here, :]
        copies.append(pltpu.make_async_copy(
            done_ref.at[:, here], out_hbm.at[:, at_level[slot], here], out_sem.at[len(copies)]
        ))
        copies[-1].start()
    for copy in copies:
        copy.wait()


def react(shape, c, wet_mask, rates, slot, own, other, received, extra, into=None, strip=16):
    count, _, height, width = shape
    args = near_core(c, wet_mask, rates, extra, *own, *other, *received)
    specs = [VM] * len(args)
    aliases = {}
    if into is not None:
        aliases = {len(args): 0}
        args.append(into)
        specs.append(HB)
    return pl.pallas_call(
        partial(react_kernel, slot=slot, strip=strip, fixed=2 * height,
                sizes=(len(own), len(other), len(received))),
        in_specs=specs,
        out_specs=HB,
        scratch_shapes=[
            pltpu.VMEM((count, height, width), f32), pltpu.VMEM((height, width), f32),
            pltpu.SemaphoreType.DMA((height // SUB,)),
        ],
        out_shape=jax.ShapeDtypeStruct(shape, f32),
        input_output_aliases=aliases,
        compiler_params=small,
        name="react",
    )(*args)


def shards(tracers, u, v, surface, depth, wet_mask, river_cells, river_loads, kinetics):
    count, own_levels, height, _ = tracers.shape
    groups, tys, txs = (lax.axis_size(a) for a in ("grp", "ty", "tx"))
    levels = own_levels * groups
    assert own_levels == 2 and groups in (2, 4)
    sent = 5 * height // 8
    cut = [SUB * (height // SUB * k // 16) for k in (9, 4)]
    cut.append(height - sum(cut))
    cell_args = (tracers, u, v, depth, wet_mask, levels)

    swap = [(i, i ^ 1) for i in range(groups)]
    middle = [(i, i + 1) for i in range(1, groups - 1, 2)]
    middle = middle + [(b, a) for a, b in middle]
    early = early_advection(*cell_args, sent)
    near_x_lo = lax.ppermute(early, "grp", swap)
    c, x_hi, *m, fields, north, south, sides = closed_advection(*cell_args, sent, cut)

    up = [(i, i + 1) for i in range(tys - 1)]
    down = [(i + 1, i) for i in range(tys - 1)]
    from_south = lax.ppermute(north, "ty", up)
    from_north = lax.ppermute(south, "ty", down)
    if txs == 2:
        from_west = from_east = lax.ppermute(sides, "tx", [(0, 1), (1, 0)])
    else:
        from_west = lax.ppermute(sides, "tx", [(i, i + 1) for i in range(txs - 1)])
        from_east = lax.ppermute(sides, "tx", [(i + 1, i) for i in range(txs - 1)])
    halos = (from_north, from_south, from_west, from_east)
    packet, x_fix, m_fix = face_corrections(fields, north, south, sides, halos, levels, count)
    near = lax.ppermute(packet, "grp", swap)
    x_lo, x_hi, *m = mend(x_fix, m_fix, early, x_hi, *m)
    near_x_hi = lax.ppermute(x_hi, "grp", swap)
    near_m = [lax.ppermute(m[0], "grp", middle)]
    for k in (1, 2):
        if groups == 4:
            handed = lax.ppermute(m[k], "grp", [(1, 3), (2, 0)])
            near_m.append(lax.ppermute(handed, "grp", [(3, 2), (0, 1)]))
        else:
            near_m.append(lax.ppermute(m[k], "grp", middle))

    columns = pair_sum(packet, near, 2 * height)
    if groups == 4:
        far = lax.ppermute(columns, "grp", [(i, i ^ 2) for i in range(groups)])
    else:
        far = jnp.zeros_like(columns)
    new_surface, pressure, south_state, west_state = new_surface_and_pressure(
        packet, near, far, fields, surface, depth, wet_mask, levels
    )
    north_state = lax.ppermute(south_state, "ty", down)
    east_state = lax.ppermute(west_state, "tx", [(i + 1, i) for i in range(txs - 1)])
    new_east, new_north = momentum(
        u, v, depth, wet_mask, new_surface, pressure, halos, (north_state, east_state), count
    )

    rates, source = rates_and_source(river_cells, river_loads, kinetics, wet_mask)
    step = partial(react, tracers.shape, c, wet_mask, rates)
    x = (x_lo, x_hi)
    out = step(0, x, m, (near_x_lo, near_x_hi), near)
    out = step(1, m, x, near_m, source, into=out)
    return (out, new_east, new_north, new_surface)


def solution(mesh):
    field = P("grp", "ty", "tx")
    plane = P("ty", "tx")
    return jax.shard_map(
        shards,
        mesh=mesh,
        in_specs=(
            P(None, "grp", "ty", "tx"), field, field, plane, plane, plane,
            P(("ty", "tx")), P(("ty", "tx"), None), P(),
        ),
        out_specs=(P(None, "grp", "ty", "tx"), field, field, plane),
        check_vma=False,
    )
```

```python
from functools import partial

import jax
import jax.numpy as jnp
from jax import lax
from jax.experimental import pallas as pl
from jax.experimental.pallas import tpu as pltpu
from jax.sharding import PartitionSpec as P


eta_rate = 0.25
gravity_rate = 0.25
baroclinic_rate = 0.4
viscous_rate = 0.1
friction_rate = 0.3
advect_rate = 0.3
mixing_rate = 0.2
haline_coef = 0.8
thermal_coef = 0.2
warming_rate = 0.46

f32 = jnp.float32
SUB = 8


def lanes_of(shape):
    return lax.broadcasted_iota(jnp.int32, shape, len(shape) - 1)


def rows_of(shape):
    return lax.broadcasted_iota(jnp.int32, shape, len(shape) - 2)


def east_of(x):
    return pltpu.roll(x, x.shape[-1] - 1, x.ndim - 1)


def west_of(x):
    return pltpu.roll(x, 1, x.ndim - 1)


def north_of(x):
    return pltpu.roll(x, x.shape[-2] - 1, x.ndim - 2)


def south_of(x):
    return pltpu.roll(x, 1, x.ndim - 2)


def keep(ref, rows, value):
    ref[rows, :] = value


VM = pl.BlockSpec(memory_space=pltpu.VMEM)


small = pltpu.CompilerParams(vmem_limit_bytes=16 << 20)


def near_core(*arrays):
    return [pltpu.with_memory_space_constraint(a, pltpu.VMEM) for a in arrays]


def far_core(*arrays):
    return [pltpu.with_memory_space_constraint(a, pltpu.HBM) for a in arrays]


def kept(shape):
    return pltpu.VMEM(shape, f32)


SM = pl.BlockSpec(memory_space=pltpu.SMEM)
HB = pl.BlockSpec(memory_space=pl.ANY)


def places():
    g, groups = lax.axis_index("grp"), lax.axis_size("grp")
    return g, groups, (1 - g % 2, g % 2)


def as_f32(flag):
    return jnp.where(flag, 1.0, 0.0).astype(f32)


def pick(refs, row):
    for ref in refs:
        if row < ref.shape[1]:
            return ref, row
        row -= ref.shape[1]


def strips(height, strip, *parts):
    ends = {height}
    for part in parts:
        ends |= {sum(part[:k + 1]) for k in range(len(part))}
    first = 0
    while first < height:
        size = min(strip, min(e for e in ends if e > first) - first)
        yield first, size
        first += size


def rows_in(parts):
    return [p.shape[1] for p in parts]


def weights(coef_ref, u, v, depth, wet, levels):
    height, width = depth.shape
    lane, row = lanes_of((height, width)), rows_of((height, width))
    half_e = 0.5 * (depth + east_of(depth)) * (wet * east_of(wet))
    half_n = 0.5 * (depth + north_of(depth)) * (wet * north_of(wet))
    flow_e = jnp.where(lane < width - 1, u * half_e / levels, 0.0)
    flow_n = jnp.where(row < height - 1, v * half_n / levels, 0.0)
    flow_w, flow_s = west_of(flow_e), south_of(flow_n)
    scale = advect_rate * levels / depth
    coef_ref[0] = 1.0 - scale * (
        jnp.maximum(flow_e, 0.0) - jnp.minimum(flow_w, 0.0)
        + jnp.maximum(flow_n, 0.0) - jnp.minimum(flow_s, 0.0)
    )
    coef_ref[1] = -scale * jnp.minimum(flow_e, 0.0)
    coef_ref[2] = scale * jnp.maximum(flow_w, 0.0)
    coef_ref[3] = -scale * jnp.minimum(flow_n, 0.0)
    coef_ref[4] = scale * jnp.maximum(flow_s, 0.0)
    return flow_e - flow_w + flow_n - flow_s


def weighed(coefs, c, above, under):
    return (
        coefs[0] * c + coefs[1] * east_of(c) + coefs[2] * west_of(c)
        + coefs[3] * above + coefs[4] * under
    )


def early_kernel(
    c_hbm, u_hbm, v_hbm, depth_hbm, wet_hbm, out_ref,
    c_ref, u_ref, v_ref, depth_ref, wet_ref, coef_ref, flat_sem, c_sem, *, levels, strip,
):
    _, _, at_level = places()
    count, taken, _ = c_ref.shape
    at, rows = at_level[0], pl.ds(0, taken)
    flat = [
        pltpu.make_async_copy(h, r, flat_sem.at[k])
        for k, (h, r) in enumerate((
            (depth_hbm.at[rows], depth_ref), (wet_hbm.at[rows], wet_ref),
            (u_hbm.at[at, rows], u_ref), (v_hbm.at[at, rows], v_ref),
        ))
    ]
    bulk = pltpu.make_async_copy(c_hbm.at[:, at, rows], c_ref, c_sem)
    for copy in flat:
        copy.start()
    bulk.start()
    for copy in flat:
        copy.wait()
    weights(coef_ref, u_ref[...], v_ref[...], depth_ref[...], wet_ref[...].astype(f32), levels)
    bulk.wait()
    for first in range(0, out_ref.shape[1], strip):
        here = pl.ds(first, strip)
        coefs = [coef_ref[k, here, :] for k in range(5)]
        for t in range(count):
            c = c_ref[t, here, :]
            above = c_ref[t, pl.ds(first + 1, strip), :]
            under = c_ref[t, pl.ds(first - 1, strip), :] if first else south_of(c)
            out_ref[t, here, :] = weighed(coefs, c, above, under)


def early_advection(tracers, u, v, depth, wet_mask, levels, rows, strip=16):
    count, _, _, width = tracers.shape
    taken = rows + SUB
    plane = pltpu.VMEM((taken, width), f32)
    return pl.pallas_call(
        partial(early_kernel, levels=levels, strip=strip),
        in_specs=[HB] * 5,
        out_specs=VM,
        out_shape=kept((count, rows, width)),
        scratch_shapes=[
            pltpu.VMEM((count, taken, width), f32), plane, plane, plane,
            pltpu.VMEM((taken, width), jnp.int32), pltpu.VMEM((5, taken, width), f32),
            pltpu.SemaphoreType.DMA((4,)), pltpu.SemaphoreType.DMA,
        ],
        compiler_params=small,
        name="early",
    )(*far_core(tracers, u, v, depth, wet_mask))


def closed_kernel(
    c_hbm, u_hbm, v_hbm, depth_hbm, wet_hbm,
    c_ref, x_hi, m_lo, m_hi, fields_ref, north_ref, south_ref, sides_ref,
    u_ref, v_ref, depth_ref, wet_ref, coef_ref, turned_ref, flat_sem, c_sem,
    *, levels, count, parts, strip,
):
    _, _, at_level = places()
    height, width = depth_ref.shape
    sent = height - x_hi.shape[1]
    chunk = count // parts
    flat = [
        pltpu.make_async_copy(h, r, flat_sem.at[k])
        for k, (h, r) in enumerate(
            ((depth_hbm, depth_ref), (wet_hbm, wet_ref), (u_hbm, u_ref), (v_hbm, v_ref))
        )
    ]
    for copy in flat:
        copy.start()
    bulk = []
    for slot in range(2):
        for part in range(parts):
            some = pl.ds(part * chunk, chunk)
            bulk.append(pltpu.make_async_copy(
                c_hbm.at[some, at_level[slot]], c_ref.at[slot, some], c_sem.at[slot, part]
            ))
            bulk[-1].start()
    north_ref[...] = jnp.zeros_like(north_ref)
    south_ref[...] = jnp.zeros_like(south_ref)
    for copy in flat:
        copy.wait()
    depth, wet = depth_ref[...], wet_ref[...].astype(f32)

    def lines(field, q):
        keep(north_ref, pl.ds(q, 1), field[height - 1:])
        keep(south_ref, pl.ds(q, 1), field[:1])

    def gather(got, field, q):
        mask = lanes_of((1, width)) // 2 == q
        return jnp.where(mask, pltpu.roll(field, (2 * q + 1) % width, 1), got)

    turned = jnp.zeros((height, width), f32)
    for q, field in ((4, depth), (5, wet)):
        lines(field, 2 * count + q)
        turned = gather(turned, field, 2 * count + q)
    for slot in range(2):
        u, v = u_ref[at_level[slot]], v_ref[at_level[slot]]
        lines(u, 2 * count + slot)
        lines(v, 2 * count + 2 + slot)
        turned = gather(turned, u, 2 * count + slot)
        turned = gather(turned, v, 2 * count + 2 + slot)
        fields_ref[slot] = weights(coef_ref.at[slot], u, v, depth, wet, levels)
    turned_ref[...] = turned

    for slot in range(2):
        for part in range(parts):
            bulk[slot * parts + part].wait()
            if part == 0:
                fields_ref[2 + slot] = haline_coef * c_ref[slot, 0] - thermal_coef * c_ref[slot, 1]
            cut = (rows_in((m_lo, m_hi)), [sent])[1 - slot]
            for first, size in strips(height, strip, cut):
                here = pl.ds(first, size)
                coefs = [coef_ref[slot, k, here, :] for k in range(5)]
                got = turned_ref[here, :]
                for t in range(part * chunk, (part + 1) * chunk):
                    q = slot * count + t
                    c = c_ref[slot, t, here, :]
                    got = gather(got, c, q)
                    if first == 0:
                        keep(south_ref, pl.ds(q, 1), c[:1])
                    if first + size == height:
                        keep(north_ref, pl.ds(q, 1), c[size - 1:])
                    if slot == 0 and first < sent:
                        continue
                    if first + size < height:
                        above = c_ref[slot, t, pl.ds(first + 1, size), :]
                    else:
                        above = north_of(c)
                    under = c_ref[slot, t, pl.ds(first - 1, size), :] if first else south_of(c)
                    moved = weighed(coefs, c, above, under)
                    if slot == 0:
                        x_hi[t, pl.ds(first - sent, size), :] = moved
                    else:
                        to, at = pick((m_lo, m_hi), first)
                        to[t, pl.ds(at, size), :] = moved
                turned_ref[here, :] = got
    sides_ref[...] = turned_ref[...].T[: sides_ref.shape[0]]


def closed_advection(tracers, u, v, depth, wet_mask, levels, sent, cut, parts=2, strip=16):
    count, _, height, width = tracers.shape
    edge_rows = -(-(2 * count + 6) // SUB) * SUB
    assert width == height and 2 * edge_rows <= width
    outs = [
        kept((2, count, height, width)), kept((count, height - sent, width)),
        *(kept((count, rows, width)) for rows in cut), kept((4, height, width)),
        kept((edge_rows, width)), kept((edge_rows, width)), kept((2 * edge_rows, height)),
    ]
    plane = pltpu.VMEM((height, width), f32)
    return pl.pallas_call(
        partial(closed_kernel, levels=levels, count=count, parts=parts, strip=strip),
        in_specs=[HB] * 5,
        out_specs=[VM] * len(outs),
        out_shape=outs,
        scratch_shapes=[
            pltpu.VMEM(u.shape, f32), pltpu.VMEM(v.shape, f32), plane,
            pltpu.VMEM((height, width), jnp.int32), pltpu.VMEM((2, 5, height, width), f32), plane,
            pltpu.SemaphoreType.DMA((4,)), pltpu.SemaphoreType.DMA((2, parts)),
        ],
        compiler_params=small,
        name="closed",
    )(*far_core(tracers, u, v, depth, wet_mask))


def faces_kernel(
    fields_ref, north_ref, south_ref, sides_ref, from_north_ref, from_south_ref,
    from_west_ref, from_east_ref, packet_ref, x_fix_ref, m_fix_ref, *, levels, count,
):
    height, width = fields_ref.shape[1:]
    x, txs = lax.axis_index("tx"), lax.axis_size("tx")
    half_rows = sides_ref.shape[0] // 2
    us, vs, ds, ws = 2 * count, 2 * count + 2, 2 * count + 4, 2 * count + 5
    east, west = (pl.ds(0, half_rows, stride=2), pl.ds(1, half_rows, stride=2))
    own = (north_ref[...], south_ref[...], sides_ref[west, :], sides_ref[east, :])
    halo = (from_north_ref[...], from_south_ref[...], from_west_ref[east, :], from_east_ref[west, :])
    known = (1.0, 1.0, as_f32(x > 0), as_f32(x < txs - 1))

    def side(k, slot):
        mine, theirs = own[k], halo[k]
        outgoing = k in (0, 3)
        speed = (mine if outgoing else theirs)[(vs if k < 2 else us) + slot:][:1]
        d_mine, d_theirs = mine[ds:ds + 1], theirs[ds:ds + 1]
        opened = mine[ws:ws + 1] * (theirs[ws:ws + 1] * known[k])
        flow = speed * (0.5 * (d_mine + d_theirs) * opened) / levels
        c_mine = mine[slot * count:(slot + 1) * count]
        c_theirs = theirs[slot * count:(slot + 1) * count]
        scale = advect_rate * levels / d_mine
        if outgoing:
            return -scale * (jnp.maximum(flow, 0.0) * c_mine + jnp.minimum(flow, 0.0) * c_theirs), flow
        return scale * (jnp.maximum(flow, 0.0) * c_theirs + jnp.minimum(flow, 0.0) * c_mine), -flow

    flows = [0.0, 0.0, 0.0, 0.0]
    for slot in range(2):
        ref = (x_fix_ref, m_fix_ref)[slot]
        for k in range(4):
            fix, flow = side(k, slot)
            flows[k] = flows[k] + flow
            if k < 2:
                ref[pl.ds(k * count, count), :] = fix
            else:
                ref[pl.ds(2 * count + 3 - k, count, stride=2), :] = fix
    lane, row = lanes_of((height, width)), rows_of((height, width))
    spill = jnp.concatenate([flows[3], flows[2], jnp.zeros((width - 2, height), f32)], 0).T
    spill = east_of(spill)
    spill = jnp.where((lane == 0) | (lane == width - 1), spill, 0.0)
    spill = spill + jnp.where(row == 0, flows[1], 0.0) + jnp.where(row == height - 1, flows[0], 0.0)
    packet_ref[pl.ds(0, height), :] = fields_ref[0] + fields_ref[1] + spill
    packet_ref[pl.ds(height, height), :] = fields_ref[2] + fields_ref[3]
    packet_ref[pl.ds(2 * height, 3 * count), :] = x_fix_ref[pl.ds(count, 3 * count), :]
    packet_ref[pl.ds(2 * height + 3 * count, count), :] = m_fix_ref[pl.ds(0, count), :]
    packet_ref[pl.ds(2 * height + 4 * count, 2 * count), :] = m_fix_ref[pl.ds(2 * count, 2 * count), :]


def face_corrections(fields, north, south, sides, halos, levels, count):
    height, width = fields.shape[1:]
    return pl.pallas_call(
        partial(faces_kernel, levels=levels, count=count),
        in_specs=[VM] * 8,
        out_specs=[VM] * 3,
        out_shape=[kept((2 * height + 6 * count, width))] + [kept((4 * count, width))] * 2,
        compiler_params=small,
        name="faces",
    )(*near_core(fields, north, south, sides, *halos))


def turned_columns(rows):
    return jnp.concatenate([rows, jnp.zeros((rows.shape[1] - rows.shape[0], rows.shape[1]), f32)], 0).T


def mend_kernel(x_fix, m_fix, *rest, strip):
    ins, outs, turned_ref = rest[:4], rest[4:8], rest[8]
    height, width = turned_ref.shape[1:]
    count = ins[0].shape[0]
    for slot, fix in enumerate((x_fix, m_fix)):
        turned_ref[slot] = turned_columns(fix[pl.ds(2 * count, 2 * count), :])
        base = 0
        some = slice(2 * slot, 2 * slot + 2)
        for source, target in zip(ins[some], outs[some]):
            for first, size in strips(source.shape[1], strip):
                here = pl.ds(first, size)
                lane, row = lanes_of((size, width)), rows_of((size, width))
                rim = (lane == 0) | (lane == width - 1)
                columns = turned_ref[slot, pl.ds(base + first, size), :]
                for t in range(count):
                    value = source[t, here, :]
                    value = value + jnp.where(rim, pltpu.roll(columns, width - 1 - 2 * t, 1), 0.0)
                    if base + first == 0:
                        value = value + jnp.where(row == 0, fix[pl.ds(count + t, 1), :], 0.0)
                    if base + first + size == height:
                        value = value + jnp.where(row == size - 1, fix[pl.ds(t, 1), :], 0.0)
                    target[t, here, :] = value
            base += source.shape[1]


def mend(x_fix, m_fix, *parts, strip=16):
    height = parts[0].shape[1] + parts[1].shape[1]
    return pl.pallas_call(
        partial(mend_kernel, strip=strip),
        in_specs=[VM] * 6,
        out_specs=[VM] * 4,
        out_shape=[kept(p.shape) for p in parts],
        input_output_aliases={3: 1, 4: 2},
        scratch_shapes=[pltpu.VMEM((2, height, x_fix.shape[1]), f32)],
        compiler_params=small,
        name="mend",
    )(*near_core(x_fix, m_fix, *parts))


def pair_kernel(a_ref, b_ref, out_ref, *, rows):
    more = out_ref.shape[0] - rows
    out_ref[pl.ds(0, rows), :] = a_ref[pl.ds(0, rows), :] + b_ref[pl.ds(0, rows), :]
    out_ref[pl.ds(rows, more), :] = b_ref[pl.ds(b_ref.shape[0] - more, more), :]


def pair_sum(packet, near, rows, count):
    return pl.pallas_call(
        partial(pair_kernel, rows=rows), in_specs=[VM] * 2, out_specs=VM,
        out_shape=kept((rows + 3 * count, packet.shape[1])), compiler_params=small, name="pair",
    )(*near_core(packet, near))


def surface_kernel(
    packet_ref, near_ref, far_ref, fields_ref, surface_ref, depth_ref, wet_ref,
    surface_out, pressure_out, south_out, west_out, *, levels,
):
    g, _, at_level = places()
    height, width = surface_ref.shape
    top, below = pl.ds(0, height), pl.ds(height, height)
    near_above, far_above = as_f32(g % 2 == 1), as_f32(g >= 2)
    total = packet_ref[top, :] + near_ref[top, :] + far_ref[top, :]
    surface = surface_ref[...] - eta_rate * wet_ref[...].astype(f32) * total
    above = near_above * near_ref[below, :] + far_above * far_ref[below, :]
    surface_out[...] = surface
    lane = lanes_of((height, width))
    turned = jnp.where(lane == 0, surface, 0.0)
    south_out[...] = jnp.zeros_like(south_out)
    keep(south_out, pl.ds(0, 1), surface[:1])
    for slot in range(2):
        lower = as_f32(at_level[slot] == 1)
        density = fields_ref[2 + slot]
        column = above + lower * fields_ref[3 - slot] + density - 0.5 * density
        pressure = baroclinic_rate * depth_ref[...] * column / levels
        pressure_out[slot] = pressure
        keep(south_out, pl.ds(1 + slot, 1), pressure[:1])
        turned = jnp.where(lane == 1 + slot, pltpu.roll(pressure, 1 + slot, 1), turned)
    west_out[...] = turned.T[:SUB]


def new_surface_and_pressure(packet, near, far, fields, surface, depth, wet_mask, levels):
    height, width = surface.shape
    args = (packet, near, far, fields, surface, depth, wet_mask)
    outs = [(height, width), (2, height, width), (SUB, width), (SUB, height)]
    return pl.pallas_call(
        partial(surface_kernel, levels=levels),
        in_specs=[VM] * len(args), out_specs=[VM] * len(outs),
        out_shape=[kept(s) for s in outs],
        compiler_params=small,
        name="level",
    )(*near_core(*args))


def momentum_kernel(
    u_ref, v_ref, depth_ref, wet_ref, surface_ref, pressure_ref, from_north_ref,
    from_south_ref, from_west_ref, from_east_ref, north_state_ref, east_state_ref,
    east_out, north_out, surface_out, *, count,
):
    g, groups, at_level = places()
    x, txs = lax.axis_index("tx"), lax.axis_size("tx")
    height, width = depth_ref.shape
    lane, row = lanes_of((height, width)), rows_of((height, width))
    us = 2 * count
    half_rows = from_west_ref.shape[0] // 2
    known_w, known_e = as_f32(x > 0), as_f32(x < txs - 1)
    west_halo = from_west_ref[pl.ds(0, half_rows, stride=2), :][us:us + SUB] * known_w
    east_halo = from_east_ref[pl.ds(1, half_rows, stride=2), :][us:us + SUB] * known_e
    used = 3 * SUB
    columns = jnp.concatenate(
        [west_halo, east_halo, east_state_ref[...], jnp.zeros((width - used, height), f32)], 0
    ).T
    north_halo, south_halo = from_north_ref[...], from_south_ref[...]

    def shifted(field, q, state=None):
        e_from = SUB + q if state is None else 2 * SUB + state
        e = jnp.where(lane == width - 1, pltpu.roll(columns, width - 1 - e_from, 1), east_of(field))
        line = north_halo[us + q:us + q + 1] if state is None else north_state_ref[pl.ds(state, 1), :]
        n = jnp.where(row == height - 1, line, north_of(field))
        return e, n

    def whole(field, q):
        e, n = shifted(field, q)
        w = jnp.where(lane == 0, pltpu.roll(columns, (width - q) % width, 1), west_of(field))
        s = jnp.where(row == 0, south_halo[us + q:us + q + 1], south_of(field))
        return n + s + e + w - 4.0 * field

    wet = wet_ref[...].astype(f32)
    wet_e, wet_n = shifted(wet, 5)
    open_e, open_n = wet * wet_e, wet * wet_n
    surface = surface_ref[...]
    surface_out[...] = surface
    surface_e, surface_n = shifted(surface, 0, 0)
    for slot in range(2):
        at = at_level[slot]
        bottom = as_f32((g == groups - 1) & (at == 1))
        pressure = pressure_ref[slot]
        pressure_e, pressure_n = shifted(pressure, 0, 1 + slot)
        u, v = u_ref[at], v_ref[at]
        east_out[at] = open_e * (
            u - gravity_rate * (surface_e - surface) - (pressure_e - pressure)
            + viscous_rate * whole(u, slot) - friction_rate * bottom * u
        )
        north_out[at] = open_n * (
            v - gravity_rate * (surface_n - surface) - (pressure_n - pressure)
            + viscous_rate * whole(v, 2 + slot) - friction_rate * bottom * v
        )


def momentum(u, v, depth, wet_mask, surface, pressure, halos, states, count):
    args = (u, v, depth, wet_mask, surface, pressure, *halos, *states)
    return pl.pallas_call(
        partial(momentum_kernel, count=count),
        in_specs=[VM] * len(args), out_specs=[VM] * 3,
        out_shape=[jax.ShapeDtypeStruct(a.shape, f32) for a in (u, v, surface)],
        compiler_params=small,
        name="momentum",
    )(*near_core(*args))


def rates_kernel(cells_ref, loads_ref, kinetics_ref, wet_ref, out_ref, source_ref):
    g, _, _ = places()
    count, _, width = source_ref.shape
    size = count * SUB
    spread = (
        lax.broadcasted_iota(jnp.int32, (size, count), 0) // SUB
        == lax.broadcasted_iota(jnp.int32, (size, count), 1)
    ).astype(f32)
    full = jnp.dot(spread, kinetics_ref[...], precision=lax.Precision.HIGHEST)
    full = lax.dot_general(
        full, spread, (((1,), (1,)), ((), ())), precision=lax.Precision.HIGHEST
    )
    same = lax.broadcasted_iota(jnp.int32, (size, size), 0) % SUB
    same = same == lax.broadcasted_iota(jnp.int32, (size, size), 1) % SUB
    high, low = split(jnp.where(same, full, 0.0))
    out_ref[...] = jnp.concatenate([high, high, low], 1)
    source_ref[...] = jnp.zeros_like(source_ref)

    @pl.when(g == 0)
    def _():
        @pl.loop(0, cells_ref.shape[0])
        def _(r):
            at, spot = pl.ds(cells_ref[r] // width, 1), cells_ref[r] % width
            here = (lanes_of((1, width)) == spot) & (wet_ref[at, :] != 0)
            for t in range(count):
                source_ref[t, at, :] = source_ref[t, at, :] + jnp.where(here, loads_ref[r, t], 0.0)


def rates_and_source(cells, loads, kinetics, wet_mask):
    count = kinetics.shape[0]
    size = count * SUB
    return pl.pallas_call(
        rates_kernel, in_specs=[SM, SM, VM, VM], out_specs=[VM, VM],
        out_shape=[pltpu.VMEM((size, 3 * size), jnp.bfloat16), kept((count,) + wet_mask.shape)],
        compiler_params=small, name="rates",
    )(cells, loads, kinetics, *near_core(wet_mask))


def split(x):
    high = x.astype(jnp.bfloat16)
    return high, (x - high.astype(f32)).astype(jnp.bfloat16)


def react_kernel(
    c_ref, wet_ref, rates_ref, fix_ref, *rest, slot, fixed, sizes, strip,
):
    out_hbm, done_ref, turned_ref, out_sem = rest[-4:]
    parts = [rest[sum(sizes[:k]):sum(sizes[:k + 1])] for k in range(3)]
    source_ref = rest[sum(sizes)]
    g, groups, at_level = places()
    count, height, width = done_ref.shape
    has_next = 1.0 if slot == 0 else as_f32((g > 0) & (g < groups - 1))
    keep_rate = 1.0 - mixing_rate - mixing_rate * has_next
    next_rate = mixing_rate * has_next
    border = parts[2][0].shape[1]
    turned_ref[...] = next_rate * turned_columns(fix_ref[pl.ds(fixed + count, 2 * count), :])
    rates = rates_ref[...]
    copies = []
    for first, size in strips(height, strip, *(rows_in(refs) for refs in parts)):
        here = pl.ds(first, size)
        groups_of = size // SUB
        lane, row = lanes_of((size, width)), rows_of((size, width))
        rim = (lane == 0) | (lane == width - 1)
        sources = [pick(refs, first) for refs in parts]
        wet = wet_ref[here, :] != 0
        values = []
        for t in range(count):
            own, other, beyond = (ref[t, pl.ds(at, size), :] for ref, at in sources)
            value = keep_rate * own + mixing_rate * other + next_rate * beyond
            if (first < border) == (slot == 0):
                columns = turned_ref[here, :]
                value = value + jnp.where(rim, pltpu.roll(columns, width - 1 - 2 * t, 1), 0.0)
                if first in (0, height - size):
                    line = next_rate * fix_ref[pl.ds(fixed + t, 1), :]
                    value = value + jnp.where(row == (size - 1 if first else 0), line, 0.0)
            values.append(jnp.where(wet, value, c_ref[slot, t, here, :]))
        stacked = jnp.concatenate(
            [
                jnp.concatenate([v[k * SUB:(k + 1) * SUB] for v in values], 0)
                for k in range(groups_of)
            ],
            1,
        )
        high, low = split(stacked)
        reaction = jnp.dot(
            rates, jnp.concatenate([high, low, high], 0), preferred_element_type=f32
        )
        warming = jnp.where(wet, jnp.exp(warming_rate * values[1]), 0.0)
        for t in range(count):
            gained = jnp.concatenate(
                [reaction[t * SUB:(t + 1) * SUB, k * width:(k + 1) * width] for k in range(groups_of)],
                0,
            )
            done = values[t] + warming * gained
            done_ref[t, here, :] = done if slot == 0 else done + source_ref[t, here, :]
        copies.append(pltpu.make_async_copy(
            done_ref.at[:, here], out_hbm.at[:, at_level[slot], here], out_sem.at[len(copies)]
        ))
        copies[-1].start()
    for copy in copies:
        copy.wait()


def react(shape, c, wet_mask, rates, slot, own, other, received, fix, source=None, into=None,
          strip=16):
    count, _, height, width = shape
    args = near_core(c, wet_mask, rates, fix, *own, *other, *received)
    if source is not None:
        args += near_core(source)
    specs = [VM] * len(args)
    aliases = {}
    if into is not None:
        aliases = {len(args): 0}
        args.append(into)
        specs.append(HB)
    return pl.pallas_call(
        partial(react_kernel, slot=slot, strip=strip, fixed=2 * height,
                sizes=(len(own), len(other), len(received))),
        in_specs=specs,
        out_specs=HB,
        scratch_shapes=[
            pltpu.VMEM((count, height, width), f32), pltpu.VMEM((height, width), f32),
            pltpu.SemaphoreType.DMA((height // SUB,)),
        ],
        out_shape=jax.ShapeDtypeStruct(shape, f32),
        input_output_aliases=aliases,
        compiler_params=small,
        name="react",
    )(*args)


def shards(tracers, u, v, surface, depth, wet_mask, river_cells, river_loads, kinetics):
    count, own_levels, height, _ = tracers.shape
    groups, tys, txs = (lax.axis_size(a) for a in ("grp", "ty", "tx"))
    levels = own_levels * groups
    assert own_levels == 2 and groups in (2, 4)
    sent = 5 * height // 8
    cut = (height // 2, height - height // 2)
    cell_args = (tracers, u, v, depth, wet_mask, levels)

    swap = [(i, i ^ 1) for i in range(groups)]
    middle = [(i, i + 1) for i in range(1, groups - 1, 2)]
    middle = middle + [(b, a) for a, b in middle]
    early = early_advection(*cell_args, sent)
    near_x_lo = lax.ppermute(early, "grp", swap)
    c, x_hi, *m, fields, north, south, sides = closed_advection(*cell_args, sent, cut)

    up = [(i, i + 1) for i in range(tys - 1)]
    down = [(i + 1, i) for i in range(tys - 1)]
    from_south = lax.ppermute(north, "ty", up)
    from_north = lax.ppermute(south, "ty", down)
    if txs == 2:
        from_west = from_east = lax.ppermute(sides, "tx", [(0, 1), (1, 0)])
    else:
        from_west = lax.ppermute(sides, "tx", [(i, i + 1) for i in range(txs - 1)])
        from_east = lax.ppermute(sides, "tx", [(i + 1, i) for i in range(txs - 1)])
    rates, source = rates_and_source(river_cells, river_loads, kinetics, wet_mask)
    halos = (from_north, from_south, from_west, from_east)
    packet, x_fix, m_fix = face_corrections(fields, north, south, sides, halos, levels, count)
    near = lax.ppermute(packet, "grp", swap)
    x_lo, x_hi, *mended = mend(x_fix, m_fix, early, x_hi, *m)
    near_x_hi = lax.ppermute(x_hi, "grp", swap)
    near_m = [lax.ppermute(mended[0], "grp", middle)]
    if groups == 4:
        handed = lax.ppermute(m[1], "grp", [(1, 3), (2, 0)])
        near_m.append(lax.ppermute(handed, "grp", [(3, 2), (0, 1)]))
    else:
        near_m.append(lax.ppermute(m[1], "grp", middle))

    columns = pair_sum(packet, near, 2 * height, count)
    if groups == 4:
        far = lax.ppermute(columns, "grp", [(i, i ^ 2) for i in range(groups)])
    else:
        far = jnp.zeros_like(columns)
    new_surface, pressure, south_state, west_state = new_surface_and_pressure(
        packet, near, far, fields, surface, depth, wet_mask, levels
    )
    north_state = lax.ppermute(south_state, "ty", down)
    east_state = lax.ppermute(west_state, "tx", [(i + 1, i) for i in range(txs - 1)])
    new_east, new_north, new_surface = momentum(
        u, v, depth, wet_mask, new_surface, pressure, halos, (north_state, east_state), count
    )

    step = partial(react, tracers.shape, c, wet_mask, rates)
    x = (x_lo, x_hi)
    out = step(0, x, mended, (near_x_lo, near_x_hi), near)
    out = step(1, mended, x, near_m, far, source, into=out)
    return (out, new_east, new_north, new_surface)


def solution(mesh):
    field = P("grp", "ty", "tx")
    plane = P("ty", "tx")
    return jax.shard_map(
        shards,
        mesh=mesh,
        in_specs=(
            P(None, "grp", "ty", "tx"), field, field, plane, plane, plane,
            P(("ty", "tx")), P(("ty", "tx"), None), P(),
        ),
        out_specs=(P(None, "grp", "ty", "tx"), field, field, plane),
        check_vma=False,
    )
```

```python
from functools import partial

import jax
import jax.numpy as jnp
from jax import lax
from jax.experimental import pallas as pl
from jax.experimental.pallas import tpu as pltpu
from jax.sharding import PartitionSpec as P


eta_rate = 0.25
gravity_rate = 0.25
baroclinic_rate = 0.4
viscous_rate = 0.1
friction_rate = 0.3
advect_rate = 0.3
mixing_rate = 0.2
haline_coef = 0.8
thermal_coef = 0.2
warming_rate = 0.46

f32 = jnp.float32
SUB = 8


def lanes_of(shape):
    return lax.broadcasted_iota(jnp.int32, shape, len(shape) - 1)


def rows_of(shape):
    return lax.broadcasted_iota(jnp.int32, shape, len(shape) - 2)


def east_of(x):
    return pltpu.roll(x, x.shape[-1] - 1, x.ndim - 1)


def west_of(x):
    return pltpu.roll(x, 1, x.ndim - 1)


def north_of(x):
    return pltpu.roll(x, x.shape[-2] - 1, x.ndim - 2)


def south_of(x):
    return pltpu.roll(x, 1, x.ndim - 2)


def keep(ref, rows, value):
    ref[rows, :] = value


VM = pl.BlockSpec(memory_space=pltpu.VMEM)


small = pltpu.CompilerParams(vmem_limit_bytes=16 << 20)


def near_core(*arrays):
    return [pltpu.with_memory_space_constraint(a, pltpu.VMEM) for a in arrays]


def far_core(*arrays):
    return [pltpu.with_memory_space_constraint(a, pltpu.HBM) for a in arrays]


def kept(shape):
    return pltpu.VMEM(shape, f32)


SM = pl.BlockSpec(memory_space=pltpu.SMEM)
HB = pl.BlockSpec(memory_space=pl.ANY)


def places():
    g, groups = lax.axis_index("grp"), lax.axis_size("grp")
    return g, groups, (1 - g % 2, g % 2)


def as_f32(flag):
    return jnp.where(flag, 1.0, 0.0).astype(f32)


def pick(refs, row):
    for ref in refs:
        if row < ref.shape[1]:
            return ref, row
        row -= ref.shape[1]


def strips(height, strip, *parts):
    ends = {height}
    for part in parts:
        ends |= {sum(part[:k + 1]) for k in range(len(part))}
    first = 0
    while first < height:
        size = min(strip, min(e for e in ends if e > first) - first)
        yield first, size
        first += size


def rows_in(parts):
    return [p.shape[1] for p in parts]


def weights(coef_ref, u, v, depth, wet, levels):
    height, width = depth.shape
    lane, row = lanes_of((height, width)), rows_of((height, width))
    half_e = 0.5 * (depth + east_of(depth)) * (wet * east_of(wet))
    half_n = 0.5 * (depth + north_of(depth)) * (wet * north_of(wet))
    flow_e = jnp.where(lane < width - 1, u * half_e / levels, 0.0)
    flow_n = jnp.where(row < height - 1, v * half_n / levels, 0.0)
    flow_w, flow_s = west_of(flow_e), south_of(flow_n)
    scale = advect_rate * levels / depth
    coef_ref[0] = 1.0 - scale * (
        jnp.maximum(flow_e, 0.0) - jnp.minimum(flow_w, 0.0)
        + jnp.maximum(flow_n, 0.0) - jnp.minimum(flow_s, 0.0)
    )
    coef_ref[1] = -scale * jnp.minimum(flow_e, 0.0)
    coef_ref[2] = scale * jnp.maximum(flow_w, 0.0)
    coef_ref[3] = -scale * jnp.minimum(flow_n, 0.0)
    coef_ref[4] = scale * jnp.maximum(flow_s, 0.0)
    return flow_e - flow_w + flow_n - flow_s


def weighed(coefs, c, above, under):
    return (
        coefs[0] * c + coefs[1] * east_of(c) + coefs[2] * west_of(c)
        + coefs[3] * above + coefs[4] * under
    )


def early_kernel(
    c_hbm, u_hbm, v_hbm, depth_hbm, wet_hbm, out_ref,
    c_ref, u_ref, v_ref, depth_ref, wet_ref, coef_ref, flat_sem, c_sem, *, levels, strip,
):
    _, _, at_level = places()
    count, taken, _ = c_ref.shape
    at, rows = at_level[0], pl.ds(0, taken)
    flat = [
        pltpu.make_async_copy(h, r, flat_sem.at[k])
        for k, (h, r) in enumerate((
            (depth_hbm.at[rows], depth_ref), (wet_hbm.at[rows], wet_ref),
            (u_hbm.at[at, rows], u_ref), (v_hbm.at[at, rows], v_ref),
        ))
    ]
    bulk = pltpu.make_async_copy(c_hbm.at[:, at, rows], c_ref, c_sem)
    for copy in flat:
        copy.start()
    bulk.start()
    for copy in flat:
        copy.wait()
    weights(coef_ref, u_ref[...], v_ref[...], depth_ref[...], wet_ref[...].astype(f32), levels)
    bulk.wait()
    for first in range(0, out_ref.shape[1], strip):
        here = pl.ds(first, strip)
        coefs = [coef_ref[k, here, :] for k in range(5)]
        for t in range(count):
            c = c_ref[t, here, :]
            above = c_ref[t, pl.ds(first + 1, strip), :]
            under = c_ref[t, pl.ds(first - 1, strip), :] if first else south_of(c)
            out_ref[t, here, :] = weighed(coefs, c, above, under)


def early_advection(tracers, u, v, depth, wet_mask, levels, rows, strip=16):
    count, _, _, width = tracers.shape
    taken = rows + SUB
    plane = pltpu.VMEM((taken, width), f32)
    return pl.pallas_call(
        partial(early_kernel, levels=levels, strip=strip),
        in_specs=[HB] * 5,
        out_specs=VM,
        out_shape=kept((count, rows, width)),
        scratch_shapes=[
            pltpu.VMEM((count, taken, width), f32), plane, plane, plane,
            pltpu.VMEM((taken, width), jnp.int32), pltpu.VMEM((5, taken, width), f32),
            pltpu.SemaphoreType.DMA((4,)), pltpu.SemaphoreType.DMA,
        ],
        compiler_params=small,
        name="early",
    )(*far_core(tracers, u, v, depth, wet_mask))


def edges_kernel(
    c_hbm, u_hbm, v_hbm, depth_hbm, wet_hbm,
    c_ref, coef_ref, fields_ref, north_ref, south_ref, sides_ref,
    u_ref, v_ref, depth_ref, wet_ref, turned_ref, flat_sem, c_sem, *, levels, count, parts, strip,
):
    _, _, at_level = places()
    height, width = depth_ref.shape
    chunk = count // parts
    flat = [
        pltpu.make_async_copy(h, r, flat_sem.at[k])
        for k, (h, r) in enumerate(
            ((depth_hbm, depth_ref), (wet_hbm, wet_ref), (u_hbm, u_ref), (v_hbm, v_ref))
        )
    ]
    for copy in flat:
        copy.start()
    bulk = []
    for slot in range(2):
        for part in range(parts):
            some = pl.ds(part * chunk, chunk)
            bulk.append(pltpu.make_async_copy(
                c_hbm.at[some, at_level[slot]], c_ref.at[slot, some], c_sem.at[slot, part]
            ))
            bulk[-1].start()
    north_ref[...] = jnp.zeros_like(north_ref)
    south_ref[...] = jnp.zeros_like(south_ref)
    for copy in flat:
        copy.wait()
    depth, wet = depth_ref[...], wet_ref[...].astype(f32)

    def lines(field, q):
        keep(north_ref, pl.ds(q, 1), field[height - 1:])
        keep(south_ref, pl.ds(q, 1), field[:1])

    def gather(got, field, q):
        mask = lanes_of((1, width)) // 2 == q
        return jnp.where(mask, pltpu.roll(field, (2 * q + 1) % width, 1), got)

    turned = jnp.zeros((height, width), f32)
    for q, field in ((4, depth), (5, wet)):
        lines(field, 2 * count + q)
        turned = gather(turned, field, 2 * count + q)
    for slot in range(2):
        u, v = u_ref[at_level[slot]], v_ref[at_level[slot]]
        lines(u, 2 * count + slot)
        lines(v, 2 * count + 2 + slot)
        turned = gather(turned, u, 2 * count + slot)
        turned = gather(turned, v, 2 * count + 2 + slot)
        fields_ref[slot] = weights(coef_ref.at[slot], u, v, depth, wet, levels)
    turned_ref[...] = turned

    for slot in range(2):
        for part in range(parts):
            bulk[slot * parts + part].wait()
            if part == 0:
                fields_ref[2 + slot] = haline_coef * c_ref[slot, 0] - thermal_coef * c_ref[slot, 1]
            some = range(part * chunk, (part + 1) * chunk)
            for t in some:
                keep(south_ref, pl.ds(slot * count + t, 1), c_ref[slot, t, pl.ds(0, 1), :])
                keep(north_ref, pl.ds(slot * count + t, 1), c_ref[slot, t, pl.ds(height - 1, 1), :])
            for first in range(0, height, strip):
                here = pl.ds(first, strip)
                got = turned_ref[here, :]
                for t in some:
                    got = gather(got, c_ref[slot, t, here, :], slot * count + t)
                turned_ref[here, :] = got
    sides_ref[...] = turned_ref[...].T[: sides_ref.shape[0]]


def tile_edges(tracers, u, v, depth, wet_mask, levels, parts=2, strip=32):
    count, _, height, width = tracers.shape
    edge_rows = -(-(2 * count + 6) // SUB) * SUB
    assert width == height and 2 * edge_rows <= width
    outs = [
        kept((2, count, height, width)), kept((2, 5, height, width)), kept((4, height, width)),
        kept((edge_rows, width)), kept((edge_rows, width)), kept((2 * edge_rows, height)),
    ]
    plane = pltpu.VMEM((height, width), f32)
    return pl.pallas_call(
        partial(edges_kernel, levels=levels, count=count, parts=parts, strip=strip),
        in_specs=[HB] * 5,
        out_specs=[VM] * len(outs),
        out_shape=outs,
        scratch_shapes=[
            pltpu.VMEM(u.shape, f32), pltpu.VMEM(v.shape, f32), plane,
            pltpu.VMEM((height, width), jnp.int32), plane,
            pltpu.SemaphoreType.DMA((4,)), pltpu.SemaphoreType.DMA((2, parts)),
        ],
        compiler_params=small,
        name="edges",
    )(*far_core(tracers, u, v, depth, wet_mask))


def closed_kernel(c_ref, coef_ref, x_hi, m_lo, m_hi, *, strip):
    _, count, height, _ = c_ref.shape
    sent = height - x_hi.shape[1]
    for slot in range(2):
        cut = ([sent, x_hi.shape[1]], rows_in((m_lo, m_hi)))[slot]
        for first, size in strips(height, strip, cut):
            if slot == 0 and first < sent:
                continue
            here = pl.ds(first, size)
            coefs = [coef_ref[slot, k, here, :] for k in range(5)]
            to, at = pick((m_lo, m_hi), first) if slot else (x_hi, first - sent)
            for t in range(count):
                c = c_ref[slot, t, here, :]
                if first + size < height:
                    above = c_ref[slot, t, pl.ds(first + 1, size), :]
                else:
                    above = north_of(c)
                under = c_ref[slot, t, pl.ds(first - 1, size), :] if first else south_of(c)
                to[t, pl.ds(at, size), :] = weighed(coefs, c, above, under)


def closed_advection(c, coefs, cuts, strip=16):
    _, count, _, width = c.shape
    return pl.pallas_call(
        partial(closed_kernel, strip=strip),
        in_specs=[VM] * 2,
        out_specs=[VM] * 3,
        out_shape=[kept((count, rows, width)) for rows in cuts],
        compiler_params=small,
        name="closed",
    )(*near_core(c, coefs))


def faces_kernel(
    fields_ref, north_ref, south_ref, sides_ref, from_north_ref, from_south_ref,
    from_west_ref, from_east_ref, packet_ref, x_fix_ref, m_fix_ref, *, levels, count,
):
    height, width = fields_ref.shape[1:]
    x, txs = lax.axis_index("tx"), lax.axis_size("tx")
    half_rows = sides_ref.shape[0] // 2
    us, vs, ds, ws = 2 * count, 2 * count + 2, 2 * count + 4, 2 * count + 5
    east, west = (pl.ds(0, half_rows, stride=2), pl.ds(1, half_rows, stride=2))
    own = (north_ref[...], south_ref[...], sides_ref[west, :], sides_ref[east, :])
    halo = (from_north_ref[...], from_south_ref[...], from_west_ref[east, :], from_east_ref[west, :])
    known = (1.0, 1.0, as_f32(x > 0), as_f32(x < txs - 1))

    def side(k, slot):
        mine, theirs = own[k], halo[k]
        outgoing = k in (0, 3)
        speed = (mine if outgoing else theirs)[(vs if k < 2 else us) + slot:][:1]
        d_mine, d_theirs = mine[ds:ds + 1], theirs[ds:ds + 1]
        opened = mine[ws:ws + 1] * (theirs[ws:ws + 1] * known[k])
        flow = speed * (0.5 * (d_mine + d_theirs) * opened) / levels
        c_mine = mine[slot * count:(slot + 1) * count]
        c_theirs = theirs[slot * count:(slot + 1) * count]
        scale = advect_rate * levels / d_mine
        if outgoing:
            return -scale * (jnp.maximum(flow, 0.0) * c_mine + jnp.minimum(flow, 0.0) * c_theirs), flow
        return scale * (jnp.maximum(flow, 0.0) * c_theirs + jnp.minimum(flow, 0.0) * c_mine), -flow

    flows = [0.0, 0.0, 0.0, 0.0]
    for slot in range(2):
        ref = (x_fix_ref, m_fix_ref)[slot]
        for k in range(4):
            fix, flow = side(k, slot)
            flows[k] = flows[k] + flow
            if k < 2:
                ref[pl.ds(k * count, count), :] = fix
            else:
                ref[pl.ds(2 * count + 3 - k, count, stride=2), :] = fix
    lane, row = lanes_of((height, width)), rows_of((height, width))
    spill = jnp.concatenate([flows[3], flows[2], jnp.zeros((width - 2, height), f32)], 0).T
    spill = east_of(spill)
    spill = jnp.where((lane == 0) | (lane == width - 1), spill, 0.0)
    spill = spill + jnp.where(row == 0, flows[1], 0.0) + jnp.where(row == height - 1, flows[0], 0.0)
    packet_ref[pl.ds(0, height), :] = fields_ref[0] + fields_ref[1] + spill
    packet_ref[pl.ds(height, height), :] = fields_ref[2] + fields_ref[3]
    packet_ref[pl.ds(2 * height, 3 * count), :] = x_fix_ref[pl.ds(count, 3 * count), :]
    packet_ref[pl.ds(2 * height + 3 * count, count), :] = m_fix_ref[pl.ds(0, count), :]
    packet_ref[pl.ds(2 * height + 4 * count, 2 * count), :] = m_fix_ref[pl.ds(2 * count, 2 * count), :]


def face_corrections(fields, north, south, sides, halos, levels, count):
    height, width = fields.shape[1:]
    return pl.pallas_call(
        partial(faces_kernel, levels=levels, count=count),
        in_specs=[VM] * 8,
        out_specs=[VM] * 3,
        out_shape=[kept((2 * height + 6 * count, width))] + [kept((4 * count, width))] * 2,
        compiler_params=small,
        name="faces",
    )(*near_core(fields, north, south, sides, *halos))


def turned_columns(rows):
    return jnp.concatenate([rows, jnp.zeros((rows.shape[1] - rows.shape[0], rows.shape[1]), f32)], 0).T


def mend_kernel(x_fix, m_fix, *rest, strip):
    ins, outs, turned_ref = rest[:4], rest[4:8], rest[8]
    height, width = turned_ref.shape[1:]
    count = ins[0].shape[0]
    for slot, fix in enumerate((x_fix, m_fix)):
        turned_ref[slot] = turned_columns(fix[pl.ds(2 * count, 2 * count), :])
        base = 0
        some = slice(2, 4) if slot else slice(0, 2)
        for source, target in zip(ins[some], outs[some]):
            for first, size in strips(source.shape[1], strip):
                here = pl.ds(first, size)
                lane, row = lanes_of((size, width)), rows_of((size, width))
                rim = (lane == 0) | (lane == width - 1)
                columns = turned_ref[slot, pl.ds(base + first, size), :]
                for t in range(count):
                    value = source[t, here, :]
                    value = value + jnp.where(rim, pltpu.roll(columns, width - 1 - 2 * t, 1), 0.0)
                    if base + first == 0:
                        value = value + jnp.where(row == 0, fix[pl.ds(count + t, 1), :], 0.0)
                    if base + first + size == height:
                        value = value + jnp.where(row == size - 1, fix[pl.ds(t, 1), :], 0.0)
                    target[t, here, :] = value
            base += source.shape[1]


def mend(x_fix, m_fix, *parts, strip=16):
    height = sum(rows_in(parts[:2]))
    return pl.pallas_call(
        partial(mend_kernel, strip=strip),
        in_specs=[VM] * 6,
        out_specs=[VM] * 4,
        out_shape=[kept(p.shape) for p in parts],
        input_output_aliases={3: 1, 4: 2},
        scratch_shapes=[pltpu.VMEM((2, height, x_fix.shape[1]), f32)],
        compiler_params=small,
        name="mend",
    )(*near_core(x_fix, m_fix, *parts))


def pair_kernel(a_ref, b_ref, out_ref, *, rows):
    more = out_ref.shape[0] - rows
    out_ref[pl.ds(0, rows), :] = a_ref[pl.ds(0, rows), :] + b_ref[pl.ds(0, rows), :]
    out_ref[pl.ds(rows, more), :] = b_ref[pl.ds(b_ref.shape[0] - more, more), :]


def pair_sum(packet, near, rows, count):
    return pl.pallas_call(
        partial(pair_kernel, rows=rows), in_specs=[VM] * 2, out_specs=VM,
        out_shape=kept((rows + 3 * count, packet.shape[1])), compiler_params=small, name="pair",
    )(*near_core(packet, near))


def surface_kernel(
    packet_ref, near_ref, far_ref, fields_ref, surface_ref, depth_ref, wet_ref,
    surface_out, pressure_out, south_out, west_out, *, levels,
):
    g, _, at_level = places()
    height, width = surface_ref.shape
    top, below = pl.ds(0, height), pl.ds(height, height)
    near_above, far_above = as_f32(g % 2 == 1), as_f32(g >= 2)
    total = packet_ref[top, :] + near_ref[top, :] + far_ref[top, :]
    surface = surface_ref[...] - eta_rate * wet_ref[...].astype(f32) * total
    above = near_above * near_ref[below, :] + far_above * far_ref[below, :]
    surface_out[...] = surface
    lane = lanes_of((height, width))
    turned = jnp.where(lane == 0, surface, 0.0)
    south_out[...] = jnp.zeros_like(south_out)
    keep(south_out, pl.ds(0, 1), surface[:1])
    for slot in range(2):
        lower = as_f32(at_level[slot] == 1)
        density = fields_ref[2 + slot]
        column = above + lower * fields_ref[3 - slot] + density - 0.5 * density
        pressure = baroclinic_rate * depth_ref[...] * column / levels
        pressure_out[slot] = pressure
        keep(south_out, pl.ds(1 + slot, 1), pressure[:1])
        turned = jnp.where(lane == 1 + slot, pltpu.roll(pressure, 1 + slot, 1), turned)
    west_out[...] = turned.T[:SUB]


def new_surface_and_pressure(packet, near, far, fields, surface, depth, wet_mask, levels):
    height, width = surface.shape
    args = (packet, near, far, fields, surface, depth, wet_mask)
    outs = [(height, width), (2, height, width), (SUB, width), (SUB, height)]
    return pl.pallas_call(
        partial(surface_kernel, levels=levels),
        in_specs=[VM] * len(args), out_specs=[VM] * len(outs),
        out_shape=[kept(s) for s in outs],
        compiler_params=small,
        name="level",
    )(*near_core(*args))


def momentum_kernel(
    u_ref, v_ref, depth_ref, wet_ref, surface_ref, pressure_ref, from_north_ref,
    from_south_ref, from_west_ref, from_east_ref, north_state_ref, east_state_ref,
    east_out, north_out, surface_out, *, count,
):
    g, groups, at_level = places()
    x, txs = lax.axis_index("tx"), lax.axis_size("tx")
    height, width = depth_ref.shape
    lane, row = lanes_of((height, width)), rows_of((height, width))
    us = 2 * count
    half_rows = from_west_ref.shape[0] // 2
    known_w, known_e = as_f32(x > 0), as_f32(x < txs - 1)
    west_halo = from_west_ref[pl.ds(0, half_rows, stride=2), :][us:us + SUB] * known_w
    east_halo = from_east_ref[pl.ds(1, half_rows, stride=2), :][us:us + SUB] * known_e
    used = 3 * SUB
    columns = jnp.concatenate(
        [west_halo, east_halo, east_state_ref[...], jnp.zeros((width - used, height), f32)], 0
    ).T
    north_halo, south_halo = from_north_ref[...], from_south_ref[...]

    def shifted(field, q, state=None):
        e_from = SUB + q if state is None else 2 * SUB + state
        e = jnp.where(lane == width - 1, pltpu.roll(columns, width - 1 - e_from, 1), east_of(field))
        line = north_halo[us + q:us + q + 1] if state is None else north_state_ref[pl.ds(state, 1), :]
        n = jnp.where(row == height - 1, line, north_of(field))
        return e, n

    def whole(field, q):
        e, n = shifted(field, q)
        w = jnp.where(lane == 0, pltpu.roll(columns, (width - q) % width, 1), west_of(field))
        s = jnp.where(row == 0, south_halo[us + q:us + q + 1], south_of(field))
        return n + s + e + w - 4.0 * field

    wet = wet_ref[...].astype(f32)
    wet_e, wet_n = shifted(wet, 5)
    open_e, open_n = wet * wet_e, wet * wet_n
    surface = surface_ref[...]
    surface_out[...] = surface
    surface_e, surface_n = shifted(surface, 0, 0)
    for slot in range(2):
        at = at_level[slot]
        bottom = as_f32((g == groups - 1) & (at == 1))
        pressure = pressure_ref[slot]
        pressure_e, pressure_n = shifted(pressure, 0, 1 + slot)
        u, v = u_ref[at], v_ref[at]
        east_out[at] = open_e * (
            u - gravity_rate * (surface_e - surface) - (pressure_e - pressure)
            + viscous_rate * whole(u, slot) - friction_rate * bottom * u
        )
        north_out[at] = open_n * (
            v - gravity_rate * (surface_n - surface) - (pressure_n - pressure)
            + viscous_rate * whole(v, 2 + slot) - friction_rate * bottom * v
        )


def momentum(u, v, depth, wet_mask, surface, pressure, halos, states, count):
    args = (u, v, depth, wet_mask, surface, pressure, *halos, *states)
    return pl.pallas_call(
        partial(momentum_kernel, count=count),
        in_specs=[VM] * len(args), out_specs=[VM] * 3,
        out_shape=[jax.ShapeDtypeStruct(a.shape, f32) for a in (u, v, surface)],
        compiler_params=small,
        name="momentum",
    )(*near_core(*args))


def rates_kernel(cells_ref, loads_ref, kinetics_ref, wet_ref, out_ref, source_ref):
    g, _, _ = places()
    count, _, width = source_ref.shape
    size = count * SUB
    spread = (
        lax.broadcasted_iota(jnp.int32, (size, count), 0) // SUB
        == lax.broadcasted_iota(jnp.int32, (size, count), 1)
    ).astype(f32)
    full = jnp.dot(spread, kinetics_ref[...], precision=lax.Precision.HIGHEST)
    full = lax.dot_general(
        full, spread, (((1,), (1,)), ((), ())), precision=lax.Precision.HIGHEST
    )
    same = lax.broadcasted_iota(jnp.int32, (size, size), 0) % SUB
    same = same == lax.broadcasted_iota(jnp.int32, (size, size), 1) % SUB
    high, low = split(jnp.where(same, full, 0.0))
    out_ref[...] = jnp.concatenate([high, high, low], 1)
    source_ref[...] = jnp.zeros_like(source_ref)

    @pl.when(g == 0)
    def _():
        @pl.loop(0, cells_ref.shape[0])
        def _(r):
            at, spot = pl.ds(cells_ref[r] // width, 1), cells_ref[r] % width
            here = (lanes_of((1, width)) == spot) & (wet_ref[at, :] != 0)
            for t in range(count):
                source_ref[t, at, :] = source_ref[t, at, :] + jnp.where(here, loads_ref[r, t], 0.0)


def rates_and_source(cells, loads, kinetics, wet_mask):
    count = kinetics.shape[0]
    size = count * SUB
    return pl.pallas_call(
        rates_kernel, in_specs=[SM, SM, VM, VM], out_specs=[VM, VM],
        out_shape=[pltpu.VMEM((size, 3 * size), jnp.bfloat16), kept((count,) + wet_mask.shape)],
        compiler_params=small, name="rates",
    )(cells, loads, kinetics, *near_core(wet_mask))


def split(x):
    high = x.astype(jnp.bfloat16)
    return high, (x - high.astype(f32)).astype(jnp.bfloat16)


def mixing_rates(slot):
    g, groups, _ = places()
    has_next = 1.0 if slot == 0 else as_f32((g > 0) & (g < groups - 1))
    return 1.0 - mixing_rate - mixing_rate * has_next, mixing_rate * has_next


def mixed_rows(t, first, size, parts, fix_ref, fixed, turned_ref, rates, border, slot):
    keep_rate, next_rate = rates
    height = turned_ref.shape[0]
    (own, at), (other, there) = (pick(refs, first) for refs in parts)
    value = keep_rate * own[t, pl.ds(at, size), :] + mixing_rate * other[t, pl.ds(there, size), :]
    if (first < border) == (slot == 0):
        lane, row = lanes_of((size, height)), rows_of((size, height))
        rim = (lane == 0) | (lane == height - 1)
        columns = turned_ref[pl.ds(first, size), :]
        value = value + jnp.where(rim, pltpu.roll(columns, height - 1 - 2 * t, 1), 0.0)
        if first in (0, height - size):
            line = next_rate * fix_ref[pl.ds(fixed + t, 1), :]
            value = value + jnp.where(row == (size - 1 if first else 0), line, 0.0)
    return value


def turn_share(fix_ref, fixed, count, turned_ref, next_rate):
    turned_ref[...] = next_rate * turned_columns(fix_ref[pl.ds(fixed + count, 2 * count), :])


def ready_kernel(c_ref, wet_ref, fix_ref, *rest, fixed, sizes, border, strip):
    ready_ref, turned_ref = rest[-2:]
    parts = [rest[:sizes[0]], rest[sizes[0]:sum(sizes)]]
    count, height, _ = ready_ref.shape
    rates = mixing_rates(1)
    turn_share(fix_ref, fixed, count, turned_ref, rates[1])
    for first, size in strips(height, strip, *(rows_in(refs) for refs in parts)):
        here = pl.ds(first, size)
        wet = wet_ref[here, :] != 0
        for t in range(count):
            value = mixed_rows(t, first, size, parts, fix_ref, fixed, turned_ref, rates, border, 1)
            ready_ref[t, here, :] = jnp.where(wet, value, c_ref[1, t, here, :])


def make_ready(c, wet_mask, fix, own, other, fixed, border, strip=16):
    _, count, height, width = c.shape
    args = near_core(c, wet_mask, fix, *own, *other)
    return pl.pallas_call(
        partial(ready_kernel, fixed=fixed, sizes=(len(own), len(other)), border=border, strip=strip),
        in_specs=[VM] * len(args),
        out_specs=VM,
        out_shape=kept((count, height, width)),
        scratch_shapes=[pltpu.VMEM((height, width), f32)],
        compiler_params=small,
        name="ready",
    )(*args)


def react_kernel(wet_ref, rates_ref, *rest, slot, fixed, sizes, border, strip):
    out_hbm, done_ref, turned_ref, out_sem = rest[-4:]
    parts = [rest[sum(sizes[:k]):sum(sizes[:k + 1])] for k in range(len(sizes))]
    more = rest[sum(sizes):]
    _, _, at_level = places()
    count, height, width = done_ref.shape
    mixing = mixing_rates(slot)
    if slot == 0:
        turn_share(more[1], fixed, count, turned_ref, mixing[1])
    rates = rates_ref[...]
    copies = []
    for first, size in strips(height, strip, *(rows_in(refs) for refs in parts)):
        here = pl.ds(first, size)
        groups_of = size // SUB
        beyond, at = pick(parts[0], first)
        wet = wet_ref[here, :] != 0
        passed = jnp.where(wet, mixing[1], 0.0)
        values = []
        for t in range(count):
            far = beyond[t, pl.ds(at, size), :]
            if slot == 0:
                value = mixed_rows(
                    t, first, size, parts[1:], more[1], fixed, turned_ref, mixing, border, 0
                )
                values.append(jnp.where(wet, value + mixing[1] * far, more[0][0, t, here, :]))
            else:
                values.append(more[0][t, here, :] + passed * far)
        stacked = jnp.concatenate(
            [
                jnp.concatenate([v[k * SUB:(k + 1) * SUB] for v in values], 0)
                for k in range(groups_of)
            ],
            1,
        )
        high, low = split(stacked)
        reaction = jnp.dot(
            rates, jnp.concatenate([high, low, high], 0), preferred_element_type=f32
        )
        warming = jnp.where(wet, jnp.exp(warming_rate * values[1]), 0.0)
        for t in range(count):
            gained = jnp.concatenate(
                [reaction[t * SUB:(t + 1) * SUB, k * width:(k + 1) * width] for k in range(groups_of)],
                0,
            )
            done = values[t] + warming * gained
            done_ref[t, here, :] = done if slot == 0 else done + more[1][t, here, :]
        copies.append(pltpu.make_async_copy(
            done_ref.at[:, here], out_hbm.at[:, at_level[slot], here], out_sem.at[len(copies)]
        ))
        copies[-1].start()
    for copy in copies:
        copy.wait()


def react(shape, wet_mask, rates, slot, received, more, mixed=(), into=None, fixed=0, border=0,
          strip=16):
    count, _, height, width = shape
    sizes = tuple(len(part) for part in (received, *mixed))
    flat = [a for part in (received, *mixed) for a in part]
    args = near_core(wet_mask, rates, *flat, *more)
    specs = [VM] * len(args)
    aliases = {}
    if into is not None:
        aliases = {len(args): 0}
        args.append(into)
        specs.append(HB)
    return pl.pallas_call(
        partial(react_kernel, slot=slot, strip=strip, fixed=fixed, sizes=sizes, border=border),
        in_specs=specs,
        out_specs=HB,
        scratch_shapes=[
            pltpu.VMEM((count, height, width), f32), pltpu.VMEM((height, width), f32),
            pltpu.SemaphoreType.DMA((height // SUB,)),
        ],
        out_shape=jax.ShapeDtypeStruct(shape, f32),
        input_output_aliases=aliases,
        compiler_params=small,
        name="react",
    )(*args)


def shards(tracers, u, v, surface, depth, wet_mask, river_cells, river_loads, kinetics):
    count, own_levels, height, _ = tracers.shape
    groups, tys, txs = (lax.axis_size(a) for a in ("grp", "ty", "tx"))
    levels = own_levels * groups
    assert own_levels == 2 and groups in (2, 4)
    direct, border = height // 2, 5 * height // 8
    cuts = (height - border, direct, height - direct)
    cell_args = (tracers, u, v, depth, wet_mask, levels)

    swap = [(i, i ^ 1) for i in range(groups)]
    middle = [(i, i + 1) for i in range(1, groups - 1, 2)]
    middle = middle + [(b, a) for a, b in middle]
    early = early_advection(*cell_args, border)
    near_x_lo = lax.ppermute(early, "grp", swap)
    c, coefs, fields, north, south, sides = tile_edges(*cell_args)

    up = [(i, i + 1) for i in range(tys - 1)]
    down = [(i + 1, i) for i in range(tys - 1)]
    from_south = lax.ppermute(north, "ty", up)
    from_north = lax.ppermute(south, "ty", down)
    if txs == 2:
        from_west = from_east = lax.ppermute(sides, "tx", [(0, 1), (1, 0)])
    else:
        from_west = lax.ppermute(sides, "tx", [(i, i + 1) for i in range(txs - 1)])
        from_east = lax.ppermute(sides, "tx", [(i + 1, i) for i in range(txs - 1)])
    x_hi, *m = closed_advection(c, coefs, cuts)
    rates, source = rates_and_source(river_cells, river_loads, kinetics, wet_mask)
    halos = (from_north, from_south, from_west, from_east)
    packet, x_fix, m_fix = face_corrections(fields, north, south, sides, halos, levels, count)
    near = lax.ppermute(packet, "grp", swap)
    *x, m_0, m_1 = mend(x_fix, m_fix, early, x_hi, *m)
    near_x_hi = lax.ppermute(x[1], "grp", swap)
    near_m = [lax.ppermute(m_0, "grp", middle)]
    if groups == 4:
        handed = lax.ppermute(m[1], "grp", [(1, 3), (2, 0)])
        near_m.append(lax.ppermute(handed, "grp", [(3, 2), (0, 1)]))
    else:
        near_m.append(lax.ppermute(m[1], "grp", middle))

    columns = pair_sum(packet, near, 2 * height, count)
    if groups == 4:
        far = lax.ppermute(columns, "grp", [(i, i ^ 2) for i in range(groups)])
    else:
        far = jnp.zeros_like(columns)
    new_surface, pressure, south_state, west_state = new_surface_and_pressure(
        packet, near, far, fields, surface, depth, wet_mask, levels
    )
    north_state = lax.ppermute(south_state, "ty", down)
    east_state = lax.ppermute(west_state, "tx", [(i + 1, i) for i in range(txs - 1)])
    new_east, new_north, new_surface = momentum(
        u, v, depth, wet_mask, new_surface, pressure, halos, (north_state, east_state), count
    )

    mixed = (m_0, m_1)
    out = react(
        tracers.shape, wet_mask, rates, 0, (near_x_lo, near_x_hi), (c, near),
        (x, mixed), fixed=2 * height, border=border,
    )
    ready = make_ready(c, wet_mask, far, mixed, x, 2 * height, direct)
    out = react(tracers.shape, wet_mask, rates, 1, near_m, (ready, source), into=out)
    return (out, new_east, new_north, new_surface)


def solution(mesh):
    field = P("grp", "ty", "tx")
    plane = P("ty", "tx")
    return jax.shard_map(
        shards,
        mesh=mesh,
        in_specs=(
            P(None, "grp", "ty", "tx"), field, field, plane, plane, plane,
            P(("ty", "tx")), P(("ty", "tx"), None), P(),
        ),
        out_specs=(P(None, "grp", "ty", "tx"), field, field, plane),
        check_vma=False,
    )
```

```python
from functools import partial

import jax
import jax.numpy as jnp
from jax import lax
from jax.experimental import pallas as pl
from jax.experimental.pallas import tpu as pltpu
from jax.sharding import PartitionSpec as P


eta_rate = 0.25
gravity_rate = 0.25
baroclinic_rate = 0.4
viscous_rate = 0.1
friction_rate = 0.3
advect_rate = 0.3
mixing_rate = 0.2
haline_coef = 0.8
thermal_coef = 0.2
warming_rate = 0.46

f32 = jnp.float32
SUB = 8


def lanes_of(shape):
    return lax.broadcasted_iota(jnp.int32, shape, len(shape) - 1)


def rows_of(shape):
    return lax.broadcasted_iota(jnp.int32, shape, len(shape) - 2)


def east_of(x):
    return pltpu.roll(x, x.shape[-1] - 1, x.ndim - 1)


def west_of(x):
    return pltpu.roll(x, 1, x.ndim - 1)


def north_of(x):
    return pltpu.roll(x, x.shape[-2] - 1, x.ndim - 2)


def south_of(x):
    return pltpu.roll(x, 1, x.ndim - 2)


def keep(ref, rows, value):
    ref[rows, :] = value


VM = pl.BlockSpec(memory_space=pltpu.VMEM)


small = pltpu.CompilerParams(vmem_limit_bytes=16 << 20)


def near_core(*arrays):
    return [pltpu.with_memory_space_constraint(a, pltpu.VMEM) for a in arrays]


def far_core(*arrays):
    return [pltpu.with_memory_space_constraint(a, pltpu.HBM) for a in arrays]


def kept(shape):
    return pltpu.VMEM(shape, f32)


SM = pl.BlockSpec(memory_space=pltpu.SMEM)
HB = pl.BlockSpec(memory_space=pl.ANY)


def places():
    g, groups = lax.axis_index("grp"), lax.axis_size("grp")
    return g, groups, (1 - g % 2, g % 2)


def as_f32(flag):
    return jnp.where(flag, 1.0, 0.0).astype(f32)


def pick(refs, row):
    for ref in refs:
        if row < ref.shape[1]:
            return ref, row
        row -= ref.shape[1]


def strips(height, strip, *parts):
    ends = {height}
    for part in parts:
        ends |= {sum(part[:k + 1]) for k in range(len(part))}
    first = 0
    while first < height:
        size = min(strip, min(e for e in ends if e > first) - first)
        yield first, size
        first += size


def rows_in(parts):
    return [p.shape[1] for p in parts]


def weights(coef_ref, u, v, depth, wet, levels):
    height, width = depth.shape
    lane, row = lanes_of((height, width)), rows_of((height, width))
    half_e = 0.5 * (depth + east_of(depth)) * (wet * east_of(wet))
    half_n = 0.5 * (depth + north_of(depth)) * (wet * north_of(wet))
    flow_e = jnp.where(lane < width - 1, u * half_e / levels, 0.0)
    flow_n = jnp.where(row < height - 1, v * half_n / levels, 0.0)
    flow_w, flow_s = west_of(flow_e), south_of(flow_n)
    scale = advect_rate * levels / depth
    coef_ref[0] = 1.0 - scale * (
        jnp.maximum(flow_e, 0.0) - jnp.minimum(flow_w, 0.0)
        + jnp.maximum(flow_n, 0.0) - jnp.minimum(flow_s, 0.0)
    )
    coef_ref[1] = -scale * jnp.minimum(flow_e, 0.0)
    coef_ref[2] = scale * jnp.maximum(flow_w, 0.0)
    coef_ref[3] = -scale * jnp.minimum(flow_n, 0.0)
    coef_ref[4] = scale * jnp.maximum(flow_s, 0.0)
    return flow_e - flow_w + flow_n - flow_s


def weighed(coefs, c, above, under):
    return (
        coefs[0] * c + coefs[1] * east_of(c) + coefs[2] * west_of(c)
        + coefs[3] * above + coefs[4] * under
    )


def early_kernel(
    c_hbm, u_hbm, v_hbm, depth_hbm, wet_hbm, out_ref,
    c_ref, u_ref, v_ref, depth_ref, wet_ref, coef_ref, flat_sem, c_sem, *, levels, strip,
):
    _, _, at_level = places()
    count, taken, _ = c_ref.shape
    at, rows = at_level[0], pl.ds(0, taken)
    flat = [
        pltpu.make_async_copy(h, r, flat_sem.at[k])
        for k, (h, r) in enumerate((
            (depth_hbm.at[rows], depth_ref), (wet_hbm.at[rows], wet_ref),
            (u_hbm.at[at, rows], u_ref), (v_hbm.at[at, rows], v_ref),
        ))
    ]
    bulk = pltpu.make_async_copy(c_hbm.at[:, at, rows], c_ref, c_sem)
    for copy in flat:
        copy.start()
    bulk.start()
    for copy in flat:
        copy.wait()
    weights(coef_ref, u_ref[...], v_ref[...], depth_ref[...], wet_ref[...].astype(f32), levels)
    bulk.wait()
    for first in range(0, out_ref.shape[1], strip):
        here = pl.ds(first, strip)
        coefs = [coef_ref[k, here, :] for k in range(5)]
        for t in range(count):
            c = c_ref[t, here, :]
            above = c_ref[t, pl.ds(first + 1, strip), :]
            under = c_ref[t, pl.ds(first - 1, strip), :] if first else south_of(c)
            out_ref[t, here, :] = weighed(coefs, c, above, under)


def early_advection(tracers, u, v, depth, wet_mask, levels, rows, strip=16):
    count, _, _, width = tracers.shape
    taken = rows + SUB
    plane = pltpu.VMEM((taken, width), f32)
    return pl.pallas_call(
        partial(early_kernel, levels=levels, strip=strip),
        in_specs=[HB] * 5,
        out_specs=VM,
        out_shape=kept((count, rows, width)),
        scratch_shapes=[
            pltpu.VMEM((count, taken, width), f32), plane, plane, plane,
            pltpu.VMEM((taken, width), jnp.int32), pltpu.VMEM((5, taken, width), f32),
            pltpu.SemaphoreType.DMA((4,)), pltpu.SemaphoreType.DMA,
        ],
        compiler_params=small,
        name="early",
    )(*far_core(tracers, u, v, depth, wet_mask))


def edges_kernel(
    c_hbm, u_hbm, v_hbm, depth_hbm, wet_hbm,
    c_ref, coef_ref, fields_ref, north_ref, south_ref, sides_ref,
    u_ref, v_ref, depth_ref, wet_ref, turned_ref, flat_sem, c_sem, *, levels, count, parts, strip,
):
    _, _, at_level = places()
    height, width = depth_ref.shape
    chunk = count // parts
    flat = [
        pltpu.make_async_copy(h, r, flat_sem.at[k])
        for k, (h, r) in enumerate(
            ((depth_hbm, depth_ref), (wet_hbm, wet_ref), (u_hbm, u_ref), (v_hbm, v_ref))
        )
    ]
    for copy in flat:
        copy.start()
    bulk = []
    for slot in range(2):
        for part in range(parts):
            some = pl.ds(part * chunk, chunk)
            bulk.append(pltpu.make_async_copy(
                c_hbm.at[some, at_level[slot]], c_ref.at[slot, some], c_sem.at[slot, part]
            ))
            bulk[-1].start()
    north_ref[...] = jnp.zeros_like(north_ref)
    south_ref[...] = jnp.zeros_like(south_ref)
    for copy in flat:
        copy.wait()
    depth, wet = depth_ref[...], wet_ref[...].astype(f32)

    def lines(field, q):
        keep(north_ref, pl.ds(q, 1), field[height - 1:])
        keep(south_ref, pl.ds(q, 1), field[:1])

    def gather(got, field, q):
        mask = lanes_of((1, width)) // 2 == q
        return jnp.where(mask, pltpu.roll(field, (2 * q + 1) % width, 1), got)

    turned = jnp.zeros((height, width), f32)
    for q, field in ((4, depth), (5, wet)):
        lines(field, 2 * count + q)
        turned = gather(turned, field, 2 * count + q)
    for slot in range(2):
        u, v = u_ref[at_level[slot]], v_ref[at_level[slot]]
        lines(u, 2 * count + slot)
        lines(v, 2 * count + 2 + slot)
        turned = gather(turned, u, 2 * count + slot)
        turned = gather(turned, v, 2 * count + 2 + slot)
        fields_ref[slot] = weights(coef_ref.at[slot], u, v, depth, wet, levels)
    turned_ref[...] = turned

    for slot in range(2):
        for part in range(parts):
            bulk[slot * parts + part].wait()
            if part == 0:
                fields_ref[2 + slot] = haline_coef * c_ref[slot, 0] - thermal_coef * c_ref[slot, 1]
            some = range(part * chunk, (part + 1) * chunk)
            for t in some:
                keep(south_ref, pl.ds(slot * count + t, 1), c_ref[slot, t, pl.ds(0, 1), :])
                keep(north_ref, pl.ds(slot * count + t, 1), c_ref[slot, t, pl.ds(height - 1, 1), :])
            for first in range(0, height, strip):
                here = pl.ds(first, strip)
                got = turned_ref[here, :]
                for t in some:
                    got = gather(got, c_ref[slot, t, here, :], slot * count + t)
                turned_ref[here, :] = got
    sides_ref[...] = turned_ref[...].T[: sides_ref.shape[0]]


def tile_edges(tracers, u, v, depth, wet_mask, levels, parts=2, strip=32):
    count, _, height, width = tracers.shape
    edge_rows = -(-(2 * count + 6) // SUB) * SUB
    assert width == height and 2 * edge_rows <= width
    outs = [
        kept((2, count, height, width)), kept((2, 5, height, width)), kept((4, height, width)),
        kept((edge_rows, width)), kept((edge_rows, width)), kept((2 * edge_rows, height)),
    ]
    plane = pltpu.VMEM((height, width), f32)
    return pl.pallas_call(
        partial(edges_kernel, levels=levels, count=count, parts=parts, strip=strip),
        in_specs=[HB] * 5,
        out_specs=[VM] * len(outs),
        out_shape=outs,
        scratch_shapes=[
            pltpu.VMEM(u.shape, f32), pltpu.VMEM(v.shape, f32), plane,
            pltpu.VMEM((height, width), jnp.int32), plane,
            pltpu.SemaphoreType.DMA((4,)), pltpu.SemaphoreType.DMA((2, parts)),
        ],
        compiler_params=small,
        name="edges",
    )(*far_core(tracers, u, v, depth, wet_mask))


def closed_kernel(c_ref, coef_ref, x_hi, m_lo, m_hi, *, strip):
    _, count, height, _ = c_ref.shape
    sent = height - x_hi.shape[1]
    for slot in range(2):
        cut = ([sent, x_hi.shape[1]], rows_in((m_lo, m_hi)))[slot]
        for first, size in strips(height, strip, cut):
            if slot == 0 and first < sent:
                continue
            here = pl.ds(first, size)
            coefs = [coef_ref[slot, k, here, :] for k in range(5)]
            to, at = pick((m_lo, m_hi), first) if slot else (x_hi, first - sent)
            for t in range(count):
                c = c_ref[slot, t, here, :]
                if first + size < height:
                    above = c_ref[slot, t, pl.ds(first + 1, size), :]
                else:
                    above = north_of(c)
                under = c_ref[slot, t, pl.ds(first - 1, size), :] if first else south_of(c)
                to[t, pl.ds(at, size), :] = weighed(coefs, c, above, under)


def closed_advection(c, coefs, cuts, strip=16):
    _, count, _, width = c.shape
    return pl.pallas_call(
        partial(closed_kernel, strip=strip),
        in_specs=[VM] * 2,
        out_specs=[VM] * 3,
        out_shape=[kept((count, rows, width)) for rows in cuts],
        compiler_params=small,
        name="closed",
    )(*near_core(c, coefs))


def faces_kernel(
    fields_ref, north_ref, south_ref, sides_ref, from_north_ref, from_south_ref,
    from_west_ref, from_east_ref, packet_ref, x_fix_ref, m_fix_ref, rest_ref, *, levels, count,
):
    height, width = fields_ref.shape[1:]
    x, txs = lax.axis_index("tx"), lax.axis_size("tx")
    half_rows = sides_ref.shape[0] // 2
    us, vs, ds, ws = 2 * count, 2 * count + 2, 2 * count + 4, 2 * count + 5
    east, west = (pl.ds(0, half_rows, stride=2), pl.ds(1, half_rows, stride=2))
    own = (north_ref[...], south_ref[...], sides_ref[west, :], sides_ref[east, :])
    halo = (from_north_ref[...], from_south_ref[...], from_west_ref[east, :], from_east_ref[west, :])
    known = (1.0, 1.0, as_f32(x > 0), as_f32(x < txs - 1))

    def side(k, slot):
        mine, theirs = own[k], halo[k]
        outgoing = k in (0, 3)
        speed = (mine if outgoing else theirs)[(vs if k < 2 else us) + slot:][:1]
        d_mine, d_theirs = mine[ds:ds + 1], theirs[ds:ds + 1]
        opened = mine[ws:ws + 1] * (theirs[ws:ws + 1] * known[k])
        flow = speed * (0.5 * (d_mine + d_theirs) * opened) / levels
        c_mine = mine[slot * count:(slot + 1) * count]
        c_theirs = theirs[slot * count:(slot + 1) * count]
        scale = advect_rate * levels / d_mine
        if outgoing:
            return -scale * (jnp.maximum(flow, 0.0) * c_mine + jnp.minimum(flow, 0.0) * c_theirs), flow
        return scale * (jnp.maximum(flow, 0.0) * c_theirs + jnp.minimum(flow, 0.0) * c_mine), -flow

    flows = [0.0, 0.0, 0.0, 0.0]
    for slot in range(2):
        ref = (x_fix_ref, m_fix_ref)[slot]
        for k in range(4):
            fix, flow = side(k, slot)
            flows[k] = flows[k] + flow
            if k < 2:
                ref[pl.ds(k * count, count), :] = fix
            else:
                ref[pl.ds(2 * count + 3 - k, count, stride=2), :] = fix
    lane, row = lanes_of((height, width)), rows_of((height, width))
    spill = jnp.concatenate([flows[3], flows[2], jnp.zeros((width - 2, height), f32)], 0).T
    spill = east_of(spill)
    spill = jnp.where((lane == 0) | (lane == width - 1), spill, 0.0)
    spill = spill + jnp.where(row == 0, flows[1], 0.0) + jnp.where(row == height - 1, flows[0], 0.0)
    packet_ref[pl.ds(0, height), :] = fields_ref[0] + fields_ref[1] + spill
    packet_ref[pl.ds(height, height), :] = fields_ref[2] + fields_ref[3]
    packet_ref[pl.ds(2 * height, 3 * count), :] = x_fix_ref[pl.ds(count, 3 * count), :]
    rest_ref[pl.ds(0, count), :] = m_fix_ref[pl.ds(0, count), :]
    rest_ref[pl.ds(count, 2 * count), :] = m_fix_ref[pl.ds(2 * count, 2 * count), :]


def face_corrections(fields, north, south, sides, halos, levels, count):
    height, width = fields.shape[1:]
    return pl.pallas_call(
        partial(faces_kernel, levels=levels, count=count),
        in_specs=[VM] * 8,
        out_specs=[VM] * 4,
        out_shape=[
            kept((2 * height + 3 * count, width)), kept((4 * count, width)),
            kept((4 * count, width)), kept((3 * count, width)),
        ],
        compiler_params=small,
        name="faces",
    )(*near_core(fields, north, south, sides, *halos))


def turned_columns(rows):
    return jnp.concatenate([rows, jnp.zeros((rows.shape[1] - rows.shape[0], rows.shape[1]), f32)], 0).T


def mend_kernel(x_fix, m_fix, *rest, strip):
    ins, outs, turned_ref = rest[:4], rest[4:8], rest[8]
    height, width = turned_ref.shape[1:]
    count = ins[0].shape[0]
    for slot, fix in enumerate((x_fix, m_fix)):
        turned_ref[slot] = turned_columns(fix[pl.ds(2 * count, 2 * count), :])
        base = 0
        some = slice(2, 4) if slot else slice(0, 2)
        for source, target in zip(ins[some], outs[some]):
            for first, size in strips(source.shape[1], strip):
                here = pl.ds(first, size)
                lane, row = lanes_of((size, width)), rows_of((size, width))
                rim = (lane == 0) | (lane == width - 1)
                columns = turned_ref[slot, pl.ds(base + first, size), :]
                for t in range(count):
                    value = source[t, here, :]
                    value = value + jnp.where(rim, pltpu.roll(columns, width - 1 - 2 * t, 1), 0.0)
                    if base + first == 0:
                        value = value + jnp.where(row == 0, fix[pl.ds(count + t, 1), :], 0.0)
                    if base + first + size == height:
                        value = value + jnp.where(row == size - 1, fix[pl.ds(t, 1), :], 0.0)
                    target[t, here, :] = value
            base += source.shape[1]


def mend(x_fix, m_fix, *parts, strip=16):
    height = sum(rows_in(parts[:2]))
    return pl.pallas_call(
        partial(mend_kernel, strip=strip),
        in_specs=[VM] * 6,
        out_specs=[VM] * 4,
        out_shape=[kept(p.shape) for p in parts],
        input_output_aliases={3: 1, 4: 2},
        scratch_shapes=[pltpu.VMEM((2, height, x_fix.shape[1]), f32)],
        compiler_params=small,
        name="mend",
    )(*near_core(x_fix, m_fix, *parts))


def pair_kernel(a_ref, b_ref, out_ref):
    rows = pl.ds(0, out_ref.shape[0])
    out_ref[...] = a_ref[rows, :] + b_ref[rows, :]


def pair_sum(packet, near, rows):
    return pl.pallas_call(
        pair_kernel, in_specs=[VM] * 2, out_specs=VM,
        out_shape=kept((rows, packet.shape[1])), compiler_params=small, name="pair",
    )(*near_core(packet, near))


def relay_kernel(fix_ref, handed_ref, out_ref, turned_ref, *, strip):
    count, span, width = out_ref.shape
    height = turned_ref.shape[0]
    turned_ref[...] = turned_columns(fix_ref[pl.ds(count, 2 * count), :])
    for first in range(0, span, strip):
        here = pl.ds(first, strip)
        columns = turned_ref[pl.ds(height - span + first, strip), :]
        lane, row = lanes_of((strip, width)), rows_of((strip, width))
        rim = (lane == 0) | (lane == width - 1)
        for t in range(count):
            value = handed_ref[t, here, :]
            value = value + jnp.where(rim, pltpu.roll(columns, width - 1 - 2 * t, 1), 0.0)
            if first + strip == span:
                value = value + jnp.where(row == strip - 1, fix_ref[pl.ds(t, 1), :], 0.0)
            out_ref[t, here, :] = value


def mend_handed(fix, handed, strip=16):
    return pl.pallas_call(
        partial(relay_kernel, strip=strip), in_specs=[VM] * 2, out_specs=VM,
        out_shape=kept(handed.shape), input_output_aliases={1: 0},
        scratch_shapes=[pltpu.VMEM((fix.shape[1], fix.shape[1]), f32)],
        compiler_params=small, name="relay",
    )(*near_core(fix, handed))


def surface_kernel(
    packet_ref, near_ref, far_ref, fields_ref, surface_ref, depth_ref, wet_ref,
    surface_out, pressure_out, south_out, west_out, *, levels,
):
    g, _, at_level = places()
    height, width = surface_ref.shape
    top, below = pl.ds(0, height), pl.ds(height, height)
    near_above, far_above = as_f32(g % 2 == 1), as_f32(g >= 2)
    total = packet_ref[top, :] + near_ref[top, :] + far_ref[top, :]
    surface = surface_ref[...] - eta_rate * wet_ref[...].astype(f32) * total
    above = near_above * near_ref[below, :] + far_above * far_ref[below, :]
    surface_out[...] = surface
    lane = lanes_of((height, width))
    turned = jnp.where(lane == 0, surface, 0.0)
    south_out[...] = jnp.zeros_like(south_out)
    keep(south_out, pl.ds(0, 1), surface[:1])
    for slot in range(2):
        lower = as_f32(at_level[slot] == 1)
        density = fields_ref[2 + slot]
        column = above + lower * fields_ref[3 - slot] + density - 0.5 * density
        pressure = baroclinic_rate * depth_ref[...] * column / levels
        pressure_out[slot] = pressure
        keep(south_out, pl.ds(1 + slot, 1), pressure[:1])
        turned = jnp.where(lane == 1 + slot, pltpu.roll(pressure, 1 + slot, 1), turned)
    west_out[...] = turned.T[:SUB]


def new_surface_and_pressure(packet, near, far, fields, surface, depth, wet_mask, levels):
    height, width = surface.shape
    args = (packet, near, far, fields, surface, depth, wet_mask)
    outs = [(height, width), (2, height, width), (SUB, width), (SUB, height)]
    return pl.pallas_call(
        partial(surface_kernel, levels=levels),
        in_specs=[VM] * len(args), out_specs=[VM] * len(outs),
        out_shape=[kept(s) for s in outs],
        compiler_params=small,
        name="level",
    )(*near_core(*args))


def momentum_kernel(
    u_ref, v_ref, depth_ref, wet_ref, surface_ref, pressure_ref, from_north_ref,
    from_south_ref, from_west_ref, from_east_ref, north_state_ref, east_state_ref,
    east_out, north_out, surface_out, *, count,
):
    g, groups, at_level = places()
    x, txs = lax.axis_index("tx"), lax.axis_size("tx")
    height, width = depth_ref.shape
    lane, row = lanes_of((height, width)), rows_of((height, width))
    us = 2 * count
    half_rows = from_west_ref.shape[0] // 2
    known_w, known_e = as_f32(x > 0), as_f32(x < txs - 1)
    west_halo = from_west_ref[pl.ds(0, half_rows, stride=2), :][us:us + SUB] * known_w
    east_halo = from_east_ref[pl.ds(1, half_rows, stride=2), :][us:us + SUB] * known_e
    used = 3 * SUB
    columns = jnp.concatenate(
        [west_halo, east_halo, east_state_ref[...], jnp.zeros((width - used, height), f32)], 0
    ).T
    north_halo, south_halo = from_north_ref[...], from_south_ref[...]

    def shifted(field, q, state=None):
        e_from = SUB + q if state is None else 2 * SUB + state
        e = jnp.where(lane == width - 1, pltpu.roll(columns, width - 1 - e_from, 1), east_of(field))
        line = north_halo[us + q:us + q + 1] if state is None else north_state_ref[pl.ds(state, 1), :]
        n = jnp.where(row == height - 1, line, north_of(field))
        return e, n

    def whole(field, q):
        e, n = shifted(field, q)
        w = jnp.where(lane == 0, pltpu.roll(columns, (width - q) % width, 1), west_of(field))
        s = jnp.where(row == 0, south_halo[us + q:us + q + 1], south_of(field))
        return n + s + e + w - 4.0 * field

    wet = wet_ref[...].astype(f32)
    wet_e, wet_n = shifted(wet, 5)
    open_e, open_n = wet * wet_e, wet * wet_n
    surface = surface_ref[...]
    surface_out[...] = surface
    surface_e, surface_n = shifted(surface, 0, 0)
    for slot in range(2):
        at = at_level[slot]
        bottom = as_f32((g == groups - 1) & (at == 1))
        pressure = pressure_ref[slot]
        pressure_e, pressure_n = shifted(pressure, 0, 1 + slot)
        u, v = u_ref[at], v_ref[at]
        east_out[at] = open_e * (
            u - gravity_rate * (surface_e - surface) - (pressure_e - pressure)
            + viscous_rate * whole(u, slot) - friction_rate * bottom * u
        )
        north_out[at] = open_n * (
            v - gravity_rate * (surface_n - surface) - (pressure_n - pressure)
            + viscous_rate * whole(v, 2 + slot) - friction_rate * bottom * v
        )


def momentum(u, v, depth, wet_mask, surface, pressure, halos, states, count):
    args = (u, v, depth, wet_mask, surface, pressure, *halos, *states)
    return pl.pallas_call(
        partial(momentum_kernel, count=count),
        in_specs=[VM] * len(args), out_specs=[VM] * 3,
        out_shape=[jax.ShapeDtypeStruct(a.shape, f32) for a in (u, v, surface)],
        compiler_params=small,
        name="momentum",
    )(*near_core(*args))


def rates_kernel(cells_ref, loads_ref, kinetics_ref, wet_ref, out_ref, source_ref):
    g, _, _ = places()
    count, _, width = source_ref.shape
    size = count * SUB
    spread = (
        lax.broadcasted_iota(jnp.int32, (size, count), 0) // SUB
        == lax.broadcasted_iota(jnp.int32, (size, count), 1)
    ).astype(f32)
    full = jnp.dot(spread, kinetics_ref[...], precision=lax.Precision.HIGHEST)
    full = lax.dot_general(
        full, spread, (((1,), (1,)), ((), ())), precision=lax.Precision.HIGHEST
    )
    same = lax.broadcasted_iota(jnp.int32, (size, size), 0) % SUB
    same = same == lax.broadcasted_iota(jnp.int32, (size, size), 1) % SUB
    high, low = split(jnp.where(same, full, 0.0))
    out_ref[...] = jnp.concatenate([high, high, low], 1)
    source_ref[...] = jnp.zeros_like(source_ref)

    @pl.when(g == 0)
    def _():
        @pl.loop(0, cells_ref.shape[0])
        def _(r):
            at, spot = pl.ds(cells_ref[r] // width, 1), cells_ref[r] % width
            here = (lanes_of((1, width)) == spot) & (wet_ref[at, :] != 0)
            for t in range(count):
                source_ref[t, at, :] = source_ref[t, at, :] + jnp.where(here, loads_ref[r, t], 0.0)


def rates_and_source(cells, loads, kinetics, wet_mask):
    count = kinetics.shape[0]
    size = count * SUB
    return pl.pallas_call(
        rates_kernel, in_specs=[SM, SM, VM, VM], out_specs=[VM, VM],
        out_shape=[pltpu.VMEM((size, 3 * size), jnp.bfloat16), kept((count,) + wet_mask.shape)],
        compiler_params=small, name="rates",
    )(cells, loads, kinetics, *near_core(wet_mask))


def split(x):
    high = x.astype(jnp.bfloat16)
    return high, (x - high.astype(f32)).astype(jnp.bfloat16)


def mixing_rates(slot):
    g, groups, _ = places()
    has_next = 1.0 if slot == 0 else as_f32((g > 0) & (g < groups - 1))
    return 1.0 - mixing_rate - mixing_rate * has_next, mixing_rate * has_next


def mixed_rows(t, first, size, parts, keep_rate):
    (own, at), (other, there) = (pick(refs, first) for refs in parts)
    return keep_rate * own[t, pl.ds(at, size), :] + mixing_rate * other[t, pl.ds(there, size), :]


def ready_kernel(c_ref, wet_ref, *rest, sizes, strip):
    ready_ref = rest[-1]
    parts = [rest[:sizes[0]], rest[sizes[0]:sum(sizes)]]
    count, height, _ = ready_ref.shape
    keep_rate, _ = mixing_rates(1)
    for first, size in strips(height, strip, *(rows_in(refs) for refs in parts)):
        here = pl.ds(first, size)
        wet = wet_ref[here, :] != 0
        for t in range(count):
            value = mixed_rows(t, first, size, parts, keep_rate)
            ready_ref[t, here, :] = jnp.where(wet, value, c_ref[1, t, here, :])


def make_ready(c, wet_mask, own, other, strip=16):
    _, count, height, width = c.shape
    args = near_core(c, wet_mask, *own, *other)
    return pl.pallas_call(
        partial(ready_kernel, sizes=(len(own), len(other)), strip=strip),
        in_specs=[VM] * len(args),
        out_specs=VM,
        out_shape=kept((count, height, width)),
        compiler_params=small,
        name="ready",
    )(*args)


def react_kernel(wet_ref, rates_ref, *rest, slot, fixed, sizes, border, strip):
    out_hbm, done_ref, turned_ref, out_sem = rest[-4:]
    parts = [rest[sum(sizes[:k]):sum(sizes[:k + 1])] for k in range(len(sizes))]
    more = rest[sum(sizes):]
    _, _, at_level = places()
    count, height, width = done_ref.shape
    mixing = mixing_rates(slot)
    if slot == 0:
        turned_ref[...] = mixing[1] * turned_columns(more[1][pl.ds(fixed + count, 2 * count), :])
    rates = rates_ref[...]
    copies = []
    for first, size in strips(height, strip, *(rows_in(refs) for refs in parts)):
        here = pl.ds(first, size)
        groups_of = size // SUB
        beyond, at = pick(parts[0], first)
        wet = wet_ref[here, :] != 0
        passed = jnp.where(wet, mixing[1], 0.0)
        lane, row = lanes_of((size, width)), rows_of((size, width))
        rim = (lane == 0) | (lane == width - 1)
        values = []
        for t in range(count):
            far = beyond[t, pl.ds(at, size), :]
            if slot == 0:
                value = mixed_rows(t, first, size, parts[1:], mixing[0]) + mixing[1] * far
                if first < border:
                    columns = pltpu.roll(turned_ref[here, :], width - 1 - 2 * t, 1)
                    value = value + jnp.where(rim, columns, 0.0)
                if first == 0:
                    line = mixing[1] * more[1][pl.ds(fixed + t, 1), :]
                    value = value + jnp.where(row == 0, line, 0.0)
                values.append(jnp.where(wet, value, more[0][0, t, here, :]))
            else:
                values.append(more[0][t, here, :] + passed * far)
        stacked = jnp.concatenate(
            [
                jnp.concatenate([v[k * SUB:(k + 1) * SUB] for v in values], 0)
                for k in range(groups_of)
            ],
            1,
        )
        high, low = split(stacked)
        reaction = jnp.dot(
            rates, jnp.concatenate([high, low, high], 0), preferred_element_type=f32
        )
        warming = jnp.where(wet, jnp.exp(warming_rate * values[1]), 0.0)
        for t in range(count):
            gained = jnp.concatenate(
                [reaction[t * SUB:(t + 1) * SUB, k * width:(k + 1) * width] for k in range(groups_of)],
                0,
            )
            done = values[t] + warming * gained
            done_ref[t, here, :] = done if slot == 0 else done + more[1][t, here, :]
        copies.append(pltpu.make_async_copy(
            done_ref.at[:, here], out_hbm.at[:, at_level[slot], here], out_sem.at[len(copies)]
        ))
        copies[-1].start()
    for copy in copies:
        copy.wait()


def react(shape, wet_mask, rates, slot, received, more, mixed=(), into=None, fixed=0, border=0,
          strip=16):
    count, _, height, width = shape
    sizes = tuple(len(part) for part in (received, *mixed))
    flat = [a for part in (received, *mixed) for a in part]
    args = near_core(wet_mask, rates, *flat, *more)
    specs = [VM] * len(args)
    aliases = {}
    if into is not None:
        aliases = {len(args): 0}
        args.append(into)
        specs.append(HB)
    return pl.pallas_call(
        partial(react_kernel, slot=slot, strip=strip, fixed=fixed, sizes=sizes, border=border),
        in_specs=specs,
        out_specs=HB,
        scratch_shapes=[
            pltpu.VMEM((count, height, width), f32), pltpu.VMEM((height, width), f32),
            pltpu.SemaphoreType.DMA((height // SUB,)),
        ],
        out_shape=jax.ShapeDtypeStruct(shape, f32),
        input_output_aliases=aliases,
        compiler_params=small,
        name="react",
    )(*args)


def shards(tracers, u, v, surface, depth, wet_mask, river_cells, river_loads, kinetics):
    count, own_levels, height, _ = tracers.shape
    groups, tys, txs = (lax.axis_size(a) for a in ("grp", "ty", "tx"))
    levels = own_levels * groups
    assert own_levels == 2 and groups in (2, 4)
    direct, border = height // 2, 5 * height // 8
    cuts = (height - border, direct, height - direct)
    cell_args = (tracers, u, v, depth, wet_mask, levels)

    swap = [(i, i ^ 1) for i in range(groups)]
    middle = [(i, i + 1) for i in range(1, groups - 1, 2)]
    middle = middle + [(b, a) for a, b in middle]
    early = early_advection(*cell_args, border)
    near_x_lo = lax.ppermute(early, "grp", swap)
    c, coefs, fields, north, south, sides = tile_edges(*cell_args)

    up = [(i, i + 1) for i in range(tys - 1)]
    down = [(i + 1, i) for i in range(tys - 1)]
    from_south = lax.ppermute(north, "ty", up)
    from_north = lax.ppermute(south, "ty", down)
    if txs == 2:
        from_west = from_east = lax.ppermute(sides, "tx", [(0, 1), (1, 0)])
    else:
        from_west = lax.ppermute(sides, "tx", [(i, i + 1) for i in range(txs - 1)])
        from_east = lax.ppermute(sides, "tx", [(i + 1, i) for i in range(txs - 1)])
    x_hi, *m = closed_advection(c, coefs, cuts)
    rates, source = rates_and_source(river_cells, river_loads, kinetics, wet_mask)
    halos = (from_north, from_south, from_west, from_east)
    packet, x_fix, m_fix, rest = face_corrections(fields, north, south, sides, halos, levels, count)
    near = lax.ppermute(packet, "grp", swap)
    *x, m_0, m_1 = mend(x_fix, m_fix, early, x_hi, *m)
    near_x_hi = lax.ppermute(x[1], "grp", swap)
    near_m = [lax.ppermute(m_0, "grp", middle)]
    if groups == 4:
        handed = lax.ppermute(m[1], "grp", [(1, 3), (2, 0)])
        handed = mend_handed(lax.ppermute(rest, "grp", [(1, 3), (2, 0)]), handed)
        near_m.append(lax.ppermute(handed, "grp", [(3, 2), (0, 1)]))
    else:
        near_m.append(lax.ppermute(m_1, "grp", middle))

    columns = pair_sum(packet, near, 2 * height)
    if groups == 4:
        far = lax.ppermute(columns, "grp", [(i, i ^ 2) for i in range(groups)])
    else:
        far = jnp.zeros_like(columns)
    new_surface, pressure, south_state, west_state = new_surface_and_pressure(
        packet, near, far, fields, surface, depth, wet_mask, levels
    )
    north_state = lax.ppermute(south_state, "ty", down)
    east_state = lax.ppermute(west_state, "tx", [(i + 1, i) for i in range(txs - 1)])
    new_east, new_north, new_surface = momentum(
        u, v, depth, wet_mask, new_surface, pressure, halos, (north_state, east_state), count
    )

    mixed = (m_0, m_1)
    out = react(
        tracers.shape, wet_mask, rates, 0, (near_x_lo, near_x_hi), (c, near),
        (x, mixed), fixed=2 * height, border=border,
    )
    ready = make_ready(c, wet_mask, mixed, x)
    out = react(tracers.shape, wet_mask, rates, 1, near_m, (ready, source), into=out)
    return (out, new_east, new_north, new_surface)


def solution(mesh):
    field = P("grp", "ty", "tx")
    plane = P("ty", "tx")
    return jax.shard_map(
        shards,
        mesh=mesh,
        in_specs=(
            P(None, "grp", "ty", "tx"), field, field, plane, plane, plane,
            P(("ty", "tx")), P(("ty", "tx"), None), P(),
        ),
        out_specs=(P(None, "grp", "ty", "tx"), field, field, plane),
        check_vma=False,
    )
```

```python
from functools import partial

import jax
import jax.numpy as jnp
from jax import lax
from jax.experimental import pallas as pl
from jax.experimental.pallas import tpu as pltpu
from jax.sharding import PartitionSpec as P


eta_rate = 0.25
gravity_rate = 0.25
baroclinic_rate = 0.4
viscous_rate = 0.1
friction_rate = 0.3
advect_rate = 0.3
mixing_rate = 0.2
haline_coef = 0.8
thermal_coef = 0.2
warming_rate = 0.46

f32 = jnp.float32
SUB = 8


def lanes_of(shape):
    return lax.broadcasted_iota(jnp.int32, shape, len(shape) - 1)


def rows_of(shape):
    return lax.broadcasted_iota(jnp.int32, shape, len(shape) - 2)


def east_of(x):
    return pltpu.roll(x, x.shape[-1] - 1, x.ndim - 1)


def west_of(x):
    return pltpu.roll(x, 1, x.ndim - 1)


def north_of(x):
    return pltpu.roll(x, x.shape[-2] - 1, x.ndim - 2)


def south_of(x):
    return pltpu.roll(x, 1, x.ndim - 2)


def keep(ref, rows, value):
    ref[rows, :] = value


VM = pl.BlockSpec(memory_space=pltpu.VMEM)


small = pltpu.CompilerParams(vmem_limit_bytes=16 << 20)


def near_core(*arrays):
    return [pltpu.with_memory_space_constraint(a, pltpu.VMEM) for a in arrays]


def far_core(*arrays):
    return [pltpu.with_memory_space_constraint(a, pltpu.HBM) for a in arrays]


def kept(shape):
    return pltpu.VMEM(shape, f32)


SM = pl.BlockSpec(memory_space=pltpu.SMEM)
HB = pl.BlockSpec(memory_space=pl.ANY)


def places():
    g, groups = lax.axis_index("grp"), lax.axis_size("grp")
    return g, groups, (1 - g % 2, g % 2)


def as_f32(flag):
    return jnp.where(flag, 1.0, 0.0).astype(f32)


def pick(refs, row):
    for ref in refs:
        if row < ref.shape[1]:
            return ref, row
        row -= ref.shape[1]


def strips(height, strip, *parts):
    ends = {height}
    for part in parts:
        ends |= {sum(part[:k + 1]) for k in range(len(part))}
    first = 0
    while first < height:
        size = min(strip, min(e for e in ends if e > first) - first)
        yield first, size
        first += size


def rows_in(parts):
    return [p.shape[1] for p in parts]


def weights(coef_ref, u, v, depth, wet, levels):
    height, width = depth.shape
    lane, row = lanes_of((height, width)), rows_of((height, width))
    half_e = 0.5 * (depth + east_of(depth)) * (wet * east_of(wet))
    half_n = 0.5 * (depth + north_of(depth)) * (wet * north_of(wet))
    flow_e = jnp.where(lane < width - 1, u * half_e / levels, 0.0)
    flow_n = jnp.where(row < height - 1, v * half_n / levels, 0.0)
    flow_w, flow_s = west_of(flow_e), south_of(flow_n)
    scale = advect_rate * levels / depth
    coef_ref[0] = 1.0 - scale * (
        jnp.maximum(flow_e, 0.0) - jnp.minimum(flow_w, 0.0)
        + jnp.maximum(flow_n, 0.0) - jnp.minimum(flow_s, 0.0)
    )
    coef_ref[1] = -scale * jnp.minimum(flow_e, 0.0)
    coef_ref[2] = scale * jnp.maximum(flow_w, 0.0)
    coef_ref[3] = -scale * jnp.minimum(flow_n, 0.0)
    coef_ref[4] = scale * jnp.maximum(flow_s, 0.0)
    return flow_e - flow_w + flow_n - flow_s


def weighed(coefs, c, above, under):
    return (
        coefs[0] * c + coefs[1] * east_of(c) + coefs[2] * west_of(c)
        + coefs[3] * above + coefs[4] * under
    )


def early_kernel(
    c_hbm, u_hbm, v_hbm, depth_hbm, wet_hbm, out_ref,
    c_ref, u_ref, v_ref, depth_ref, wet_ref, coef_ref, flat_sem, c_sem, *, levels, strip,
):
    _, _, at_level = places()
    count, taken, _ = c_ref.shape
    at, rows = at_level[0], pl.ds(0, taken)
    flat = [
        pltpu.make_async_copy(h, r, flat_sem.at[k])
        for k, (h, r) in enumerate((
            (depth_hbm.at[rows], depth_ref), (wet_hbm.at[rows], wet_ref),
            (u_hbm.at[at, rows], u_ref), (v_hbm.at[at, rows], v_ref),
        ))
    ]
    bulk = pltpu.make_async_copy(c_hbm.at[:, at, rows], c_ref, c_sem)
    for copy in flat:
        copy.start()
    bulk.start()
    for copy in flat:
        copy.wait()
    weights(coef_ref, u_ref[...], v_ref[...], depth_ref[...], wet_ref[...].astype(f32), levels)
    bulk.wait()
    for first in range(0, out_ref.shape[1], strip):
        here = pl.ds(first, strip)
        coefs = [coef_ref[k, here, :] for k in range(5)]
        for t in range(count):
            c = c_ref[t, here, :]
            above = c_ref[t, pl.ds(first + 1, strip), :]
            under = c_ref[t, pl.ds(first - 1, strip), :] if first else south_of(c)
            out_ref[t, here, :] = weighed(coefs, c, above, under)


def early_advection(tracers, u, v, depth, wet_mask, levels, rows, strip=8):
    count, _, _, width = tracers.shape
    taken = rows + SUB
    plane = pltpu.VMEM((taken, width), f32)
    return pl.pallas_call(
        partial(early_kernel, levels=levels, strip=strip),
        in_specs=[HB] * 5,
        out_specs=VM,
        out_shape=kept((count, rows, width)),
        scratch_shapes=[
            pltpu.VMEM((count, taken, width), f32), plane, plane, plane,
            pltpu.VMEM((taken, width), jnp.int32), pltpu.VMEM((5, taken, width), f32),
            pltpu.SemaphoreType.DMA((4,)), pltpu.SemaphoreType.DMA,
        ],
        compiler_params=small,
        name="early",
    )(*far_core(tracers, u, v, depth, wet_mask))


def edges_kernel(
    c_hbm, u_hbm, v_hbm, depth_hbm, wet_hbm,
    c_ref, coef_ref, fields_ref, north_ref, south_ref, sides_ref,
    u_ref, v_ref, depth_ref, wet_ref, turned_ref, flat_sem, c_sem, *, levels, count, parts, strip,
):
    _, _, at_level = places()
    height, width = depth_ref.shape
    chunk = count // parts
    flat = [
        pltpu.make_async_copy(h, r, flat_sem.at[k])
        for k, (h, r) in enumerate(
            ((depth_hbm, depth_ref), (wet_hbm, wet_ref), (u_hbm, u_ref), (v_hbm, v_ref))
        )
    ]
    for copy in flat:
        copy.start()
    bulk = []
    for slot in range(2):
        for part in range(parts):
            some = pl.ds(part * chunk, chunk)
            bulk.append(pltpu.make_async_copy(
                c_hbm.at[some, at_level[slot]], c_ref.at[slot, some], c_sem.at[slot, part]
            ))
            bulk[-1].start()
    north_ref[...] = jnp.zeros_like(north_ref)
    south_ref[...] = jnp.zeros_like(south_ref)
    for copy in flat:
        copy.wait()
    depth, wet = depth_ref[...], wet_ref[...].astype(f32)

    def lines(field, q):
        keep(north_ref, pl.ds(q, 1), field[height - 1:])
        keep(south_ref, pl.ds(q, 1), field[:1])

    def gather(got, field, q):
        mask = lanes_of((1, width)) // 2 == q
        return jnp.where(mask, pltpu.roll(field, (2 * q + 1) % width, 1), got)

    turned = jnp.zeros((height, width), f32)
    for q, field in ((4, depth), (5, wet)):
        lines(field, 2 * count + q)
        turned = gather(turned, field, 2 * count + q)
    for slot in range(2):
        u, v = u_ref[at_level[slot]], v_ref[at_level[slot]]
        lines(u, 2 * count + slot)
        lines(v, 2 * count + 2 + slot)
        turned = gather(turned, u, 2 * count + slot)
        turned = gather(turned, v, 2 * count + 2 + slot)
        fields_ref[slot] = weights(coef_ref.at[slot], u, v, depth, wet, levels)
    turned_ref[...] = turned

    for slot in range(2):
        for part in range(parts):
            bulk[slot * parts + part].wait()
            if part == 0:
                fields_ref[2 + slot] = haline_coef * c_ref[slot, 0] - thermal_coef * c_ref[slot, 1]
            some = range(part * chunk, (part + 1) * chunk)
            for t in some:
                keep(south_ref, pl.ds(slot * count + t, 1), c_ref[slot, t, pl.ds(0, 1), :])
                keep(north_ref, pl.ds(slot * count + t, 1), c_ref[slot, t, pl.ds(height - 1, 1), :])
            for first in range(0, height, strip):
                here = pl.ds(first, strip)
                got = turned_ref[here, :]
                for t in some:
                    got = gather(got, c_ref[slot, t, here, :], slot * count + t)
                turned_ref[here, :] = got
    sides_ref[...] = turned_ref[...].T[: sides_ref.shape[0]]


def tile_edges(tracers, u, v, depth, wet_mask, levels, parts=2, strip=32):
    count, _, height, width = tracers.shape
    edge_rows = -(-(2 * count + 6) // SUB) * SUB
    assert width == height and 2 * edge_rows <= width
    outs = [
        kept((2, count, height, width)), kept((2, 5, height, width)), kept((4, height, width)),
        kept((edge_rows, width)), kept((edge_rows, width)), kept((2 * edge_rows, height)),
    ]
    plane = pltpu.VMEM((height, width), f32)
    return pl.pallas_call(
        partial(edges_kernel, levels=levels, count=count, parts=parts, strip=strip),
        in_specs=[HB] * 5,
        out_specs=[VM] * len(outs),
        out_shape=outs,
        scratch_shapes=[
            pltpu.VMEM(u.shape, f32), pltpu.VMEM(v.shape, f32), plane,
            pltpu.VMEM((height, width), jnp.int32), plane,
            pltpu.SemaphoreType.DMA((4,)), pltpu.SemaphoreType.DMA((2, parts)),
        ],
        compiler_params=small,
        name="edges",
    )(*far_core(tracers, u, v, depth, wet_mask))


def closed_kernel(c_ref, coef_ref, x_hi, m_lo, m_hi, *, strip):
    _, count, height, _ = c_ref.shape
    sent = height - x_hi.shape[1]
    for slot in range(2):
        cut = ([sent, x_hi.shape[1]], rows_in((m_lo, m_hi)))[slot]
        for first, size in strips(height, strip, cut):
            if slot == 0 and first < sent:
                continue
            here = pl.ds(first, size)
            coefs = [coef_ref[slot, k, here, :] for k in range(5)]
            to, at = pick((m_lo, m_hi), first) if slot else (x_hi, first - sent)
            for t in range(count):
                c = c_ref[slot, t, here, :]
                if first + size < height:
                    above = c_ref[slot, t, pl.ds(first + 1, size), :]
                else:
                    above = north_of(c)
                under = c_ref[slot, t, pl.ds(first - 1, size), :] if first else south_of(c)
                to[t, pl.ds(at, size), :] = weighed(coefs, c, above, under)


def closed_advection(c, coefs, cuts, strip=16):
    _, count, _, width = c.shape
    return pl.pallas_call(
        partial(closed_kernel, strip=strip),
        in_specs=[VM] * 2,
        out_specs=[VM] * 3,
        out_shape=[kept((count, rows, width)) for rows in cuts],
        compiler_params=small,
        name="closed",
    )(*near_core(c, coefs))


def faces_kernel(
    fields_ref, north_ref, south_ref, sides_ref, from_north_ref, from_south_ref,
    from_west_ref, from_east_ref, packet_ref, x_fix_ref, m_fix_ref, rest_ref, *, levels, count,
):
    height, width = fields_ref.shape[1:]
    x, txs = lax.axis_index("tx"), lax.axis_size("tx")
    half_rows = sides_ref.shape[0] // 2
    us, vs, ds, ws = 2 * count, 2 * count + 2, 2 * count + 4, 2 * count + 5
    east, west = (pl.ds(0, half_rows, stride=2), pl.ds(1, half_rows, stride=2))
    own = (north_ref[...], south_ref[...], sides_ref[west, :], sides_ref[east, :])
    halo = (from_north_ref[...], from_south_ref[...], from_west_ref[east, :], from_east_ref[west, :])
    known = (1.0, 1.0, as_f32(x > 0), as_f32(x < txs - 1))

    def side(k, slot):
        mine, theirs = own[k], halo[k]
        outgoing = k in (0, 3)
        speed = (mine if outgoing else theirs)[(vs if k < 2 else us) + slot:][:1]
        d_mine, d_theirs = mine[ds:ds + 1], theirs[ds:ds + 1]
        opened = mine[ws:ws + 1] * (theirs[ws:ws + 1] * known[k])
        flow = speed * (0.5 * (d_mine + d_theirs) * opened) / levels
        c_mine = mine[slot * count:(slot + 1) * count]
        c_theirs = theirs[slot * count:(slot + 1) * count]
        scale = advect_rate * levels / d_mine
        if outgoing:
            return -scale * (jnp.maximum(flow, 0.0) * c_mine + jnp.minimum(flow, 0.0) * c_theirs), flow
        return scale * (jnp.maximum(flow, 0.0) * c_theirs + jnp.minimum(flow, 0.0) * c_mine), -flow

    flows = [0.0, 0.0, 0.0, 0.0]
    for slot in range(2):
        ref = (x_fix_ref, m_fix_ref)[slot]
        for k in range(4):
            fix, flow = side(k, slot)
            flows[k] = flows[k] + flow
            if k < 2:
                ref[pl.ds(k * count, count), :] = fix
            else:
                ref[pl.ds(2 * count + 3 - k, count, stride=2), :] = fix
    lane, row = lanes_of((height, width)), rows_of((height, width))
    spill = jnp.concatenate([flows[3], flows[2], jnp.zeros((width - 2, height), f32)], 0).T
    spill = east_of(spill)
    spill = jnp.where((lane == 0) | (lane == width - 1), spill, 0.0)
    spill = spill + jnp.where(row == 0, flows[1], 0.0) + jnp.where(row == height - 1, flows[0], 0.0)
    packet_ref[pl.ds(0, height), :] = fields_ref[0] + fields_ref[1] + spill
    packet_ref[pl.ds(height, height), :] = fields_ref[2] + fields_ref[3]
    packet_ref[pl.ds(2 * height, 3 * count), :] = x_fix_ref[pl.ds(count, 3 * count), :]
    rest_ref[pl.ds(0, count), :] = m_fix_ref[pl.ds(0, count), :]
    rest_ref[pl.ds(count, 2 * count), :] = m_fix_ref[pl.ds(2 * count, 2 * count), :]


def face_corrections(fields, north, south, sides, halos, levels, count):
    height, width = fields.shape[1:]
    return pl.pallas_call(
        partial(faces_kernel, levels=levels, count=count),
        in_specs=[VM] * 8,
        out_specs=[VM] * 4,
        out_shape=[
            kept((2 * height + 3 * count, width)), kept((4 * count, width)),
            kept((4 * count, width)), kept((3 * count, width)),
        ],
        compiler_params=small,
        name="faces",
    )(*near_core(fields, north, south, sides, *halos))


def turned_columns(rows):
    return jnp.concatenate([rows, jnp.zeros((rows.shape[1] - rows.shape[0], rows.shape[1]), f32)], 0).T


def mend_kernel(x_fix, m_fix, *rest, strip):
    ins, outs, turned_ref = rest[:4], rest[4:8], rest[8]
    height, width = turned_ref.shape[1:]
    count = ins[0].shape[0]
    for slot, fix in enumerate((x_fix, m_fix)):
        turned_ref[slot] = turned_columns(fix[pl.ds(2 * count, 2 * count), :])
        base = 0
        some = slice(2, 4) if slot else slice(0, 2)
        for source, target in zip(ins[some], outs[some]):
            for first, size in strips(source.shape[1], strip):
                here = pl.ds(first, size)
                lane, row = lanes_of((size, width)), rows_of((size, width))
                rim = (lane == 0) | (lane == width - 1)
                columns = turned_ref[slot, pl.ds(base + first, size), :]
                for t in range(count):
                    value = source[t, here, :]
                    value = value + jnp.where(rim, pltpu.roll(columns, width - 1 - 2 * t, 1), 0.0)
                    if base + first == 0:
                        value = value + jnp.where(row == 0, fix[pl.ds(count + t, 1), :], 0.0)
                    if base + first + size == height:
                        value = value + jnp.where(row == size - 1, fix[pl.ds(t, 1), :], 0.0)
                    target[t, here, :] = value
            base += source.shape[1]


def mend(x_fix, m_fix, *parts, strip=16):
    height = sum(rows_in(parts[:2]))
    return pl.pallas_call(
        partial(mend_kernel, strip=strip),
        in_specs=[VM] * 6,
        out_specs=[VM] * 4,
        out_shape=[kept(p.shape) for p in parts],
        input_output_aliases={3: 1, 4: 2},
        scratch_shapes=[pltpu.VMEM((2, height, x_fix.shape[1]), f32)],
        compiler_params=small,
        name="mend",
    )(*near_core(x_fix, m_fix, *parts))


def pair_kernel(a_ref, b_ref, out_ref):
    rows = pl.ds(0, out_ref.shape[0])
    out_ref[...] = a_ref[rows, :] + b_ref[rows, :]


def pair_sum(packet, near, rows):
    return pl.pallas_call(
        pair_kernel, in_specs=[VM] * 2, out_specs=VM,
        out_shape=kept((rows, packet.shape[1])), compiler_params=small, name="pair",
    )(*near_core(packet, near))


def relay_kernel(fix_ref, handed_ref, out_ref, turned_ref, *, strip):
    count, span, width = out_ref.shape
    height = turned_ref.shape[0]
    turned_ref[...] = turned_columns(fix_ref[pl.ds(count, 2 * count), :])
    for first in range(0, span, strip):
        here = pl.ds(first, strip)
        columns = turned_ref[pl.ds(height - span + first, strip), :]
        lane, row = lanes_of((strip, width)), rows_of((strip, width))
        rim = (lane == 0) | (lane == width - 1)
        for t in range(count):
            value = handed_ref[t, here, :]
            value = value + jnp.where(rim, pltpu.roll(columns, width - 1 - 2 * t, 1), 0.0)
            if first + strip == span:
                value = value + jnp.where(row == strip - 1, fix_ref[pl.ds(t, 1), :], 0.0)
            out_ref[t, here, :] = value


def mend_handed(fix, handed, strip=16):
    return pl.pallas_call(
        partial(relay_kernel, strip=strip), in_specs=[VM] * 2, out_specs=VM,
        out_shape=kept(handed.shape), input_output_aliases={1: 0},
        scratch_shapes=[pltpu.VMEM((fix.shape[1], fix.shape[1]), f32)],
        compiler_params=small, name="relay",
    )(*near_core(fix, handed))


def surface_kernel(
    packet_ref, near_ref, far_ref, fields_ref, surface_ref, depth_ref, wet_ref,
    surface_out, pressure_out, south_out, west_out, *, levels,
):
    g, _, at_level = places()
    height, width = surface_ref.shape
    top, below = pl.ds(0, height), pl.ds(height, height)
    near_above, far_above = as_f32(g % 2 == 1), as_f32(g >= 2)
    total = packet_ref[top, :] + near_ref[top, :] + far_ref[top, :]
    surface = surface_ref[...] - eta_rate * wet_ref[...].astype(f32) * total
    above = near_above * near_ref[below, :] + far_above * far_ref[below, :]
    surface_out[...] = surface
    lane = lanes_of((height, width))
    turned = jnp.where(lane == 0, surface, 0.0)
    south_out[...] = jnp.zeros_like(south_out)
    keep(south_out, pl.ds(0, 1), surface[:1])
    for slot in range(2):
        lower = as_f32(at_level[slot] == 1)
        density = fields_ref[2 + slot]
        column = above + lower * fields_ref[3 - slot] + density - 0.5 * density
        pressure = baroclinic_rate * depth_ref[...] * column / levels
        pressure_out[slot] = pressure
        keep(south_out, pl.ds(1 + slot, 1), pressure[:1])
        turned = jnp.where(lane == 1 + slot, pltpu.roll(pressure, 1 + slot, 1), turned)
    west_out[...] = turned.T[:SUB]


def new_surface_and_pressure(packet, near, far, fields, surface, depth, wet_mask, levels):
    height, width = surface.shape
    args = (packet, near, far, fields, surface, depth, wet_mask)
    outs = [(height, width), (2, height, width), (SUB, width), (SUB, height)]
    return pl.pallas_call(
        partial(surface_kernel, levels=levels),
        in_specs=[VM] * len(args), out_specs=[VM] * len(outs),
        out_shape=[kept(s) for s in outs],
        compiler_params=small,
        name="level",
    )(*near_core(*args))


def momentum_kernel(
    u_ref, v_ref, depth_ref, wet_ref, surface_ref, pressure_ref, from_north_ref,
    from_south_ref, from_west_ref, from_east_ref, north_state_ref, east_state_ref,
    east_out, north_out, surface_out, *, count,
):
    g, groups, at_level = places()
    x, txs = lax.axis_index("tx"), lax.axis_size("tx")
    height, width = depth_ref.shape
    lane, row = lanes_of((height, width)), rows_of((height, width))
    us = 2 * count
    half_rows = from_west_ref.shape[0] // 2
    known_w, known_e = as_f32(x > 0), as_f32(x < txs - 1)
    west_halo = from_west_ref[pl.ds(0, half_rows, stride=2), :][us:us + SUB] * known_w
    east_halo = from_east_ref[pl.ds(1, half_rows, stride=2), :][us:us + SUB] * known_e
    used = 3 * SUB
    columns = jnp.concatenate(
        [west_halo, east_halo, east_state_ref[...], jnp.zeros((width - used, height), f32)], 0
    ).T
    north_halo, south_halo = from_north_ref[...], from_south_ref[...]

    def shifted(field, q, state=None):
        e_from = SUB + q if state is None else 2 * SUB + state
        e = jnp.where(lane == width - 1, pltpu.roll(columns, width - 1 - e_from, 1), east_of(field))
        line = north_halo[us + q:us + q + 1] if state is None else north_state_ref[pl.ds(state, 1), :]
        n = jnp.where(row == height - 1, line, north_of(field))
        return e, n

    def whole(field, q):
        e, n = shifted(field, q)
        w = jnp.where(lane == 0, pltpu.roll(columns, (width - q) % width, 1), west_of(field))
        s = jnp.where(row == 0, south_halo[us + q:us + q + 1], south_of(field))
        return n + s + e + w - 4.0 * field

    wet = wet_ref[...].astype(f32)
    wet_e, wet_n = shifted(wet, 5)
    open_e, open_n = wet * wet_e, wet * wet_n
    surface = surface_ref[...]
    surface_out[...] = surface
    surface_e, surface_n = shifted(surface, 0, 0)
    for slot in range(2):
        at = at_level[slot]
        bottom = as_f32((g == groups - 1) & (at == 1))
        pressure = pressure_ref[slot]
        pressure_e, pressure_n = shifted(pressure, 0, 1 + slot)
        u, v = u_ref[at], v_ref[at]
        east_out[at] = open_e * (
            u - gravity_rate * (surface_e - surface) - (pressure_e - pressure)
            + viscous_rate * whole(u, slot) - friction_rate * bottom * u
        )
        north_out[at] = open_n * (
            v - gravity_rate * (surface_n - surface) - (pressure_n - pressure)
            + viscous_rate * whole(v, 2 + slot) - friction_rate * bottom * v
        )


def momentum(u, v, depth, wet_mask, surface, pressure, halos, states, count):
    args = (u, v, depth, wet_mask, surface, pressure, *halos, *states)
    return pl.pallas_call(
        partial(momentum_kernel, count=count),
        in_specs=[VM] * len(args), out_specs=[VM] * 3,
        out_shape=[jax.ShapeDtypeStruct(a.shape, f32) for a in (u, v, surface)],
        compiler_params=small,
        name="momentum",
    )(*near_core(*args))


def rates_kernel(cells_ref, loads_ref, kinetics_ref, wet_ref, out_ref, source_ref):
    g, _, _ = places()
    count, _, width = source_ref.shape
    size = count * SUB
    spread = (
        lax.broadcasted_iota(jnp.int32, (size, count), 0) // SUB
        == lax.broadcasted_iota(jnp.int32, (size, count), 1)
    ).astype(f32)
    full = jnp.dot(spread, kinetics_ref[...], precision=lax.Precision.HIGHEST)
    full = lax.dot_general(
        full, spread, (((1,), (1,)), ((), ())), precision=lax.Precision.HIGHEST
    )
    same = lax.broadcasted_iota(jnp.int32, (size, size), 0) % SUB
    same = same == lax.broadcasted_iota(jnp.int32, (size, size), 1) % SUB
    high, low = split(jnp.where(same, full, 0.0))
    out_ref[...] = jnp.concatenate([high, high, low], 1)
    source_ref[...] = jnp.zeros_like(source_ref)

    @pl.when(g == 0)
    def _():
        @pl.loop(0, cells_ref.shape[0])
        def _(r):
            at, spot = pl.ds(cells_ref[r] // width, 1), cells_ref[r] % width
            here = (lanes_of((1, width)) == spot) & (wet_ref[at, :] != 0)
            for t in range(count):
                source_ref[t, at, :] = source_ref[t, at, :] + jnp.where(here, loads_ref[r, t], 0.0)


def rates_and_source(cells, loads, kinetics, wet_mask):
    count = kinetics.shape[0]
    size = count * SUB
    return pl.pallas_call(
        rates_kernel, in_specs=[SM, SM, VM, VM], out_specs=[VM, VM],
        out_shape=[pltpu.VMEM((size, 3 * size), jnp.bfloat16), kept((count,) + wet_mask.shape)],
        compiler_params=small, name="rates",
    )(cells, loads, kinetics, *near_core(wet_mask))


def split(x):
    high = x.astype(jnp.bfloat16)
    return high, (x - high.astype(f32)).astype(jnp.bfloat16)


def mixing_rates(slot):
    g, groups, _ = places()
    has_next = 1.0 if slot == 0 else as_f32((g > 0) & (g < groups - 1))
    return 1.0 - mixing_rate - mixing_rate * has_next, mixing_rate * has_next


def mixed_rows(t, first, size, parts, keep_rate):
    (own, at), (other, there) = (pick(refs, first) for refs in parts)
    return keep_rate * own[t, pl.ds(at, size), :] + mixing_rate * other[t, pl.ds(there, size), :]


def ready_kernel(c_ref, wet_ref, *rest, sizes, strip):
    ready_ref = rest[-1]
    parts = [rest[:sizes[0]], rest[sizes[0]:sum(sizes)]]
    count, height, _ = ready_ref.shape
    keep_rate, _ = mixing_rates(1)
    for first, size in strips(height, strip, *(rows_in(refs) for refs in parts)):
        here = pl.ds(first, size)
        wet = wet_ref[here, :] != 0
        for t in range(count):
            value = mixed_rows(t, first, size, parts, keep_rate)
            ready_ref[t, here, :] = jnp.where(wet, value, c_ref[1, t, here, :])


def make_ready(c, wet_mask, own, other, strip=16):
    _, count, height, width = c.shape
    args = near_core(c, wet_mask, *own, *other)
    return pl.pallas_call(
        partial(ready_kernel, sizes=(len(own), len(other)), strip=strip),
        in_specs=[VM] * len(args),
        out_specs=VM,
        out_shape=kept((count, height, width)),
        compiler_params=small,
        name="ready",
    )(*args)


def react_kernel(wet_ref, rates_ref, *rest, slot, fixed, sizes, border, strip):
    out_hbm, done_ref, turned_ref, out_sem = rest[-4:]
    parts = [rest[sum(sizes[:k]):sum(sizes[:k + 1])] for k in range(len(sizes))]
    more = rest[sum(sizes):]
    _, _, at_level = places()
    count, height, width = done_ref.shape
    mixing = mixing_rates(slot)
    if slot == 0:
        turned_ref[...] = mixing[1] * turned_columns(more[1][pl.ds(fixed + count, 2 * count), :])
    rates = rates_ref[...]
    copies = []
    for first, size in strips(height, strip, *(rows_in(refs) for refs in parts)):
        here = pl.ds(first, size)
        groups_of = size // SUB
        beyond, at = pick(parts[0], first)
        wet = wet_ref[here, :] != 0
        passed = jnp.where(wet, mixing[1], 0.0)
        lane, row = lanes_of((size, width)), rows_of((size, width))
        rim = (lane == 0) | (lane == width - 1)
        values = []
        for t in range(count):
            far = beyond[t, pl.ds(at, size), :]
            if slot == 0:
                value = mixed_rows(t, first, size, parts[1:], mixing[0]) + mixing[1] * far
                if first < border:
                    columns = pltpu.roll(turned_ref[here, :], width - 1 - 2 * t, 1)
                    value = value + jnp.where(rim, columns, 0.0)
                if first == 0:
                    line = mixing[1] * more[1][pl.ds(fixed + t, 1), :]
                    value = value + jnp.where(row == 0, line, 0.0)
                values.append(jnp.where(wet, value, more[0][0, t, here, :]))
            else:
                values.append(more[0][t, here, :] + passed * far)
        stacked = jnp.concatenate(
            [
                jnp.concatenate([v[k * SUB:(k + 1) * SUB] for v in values], 0)
                for k in range(groups_of)
            ],
            1,
        )
        high, low = split(stacked)
        reaction = jnp.dot(
            rates, jnp.concatenate([high, low, high], 0), preferred_element_type=f32
        )
        warming = jnp.where(wet, jnp.exp(warming_rate * values[1]), 0.0)
        for t in range(count):
            gained = jnp.concatenate(
                [reaction[t * SUB:(t + 1) * SUB, k * width:(k + 1) * width] for k in range(groups_of)],
                0,
            )
            done = values[t] + warming * gained
            done_ref[t, here, :] = done if slot == 0 else done + more[1][t, here, :]
        copies.append(pltpu.make_async_copy(
            done_ref.at[:, here], out_hbm.at[:, at_level[slot], here], out_sem.at[len(copies)]
        ))
        copies[-1].start()
    for copy in copies:
        copy.wait()


def react(shape, wet_mask, rates, slot, received, more, mixed=(), into=None, fixed=0, border=0,
          strip=32):
    count, _, height, width = shape
    sizes = tuple(len(part) for part in (received, *mixed))
    flat = [a for part in (received, *mixed) for a in part]
    args = near_core(wet_mask, rates, *flat, *more)
    specs = [VM] * len(args)
    aliases = {}
    if into is not None:
        aliases = {len(args): 0}
        args.append(into)
        specs.append(HB)
    return pl.pallas_call(
        partial(react_kernel, slot=slot, strip=strip, fixed=fixed, sizes=sizes, border=border),
        in_specs=specs,
        out_specs=HB,
        scratch_shapes=[
            pltpu.VMEM((count, height, width), f32), pltpu.VMEM((height, width), f32),
            pltpu.SemaphoreType.DMA((height // SUB,)),
        ],
        out_shape=jax.ShapeDtypeStruct(shape, f32),
        input_output_aliases=aliases,
        compiler_params=small,
        name="react",
    )(*args)


def shards(tracers, u, v, surface, depth, wet_mask, river_cells, river_loads, kinetics):
    count, own_levels, height, _ = tracers.shape
    groups, tys, txs = (lax.axis_size(a) for a in ("grp", "ty", "tx"))
    levels = own_levels * groups
    assert own_levels == 2 and groups in (2, 4)
    direct, border = height // 2, 9 * height // 16
    cuts = (height - border, direct, height - direct)
    cell_args = (tracers, u, v, depth, wet_mask, levels)

    swap = [(i, i ^ 1) for i in range(groups)]
    middle = [(i, i + 1) for i in range(1, groups - 1, 2)]
    middle = middle + [(b, a) for a, b in middle]
    early = early_advection(*cell_args, border)
    near_x_lo = lax.ppermute(early, "grp", swap)
    c, coefs, fields, north, south, sides = tile_edges(*cell_args)

    up = [(i, i + 1) for i in range(tys - 1)]
    down = [(i + 1, i) for i in range(tys - 1)]
    from_south = lax.ppermute(north, "ty", up)
    from_north = lax.ppermute(south, "ty", down)
    if txs == 2:
        from_west = from_east = lax.ppermute(sides, "tx", [(0, 1), (1, 0)])
    else:
        from_west = lax.ppermute(sides, "tx", [(i, i + 1) for i in range(txs - 1)])
        from_east = lax.ppermute(sides, "tx", [(i + 1, i) for i in range(txs - 1)])
    x_hi, *m = closed_advection(c, coefs, cuts)
    rates, source = rates_and_source(river_cells, river_loads, kinetics, wet_mask)
    halos = (from_north, from_south, from_west, from_east)
    packet, x_fix, m_fix, rest = face_corrections(fields, north, south, sides, halos, levels, count)
    near = lax.ppermute(packet, "grp", swap)
    *x, m_0, m_1 = mend(x_fix, m_fix, early, x_hi, *m)
    near_x_hi = lax.ppermute(x[1], "grp", swap)
    near_m = [lax.ppermute(m_0, "grp", middle)]
    if groups == 4:
        handed = lax.ppermute(m[1], "grp", [(1, 3), (2, 0)])
        handed = mend_handed(lax.ppermute(rest, "grp", [(1, 3), (2, 0)]), handed)
        near_m.append(lax.ppermute(handed, "grp", [(3, 2), (0, 1)]))
    else:
        near_m.append(lax.ppermute(m_1, "grp", middle))

    columns = pair_sum(packet, near, 2 * height)
    if groups == 4:
        far = lax.ppermute(columns, "grp", [(i, i ^ 2) for i in range(groups)])
    else:
        far = jnp.zeros_like(columns)
    new_surface, pressure, south_state, west_state = new_surface_and_pressure(
        packet, near, far, fields, surface, depth, wet_mask, levels
    )
    north_state = lax.ppermute(south_state, "ty", down)
    east_state = lax.ppermute(west_state, "tx", [(i + 1, i) for i in range(txs - 1)])
    new_east, new_north, new_surface = momentum(
        u, v, depth, wet_mask, new_surface, pressure, halos, (north_state, east_state), count
    )

    mixed = (m_0, m_1)
    out = react(
        tracers.shape, wet_mask, rates, 0, (near_x_lo, near_x_hi), (c, near),
        (x, mixed), fixed=2 * height, border=border,
    )
    ready = make_ready(c, wet_mask, mixed, x)
    out = react(tracers.shape, wet_mask, rates, 1, near_m, (ready, source), into=out)
    return (out, new_east, new_north, new_surface)


def solution(mesh):
    field = P("grp", "ty", "tx")
    plane = P("ty", "tx")
    return jax.shard_map(
        shards,
        mesh=mesh,
        in_specs=(
            P(None, "grp", "ty", "tx"), field, field, plane, plane, plane,
            P(("ty", "tx")), P(("ty", "tx"), None), P(),
        ),
        out_specs=(P(None, "grp", "ty", "tx"), field, field, plane),
        check_vma=False,
    )
```
